32 devices in a mesh: pipe: 2 (over y), tensor: 2 (over core), dp: 8 (over z, x).
Axes of the slice: x: 2, y: 2, z: 4, core: 2. Of those that a mesh axis runs over, the one named last changes fastest.
Arguments:
- images_in: bfloat16 [2, 8, 200, 768], P(None, 'dp', 'tensor'), may hold values from -6 to 6
- out_grad: bfloat16 [2, 8, 200, 768], P(None, 'dp', 'tensor'), may hold values from -6 to 6
- attn_gain: bfloat16 [2, 768], P('pipe', 'dp'), may hold values from 0.5 to 1.5
- attn_bias: bfloat16 [2, 768], P('pipe', 'dp'), may hold values from -3 to 3
- qkv_weight: bfloat16 [2, 3, 768, 768], P('pipe', None, 'dp', 'tensor'), may hold values from -0.3125 to 0.3125
- proj_weight: bfloat16 [2, 768, 768], P('pipe', 'tensor', 'dp'), may hold values from -0.3125 to 0.3125
- moe_gain: bfloat16 [2, 768], P('pipe', 'dp'), may hold values from 0.5 to 1.5
- moe_bias: bfloat16 [2, 768], P('pipe', 'dp'), may hold values from -3 to 3
- router_weight: bfloat16 [2, 768, 4], P('pipe', 'dp'), may hold values from -0.3125 to 0.3125
- inner_weight: bfloat16 [2, 4, 768, 3072], P('pipe', None, 'dp', 'tensor'), may hold values from -0.21875 to 0.21875
- outer_weight: bfloat16 [2, 4, 3072, 768], P('pipe', None, 'tensor', 'dp'), may hold values from -0.3125 to 0.3125
- expert_ids: int32 [2, 2, 8, 200, 2], P('pipe', None, 'dp'), may hold values from 0 to 3, as said below
- slot_ids: int32 [2, 2, 8, 200, 2], P('pipe', None, 'dp'), may hold values from 0 to 128, as said below
Outputs:
- activations: bfloat16 [2, 2, 8, 200, 768], P('pipe', None, 'dp', 'tensor')
- input_grads: float32 [2, 2, 8, 200, 768], P('pipe', None, 'dp', 'tensor')
- grad_attn_gain: float32 [2, 768], P('pipe', 'dp')
- grad_attn_bias: float32 [2, 768], P('pipe', 'dp')
- grad_qkv_weight: float32 [2, 3, 768, 768], P('pipe', None, 'dp', 'tensor')
- grad_proj_weight: float32 [2, 768, 768], P('pipe', 'tensor', 'dp')
- grad_moe_gain: float32 [2, 768], P('pipe', 'dp')
- grad_moe_bias: float32 [2, 768], P('pipe', 'dp')
- grad_router_weight: float32 [2, 768, 4], P('pipe', 'dp')
- grad_inner_weight: float32 [2, 4, 768, 3072], P('pipe', None, 'dp', 'tensor')
- grad_outer_weight: float32 [2, 4, 3072, 768], P('pipe', None, 'tensor', 'dp')
The draws below stay inside these ranges and needn't reach their ends.
Inputs may be any that keep to these rules, and one draw needn't show every extreme that they name: `expert_ids`: each token's two choices name different experts; in every image some expert is the first choice of 129 or more live tokens. `slot_ids`: A choice's slot is its rank among the image's choices of that expert by live tokens, all first choices in token order before all second choices; 128 marks a choice of rank 128 or more, or of a padding position. In every image some expert fills all 128 slots.
All inputs are finite; a program needn't handle non-finite values.
Results may differ from the reference program's by a relative error of at most 0.028.
Values may be sent and summed in bfloat16 or wider, within the bound.
A program may use at most 256 MiB of HBM per device.

```python
import jax
import jax.numpy as jnp
from jax import lax

D = 768
HEADS = 12
HEAD_DIM = 64
FF = 3072
LIVE = 197
SEQ = 200
EXPERTS = 4
CAP = 128
MB = 2
SECTIONS = 2
IMAGES = 8


def route_tables(key):
    base_key = jax.random.fold_in(key, 101)
    subkeys = jax.random.split(base_key, 4)
    lead_shape = (SECTIONS, MB, IMAGES)
    position = jnp.arange(SEQ, dtype=jnp.int32)
    live_mask = position < LIVE
    busy_expert = jax.random.randint(subkeys[0], lead_shape + (1,), 0, EXPERTS, dtype=jnp.int32)
    first_choice = jax.random.randint(subkeys[1], lead_shape + (SEQ,), 0, EXPERTS, dtype=jnp.int32)
    random_rank = jax.random.randint(subkeys[2], lead_shape + (SEQ,), 0, 4096, dtype=jnp.int32)
    order_key = jnp.where(live_mask, random_rank * SEQ + position, 4096 * SEQ + position)
    order_rank = jnp.argsort(jnp.argsort(order_key, axis=-1, stable=True), axis=-1, stable=True)
    first_choice = jnp.where(order_rank <= CAP, busy_expert, first_choice)
    offset = jax.random.randint(subkeys[3], lead_shape + (SEQ,), 1, EXPERTS, dtype=jnp.int32)
    second_choice = (first_choice + offset) % EXPERTS
    expert_cols = jnp.arange(EXPERTS, dtype=jnp.int32)
    ones_first = ((first_choice[..., None] == expert_cols) & live_mask[:, None]).astype(jnp.int32)
    ones_second = ((second_choice[..., None] == expert_cols) & live_mask[:, None]).astype(jnp.int32)
    before_first = jnp.cumsum(ones_first, axis=-2) - ones_first
    before_second = jnp.sum(ones_first, axis=-2, keepdims=True) + jnp.cumsum(ones_second, axis=-2) - ones_second
    rank_first = jnp.sum(before_first * ones_first, axis=-1)
    rank_second = jnp.sum(before_second * ones_second, axis=-1)
    slot_first = jnp.where(live_mask, jnp.minimum(rank_first, CAP), CAP)
    slot_second = jnp.where(live_mask, jnp.minimum(rank_second, CAP), CAP)
    return (jnp.stack([first_choice, second_choice], axis=-1), jnp.stack([slot_first, slot_second], axis=-1).astype(jnp.int32))


def draw_expert_ids(key, part):
    return route_tables(key)[0]


def draw_slot_ids(key, part):
    return route_tables(key)[1]


def spiked(values, own_key, source, target, parts, factor):
    def block_of(dim):
        return (jnp.arange(values.shape[dim]) // (values.shape[dim] // parts)).reshape((-1,) + (1,) * (values.ndim - 1 - dim))

    one_side = jax.random.permutation(own_key, parts)[block_of(target)]
    other_side = (block_of(target) + parts // 2) % parts
    return jnp.where((block_of(source) == one_side) | (block_of(source) == other_side), factor * values, values)


def level_of(rng, shape, shards, smallest, high):
    factor_of, own = 1.0, jax.random.fold_in(rng, 6)
    for axis_at, blocks in shards:
        heights = jnp.exp(jax.random.uniform(jax.random.fold_in(own, axis_at), (blocks,), jnp.float32, smallest / len(shards), high / len(shards)))
        factor_of = factor_of * jnp.repeat(heights, shape[axis_at] // blocks).reshape([-1 if axis == axis_at else 1 for axis in range(len(shape))])
    return factor_of


def normal_values(own_key, extent, width, limit, cuts=(), kind=jnp.bfloat16):
    array = jax.random.normal(own_key, extent, jnp.float32) * width
    if len(cuts) > 0:
        array = level_of(own_key, extent, cuts, -0.22, 0.18) * array
    return jnp.clip(array, min=-limit, max=limit).astype(kind)


def bell_draw_with(key, shape, width, limit, cuts, heavy, kind=jnp.bfloat16):
    array = width * jax.random.normal(key, shape, jnp.float32)
    if cuts:
        array = array * level_of(key, shape, cuts, -0.22, 0.18)
    return jnp.clip(spiked(array, jax.random.fold_in(key, 3), *heavy), -limit, limit).astype(kind)


def setup_inputs(seed: int = 0) -> dict:
    splits = jax.random.split(jax.random.key(seed), 14)
    images_in = normal_values(splits[0], (MB, IMAGES, SEQ, D), 1.0, 6.0, ((1, 8), (2, 2)))
    out_grad = bell_draw_with(splits[1], (MB, IMAGES, SEQ, D), 1.0, 6.0, ((1, 8), (2, 2)), (1, 3, 8, 2.0))
    attn_gain = jnp.clip(1.0 + 0.1 * jax.random.normal(splits[2], (SECTIONS, D), jnp.float32), 0.5, 1.5).astype(jnp.bfloat16)
    attn_bias = normal_values(splits[3], (SECTIONS, D), 0.5, 3.0, ((0, 2), (1, 8)))
    qkv_weight = normal_values(splits[4], (SECTIONS, 3, D, D), (D // 2) ** -0.5, 0.3125, ((0, 2), (2, 8), (3, 2)))
    proj_weight = normal_values(splits[5], (SECTIONS, D, D), (D // 2) ** -0.5, 0.3125, ((0, 2), (1, 2), (2, 8)))
    moe_gain = jnp.clip(1.0 + 0.1 * jax.random.normal(splits[6], (SECTIONS, D), jnp.float32), 0.5, 1.5).astype(jnp.bfloat16)
    moe_bias = normal_values(splits[7], (SECTIONS, D), 0.5, 3.0, ((0, 2), (1, 8)))
    router_weight = normal_values(splits[8], (SECTIONS, D, EXPERTS), (D // 2) ** -0.5, 0.3125, ((0, 2), (1, 8)))
    inner_weight = normal_values(splits[9], (SECTIONS, EXPERTS, D, FF), D ** -0.5, 0.21875, ((0, 2), (2, 8), (3, 2)))
    outer_weight = normal_values(splits[10], (SECTIONS, EXPERTS, FF, D), (FF // 8) ** -0.5, 0.3125, ((0, 2), (2, 2), (3, 8)))
    expert_ids = draw_expert_ids(jax.random.fold_in(splits[13], 71), 0)
    slot_ids = draw_slot_ids(jax.random.fold_in(splits[13], 71), 0)
    return dict(images_in=images_in, out_grad=out_grad, attn_gain=attn_gain, attn_bias=attn_bias, qkv_weight=qkv_weight, proj_weight=proj_weight, moe_gain=moe_gain, moe_bias=moe_bias, router_weight=router_weight, inner_weight=inner_weight, outer_weight=outer_weight, expert_ids=expert_ids, slot_ids=slot_ids)


@jax.custom_vjp
def low(v):
    return lax.optimization_barrier(v.astype(jnp.bfloat16)).astype(jnp.float32)

@jax.custom_vjp
def low_back(v):
    return v

def low_keep(v):
    return (low(v), None)

def low_pass(kept, grad):
    return (grad,)

def back_keep(v):
    return (v, None)

def back_low(kept, grad):
    return (low(grad),)
low.defvjp(low_keep, low_pass)
low_back.defvjp(back_keep, back_low)
highest = lax.Precision.HIGHEST
epsilon = 1e-06

def layer_norm(values, norm_gain, norm_bias):
    centre = values - lax.optimization_barrier(jnp.mean(values, axis=-1, keepdims=True))
    spread = lax.optimization_barrier(jnp.mean(centre * centre, axis=-1, keepdims=True))
    return centre * lax.rsqrt(spread + epsilon) * norm_gain + norm_bias

def image_layer(params, pieces):
    attn_gain, attn_bias, qkv_weight, proj_weight, moe_gain, moe_bias, router_weight, inner_weight, outer_weight = params
    tokens, route_ids, slot_ids = pieces
    length = tokens.shape[0]
    normed = low(layer_norm(tokens, attn_gain, attn_bias))
    projected = jnp.einsum('sd,jde->jse', normed, qkv_weight, precision=highest)
    query_rows = low_back(low(projected[0])).reshape(length, HEADS, HEAD_DIM)
    key_rows = low_back(low(projected[1])).reshape(length, HEADS, HEAD_DIM)
    value_rows = low_back(low(projected[2])).reshape(length, HEADS, HEAD_DIM)
    scores = low_back(jnp.einsum('qhd,khd->hqk', query_rows, key_rows, precision=highest) * HEAD_DIM ** (-0.5))
    live_keys = jnp.arange(length) < LIVE
    scores = jnp.where(live_keys, scores, -1e+30)
    attention = jax.nn.softmax(scores, axis=-1)
    attended = jnp.einsum('hqk,khd->qhd', low(attention), value_rows, precision=highest).reshape(length, HEADS * HEAD_DIM)
    attended = low_back(low(attended))
    branch = low_back(jnp.dot(attended, proj_weight, precision=highest))
    hidden = tokens + branch
    normed_two = low(layer_norm(hidden, moe_gain, moe_bias))
    router_probs = jax.nn.softmax(jnp.dot(normed_two, router_weight, precision=highest), axis=-1)
    columns = jnp.arange(EXPERTS * CAP, dtype=jnp.int32)
    slot_codes = jnp.where(slot_ids < CAP, route_ids * CAP + slot_ids, -1)
    picked = (slot_codes[:, :, None] == columns).astype(jnp.float32)
    expert_hot = (route_ids[:, :, None] == jnp.arange(EXPERTS, dtype=jnp.int32)).astype(jnp.float32)
    gate_values = lax.optimization_barrier(jnp.sum(router_probs[:, None, :] * expert_hot, axis=-1))
    dispatch = lax.optimization_barrier(jnp.sum(picked, axis=1))
    combine = lax.optimization_barrier(jnp.sum(picked * gate_values[:, :, None], axis=1))
    expert_rows = jnp.dot(dispatch.T, normed_two, precision=highest).reshape(EXPERTS, CAP, D)
    pre_act = low_back(jnp.einsum('ecd,edf->ecf', expert_rows, inner_weight, precision=highest))
    activated = low(jax.nn.gelu(pre_act, approximate=True))
    expert_out = low_back(jnp.einsum('ecf,efd->ecd', activated, outer_weight, precision=highest))
    moe_out = jnp.dot(combine, expert_out.reshape(EXPERTS * CAP, D), precision=highest)
    return hidden + moe_out

def run_section(params, section_in, route_ids, slot_ids):
    checked = jax.checkpoint(image_layer)

    def scan_step(carry_in, pieces):
        return (carry_in, checked(params, pieces))
    carry_out, results = lax.scan(scan_step, jnp.zeros((), jnp.float32), (section_in, route_ids, slot_ids))
    return results

def forward(shift_all, params_all, images, route_all, slot_all):
    section_outputs = [[] for section_index in range(SECTIONS)]
    for mb_index in range(MB):
        section_in = images[mb_index]
        for section_index in range(SECTIONS):
            params = tuple((member[section_index] for member in params_all))
            result = run_section(params, section_in + shift_all[section_index, mb_index], route_all[section_index, mb_index], slot_all[section_index, mb_index])
            section_outputs[section_index].append(low(result))
            section_in = low_back(low(result))
    return jnp.stack([jnp.stack(per_section) for per_section in section_outputs])

def reference(images_in, out_grad, attn_gain, attn_bias, qkv_weight, proj_weight, moe_gain, moe_bias, router_weight, inner_weight, outer_weight, expert_ids, slot_ids):
    params_all = tuple((weight_array.astype(jnp.float32) for weight_array in (attn_gain, attn_bias, qkv_weight, proj_weight, moe_gain, moe_bias, router_weight, inner_weight, outer_weight)))
    images = images_in.astype(jnp.float32)
    shift_zero = jnp.zeros((SECTIONS,) + images.shape, jnp.float32)

    def whole_pass(shift_all, params_given):
        return forward(shift_all, params_given, images, expert_ids, slot_ids)
    activations, pull_back = jax.vjp(whole_pass, shift_zero, params_all)
    cotangent = jnp.zeros_like(activations).at[SECTIONS - 1].set(out_grad.astype(jnp.float32))
    grad_shift, grad_params = pull_back(cotangent)
    return (activations.astype(jnp.bfloat16), grad_shift, grad_params[0], grad_params[1], grad_params[2], grad_params[3], grad_params[4], grad_params[5], grad_params[6], grad_params[7], grad_params[8])
```

```python
import functools
import math

import jax
import jax.numpy as jnp
from jax import lax
from jax.experimental import pallas as pl
from jax.experimental.pallas import tpu as pltpu
from jax.sharding import PartitionSpec as P

HEAD_DIM = 64
LIVE = 197
CAP = 128
ROWS = 128
EPS = 1e-06
TILE = 512
BF = jnp.bfloat16
F32 = jnp.float32
MESH = pl.DeviceIdType.MESH


def nn(left, right):
    return lax.dot_general(left, right, (((1,), (0,)), ((), ())), preferred_element_type=F32)


def nt(left, right):
    return lax.dot_general(left, right, (((1,), (1,)), ((), ())), preferred_element_type=F32)


def tn(left, right):
    return lax.dot_general(left, right, (((0,), (0,)), ((), ())), preferred_element_type=F32)


def norm_stats(values):
    centre = values - jnp.mean(values, axis=-1, keepdims=True)
    inv = lax.rsqrt(jnp.mean(centre * centre, axis=-1, keepdims=True) + EPS)
    return centre * inv, inv


def norm_back(grad, unit, inv, gain):
    scaled = grad * gain
    return (
        scaled
        - jnp.mean(scaled, axis=-1, keepdims=True)
        - unit * jnp.mean(scaled * unit, axis=-1, keepdims=True)
    ) * inv


def iota(shape, dim):
    return lax.broadcasted_iota(jnp.int32, shape, dim)


class Place:
    def __init__(self, experts, spread):
        self.experts, self.spread = experts, spread
        self.plane = lax.axis_index("pipe")
        self.side = lax.axis_index("tensor")
        dp = lax.axis_index("dp")
        self.mine = dp // spread
        self.column = lax.rem(dp, spread)
        self.twin = {"tensor": 1 - self.side}

    def ahead(self, steps):
        return lax.rem(self.mine + steps, self.experts)

    def behind(self, steps):
        return lax.rem(self.mine + self.experts - steps, self.experts)

    def peer(self, group):
        return {"dp": group * self.spread + self.column}

    def greet(self):
        barrier = pltpu.get_barrier_semaphore()
        pl.semaphore_signal(barrier, inc=1, device_id=self.twin, device_id_type=MESH)
        for steps in range(1, self.experts):
            pl.semaphore_signal(
                barrier, inc=1, device_id=self.peer(self.ahead(steps)), device_id_type=MESH
            )
        pl.semaphore_wait(barrier, self.experts)


def send(source, target, sems, slot, device):
    copy = pltpu.make_async_remote_copy(
        src_ref=source,
        dst_ref=target,
        send_sem=sems.at[0, slot],
        recv_sem=sems.at[1, slot],
        device_id=device,
        device_id_type=MESH,
    )
    copy.start()
    return copy


def load_weights(place, section, own, other, inner, outer, sems):
    experts, spread = place.experts, place.spread
    shard, half = own[0].shape[1], own[0].shape[2]

    def start(pieces):
        at = 0
        for matrix, target in enumerate((inner, outer)):
            for shift in range(spread):
                column = lax.rem(place.column + spread - shift, spread)
                for flip in range(2):
                    side = lax.rem(place.side + flip, 2)
                    cols = pl.ds(pl.multiple_of(side * half, 128), half)
                    for steps in range(experts):
                        row = (place.behind(steps) * spread + column) * shard
                        pltpu.make_async_copy(
                            pieces[at].at[steps],
                            target.at[pl.ds(pl.multiple_of(row, math.gcd(shard, 16)), shard), cols],
                            sems.at[matrix],
                        ).start()
                    at += 1

    @pl.when(place.plane == section)
    def _():
        start(own)

    @pl.when(place.plane != section)
    def _():
        start(other)


def exchange_rows(place, out, into, sems, first, own_slot):
    copies = []
    for steps in range(1, place.experts):
        group = place.ahead(steps)
        copies.append(
            send(out.at[group], own_slot(into, place.mine), sems, first + steps - 1,
                 place.peer(group))
        )
    target = own_slot(into, place.mine)
    target[...] = out[place.mine]
    return copies


def gelu_tanh(pre):
    return jnp.tanh(0.7978845608028654 * (pre + 0.044715 * pre * pre * pre))


def fwd_kernel(cfg, *refs):
    section, experts, spread, wide = cfg
    pieces = 2 * 2 * spread
    z_ref, trow_ref, tcol_ref, attn_hbm = refs[:4]
    own, other = refs[4:4 + pieces], refs[4 + pieces:4 + 2 * pieces]
    (y_ref, h1_ref, a1_ref, qkv_ref, probs_ref, att_ref, a2_ref, rp_ref, rows_ref, pre_ref,
     chosen_ref,
     attn, inner, outer, a1_full, part, came, a2_full, disp, rows, acc, outb, ret,
     wsem, sems) = refs[4 + 2 * pieces:]
    place = Place(experts, spread)
    side = place.side
    features = z_ref.shape[1]
    ff = inner.shape[1]
    slots = CAP // 2
    full = 2 * ROWS
    fetch = pltpu.make_async_copy(
        attn_hbm.at[pl.ds(section * features, features)], attn, wsem.at[2]
    )
    fetch.start()
    load_weights(place, section, own, other, inner, outer, wsem)
    place.greet()

    z = z_ref[...].astype(F32)
    unit1, _ = norm_stats(z)
    fetch.wait()
    block = attn[:, 4 * wide:]
    vectors = block.astype(F32).T
    a1_full[side] = (unit1 * vectors[0:1] + vectors[1:2]).astype(BF)
    copy_a1 = send(a1_full.at[side], a1_full.at[side], sems, 0, place.twin)
    copy_a1.wait()
    a1 = a1_full[...].reshape(full, features)
    a1_ref[...] = a1
    for j in range(3):
        qkv_ref[j] = nn(a1, attn[:, j * wide:(j + 1) * wide]).astype(BF)
    key = iota((1, full), 1)
    key_row = lax.rem(key, ROWS)
    piece = (LIVE + 3) // 2
    key_live = (key_row < piece) & ((key // ROWS) * piece + key_row < LIVE)
    low_lane = iota((1, 128), 1) < HEAD_DIM
    for pair in range(wide // 128):
        lanes = slice(pair * 128, (pair + 1) * 128)
        q, k, v = qkv_ref[0, :, lanes], qkv_ref[1, :, lanes], qkv_ref[2, :, lanes]
        results = []
        for which in range(2):
            mask = low_lane if which == 0 else ~low_lane
            scores = nt(jnp.where(mask, q, jnp.zeros_like(q)), k) * HEAD_DIM**-0.5
            scores = jnp.where(key_live, scores, -1e30)
            weights = jnp.exp(scores - jnp.max(scores, axis=-1, keepdims=True))
            probs = weights / jnp.sum(weights, axis=-1, keepdims=True)
            probs_ref[2 * pair + which] = probs
            results.append(nn(probs.astype(BF), v))
        att_ref[:, lanes] = jnp.where(low_lane, results[0], results[1]).astype(BF)
    part[...] = nt(att_ref[...], attn[:, 3 * wide:4 * wide]).reshape(2, ROWS, features)
    copy_part = send(part.at[1 - side], came, sems, 1, place.twin)
    copy_part.wait()
    h1 = z + part[side] + came[...]
    h1_ref[...] = h1
    unit2, _ = norm_stats(h1)
    a2_full[side] = (unit2 * vectors[2:3] + vectors[3:4]).astype(BF)
    copy_a2 = send(a2_full.at[side], a2_full.at[side], sems, 2, place.twin)
    copy_a2.wait()
    a2 = a2_full[...].reshape(full, features)
    a2_ref[...] = a2

    slot = iota((experts * slots, full), 0) + side * (experts * slots)
    hit = (trow_ref[0:1, :] == slot) | (trow_ref[1:2, :] == slot)
    disp[...] = nn(hit.astype(F32).astype(BF), a2).astype(BF).reshape(experts, slots, features)
    sent = exchange_rows(place, disp, rows, sems, 3, lambda ref, group: ref.at[group])

    lane = iota((1, 128), 1)
    valid = (lane >= 4) & (lane < 4 + experts)
    logits = jnp.where(valid, nn(a2, block), -1e30)
    odds = jnp.where(valid, jnp.exp(logits - jnp.max(logits, axis=-1, keepdims=True)), 0.0)
    rp_ref[...] = odds / jnp.sum(odds, axis=-1, keepdims=True)

    pltpu.make_async_copy(inner, inner, wsem.at[0]).wait()
    pltpu.make_async_copy(outer, outer, wsem.at[1]).wait()
    for copy in sent:
        copy.wait()
    mine = rows[...].reshape(experts * slots, features)
    rows_ref[...] = mine
    acc[...] = jnp.zeros_like(acc)

    def tile_step(step, carry):
        cols = pl.ds(pl.multiple_of(step * TILE, TILE), TILE)
        pre = nn(rows_ref[...], inner[:, cols])
        pre_ref[:, cols] = pre
        act = (0.5 * pre * (1.0 + gelu_tanh(pre))).astype(BF)
        acc[...] += nt(act, outer[:, cols])
        return carry

    lax.fori_loop(0, ff // TILE, tile_step, 0)
    outb[...] = acc[...].astype(BF).reshape(experts, slots, features)
    sent = exchange_rows(
        place, outb, ret, sems, 2 + experts, lambda ref, group: ref.at[side, group]
    )
    for copy in sent:
        copy.wait()
    copy_ret = send(ret.at[side], ret.at[side], sems, 1 + 2 * experts, place.twin)
    copy_ret.wait()
    home = ret[...].reshape(2 * experts * slots, features)
    own_rows = pl.ds(pl.multiple_of(side * ROWS, ROWS), ROWS)
    table = tcol_ref[own_rows, :]
    odds = rp_ref[own_rows, :]
    column = iota((ROWS, 2 * experts * slots), 1)
    y = h1
    for choice in range(2):
        pick = (table[:, choice:choice + 1] == column).astype(F32).astype(BF)
        chosen = nn(pick, home)
        chosen_ref[choice] = chosen.astype(BF)
        hot = table[:, 2 + choice:3 + choice] + 4 == lane
        y = y + chosen * jnp.sum(jnp.where(hot, odds, 0.0), axis=-1, keepdims=True)
    y_ref[...] = y.astype(BF)


def bwd_kernel(cfg, *refs):
    section, experts, spread, wide = cfg
    pieces = 2 * 2 * spread
    (dy_ref, z_ref, h1_ref, a1_ref, qkv_ref, probs_ref, att_ref, a2_ref, rp_ref, rows_ref,
     pre_ref, chosen_ref, trow_ref, tcol_ref, attn_hbm) = refs[:15]
    own, other = refs[15:15 + pieces], refs[15 + pieces:15 + 2 * pieces]
    (dz_ref, gin_ref, gout_ref, gattn_ref,
     attn, inner, outer, dy_full, disp, dexp, acc, outb, ret, act_all, dpre_all, lhs_t,
     dbr_full, dqkv, part, came, wsem, sems) = refs[15 + 2 * pieces:]
    place = Place(experts, spread)
    side = place.side
    features = z_ref.shape[1]
    ff = inner.shape[1]
    slots = CAP // 2
    full = 2 * ROWS
    fetch = pltpu.make_async_copy(
        attn_hbm.at[pl.ds(section * features, features)], attn, wsem.at[2]
    )
    fetch.start()
    load_weights(place, section, own, other, inner, outer, wsem)
    place.greet()

    dy_full[side] = dy_ref[...]
    copy_dy = send(dy_full.at[side], dy_full.at[side], sems, 0, place.twin)
    copy_dy.wait()
    lane = iota((1, 128), 1)
    grad = dy_full[...].reshape(full, features).astype(F32)
    slot = iota((experts * slots, full), 0) + side * (experts * slots)
    total = jnp.zeros((experts * slots, features), F32)
    for choice in range(2):
        hot = tcol_ref[:, 2 + choice:3 + choice] + 4 == lane
        gate = jnp.sum(jnp.where(hot, rp_ref[...], 0.0), axis=-1, keepdims=True)
        hit = (trow_ref[choice:choice + 1, :] == slot).astype(F32).astype(BF)
        total = total + nn(hit, (gate * grad).astype(BF))
    disp[...] = total.astype(BF).reshape(experts, slots, features)
    sent = exchange_rows(place, disp, dexp, sems, 1, lambda ref, group: ref.at[group])

    fetch.wait()
    block = attn[:, 4 * wide:]
    vectors = block.astype(F32).T
    own_rows = pl.ds(pl.multiple_of(side * ROWS, ROWS), ROWS)
    table = tcol_ref[own_rows, :]
    odds = rp_ref[own_rows, :]
    dy = dy_ref[...].astype(F32)
    drouter = jnp.zeros((ROWS, 128), F32)
    for choice in range(2):
        dgate = jnp.sum(dy * chosen_ref[choice].astype(F32), axis=-1, keepdims=True)
        dgate = jnp.where(table[:, choice:choice + 1] >= 0, dgate, 0.0)
        hot = table[:, 2 + choice:3 + choice] + 4 == lane
        drouter = drouter + jnp.where(hot, dgate, 0.0)
    dlogit = odds * (drouter - jnp.sum(odds * drouter, axis=-1, keepdims=True))
    high = dlogit.astype(BF)
    rest = (dlogit - high.astype(F32)).astype(BF)
    da2 = nt(high, block) + nt(rest, block)
    a2 = a2_ref[own_rows, :]
    grad_router = tn(a2, high) + tn(a2, rest)

    pltpu.make_async_copy(inner, inner, wsem.at[0]).wait()
    pltpu.make_async_copy(outer, outer, wsem.at[1]).wait()
    for copy in sent:
        copy.wait()
    acc[...] = jnp.zeros_like(acc)

    def tile_step(step, carry):
        cols = pl.ds(pl.multiple_of(step * TILE, TILE), TILE)
        grad_act = nn(dexp[...].reshape(experts * slots, features), outer[:, cols])
        pre = pre_ref[:, cols]
        tanh = gelu_tanh(pre)
        act_all[:, cols] = (0.5 * pre * (1.0 + tanh)).astype(BF)
        slope = 0.5 * (1.0 + tanh) + 0.5 * pre * (1.0 - tanh * tanh) * (
            0.7978845608028654 * (1.0 + 3 * 0.044715 * pre * pre)
        )
        dpre = (grad_act * slope).astype(BF)
        dpre_all[:, cols] = dpre
        acc[...] += nt(dpre, inner[:, cols])
        return carry

    lax.fori_loop(0, ff // TILE, tile_step, 0)
    outb[...] = acc[...].astype(BF).reshape(experts, slots, features)
    sent = exchange_rows(
        place, outb, ret, sems, experts, lambda ref, group: ref.at[side, group]
    )
    lhs_t[0] = dexp[...].reshape(experts * slots, features).T
    lhs_t[1] = rows_ref[...].T

    def grad_step(step, carry):
        cols = pl.ds(pl.multiple_of(step * TILE, TILE), TILE)
        gout_ref[:, cols] = nn(lhs_t[0], act_all[:, cols]).astype(BF)
        gin_ref[:, cols] = nn(lhs_t[1], dpre_all[:, cols]).astype(BF)
        return carry

    lax.fori_loop(0, ff // TILE, grad_step, 0)
    for copy in sent:
        copy.wait()
    copy_ret = send(ret.at[side], ret.at[side], sems, 2 * experts - 1, place.twin)
    copy_ret.wait()
    home = ret[...].reshape(2 * experts * slots, features)
    column = iota((ROWS, 2 * experts * slots), 1)
    pick = (table[:, 0:1] == column) | (table[:, 1:2] == column)
    da2 = da2 + nn(pick.astype(F32).astype(BF), home)
    unit2, inv2 = norm_stats(h1_ref[...])
    grad_gain2 = jnp.sum(da2 * unit2, axis=0, keepdims=True)
    grad_bias2 = jnp.sum(da2, axis=0, keepdims=True)
    dh1 = dy + norm_back(da2, unit2, inv2, vectors[2:3])
    dbr_full[side] = dh1.astype(BF)
    copy_dbr = send(dbr_full.at[side], dbr_full.at[side], sems, 2 * experts, place.twin)
    copy_dbr.wait()
    dbr = dbr_full[...].reshape(full, features)
    gattn_ref[:, 3 * wide:4 * wide] = tn(dbr, att_ref[...]).astype(BF)
    datt = nn(dbr, attn[:, 3 * wide:4 * wide]).astype(BF)
    low_lane = lane < HEAD_DIM
    for pair in range(wide // 128):
        lanes = slice(pair * 128, (pair + 1) * 128)
        q, k, v = qkv_ref[0, :, lanes], qkv_ref[1, :, lanes], qkv_ref[2, :, lanes]
        wide_datt = datt[:, lanes]
        dq = dk = dv = 0.0
        for which in range(2):
            mask = low_lane if which == 0 else ~low_lane
            zero = jnp.zeros_like(q)
            probs = probs_ref[2 * pair + which]
            head = jnp.where(mask, wide_datt, zero)
            dv = dv + tn(probs.astype(BF), head)
            dprobs = nt(head, v)
            dscores = probs * (dprobs - jnp.sum(probs * dprobs, axis=-1, keepdims=True))
            dscores = dscores.astype(BF)
            dq = dq + nn(dscores, jnp.where(mask, k, zero))
            dk = dk + tn(dscores, jnp.where(mask, q, zero))
        dqkv[0, :, lanes] = (dq * HEAD_DIM**-0.5).astype(BF)
        dqkv[1, :, lanes] = (dk * HEAD_DIM**-0.5).astype(BF)
        dqkv[2, :, lanes] = dv.astype(BF)
    da1 = jnp.zeros((full, features), F32)
    for j in range(3):
        da1 = da1 + nt(dqkv[j], attn[:, j * wide:(j + 1) * wide])
    part[...] = da1.reshape(2, ROWS, features)
    copy_part = send(part.at[1 - side], came, sems, 2 * experts + 1, place.twin)
    for j in range(3):
        gattn_ref[:, j * wide:(j + 1) * wide] = tn(a1_ref[...], dqkv[j]).astype(BF)
    unit1, inv1 = norm_stats(z_ref[...].astype(F32))
    copy_part.wait()
    da1 = part[side] + came[...]
    grad_gain1 = jnp.sum(da1 * unit1, axis=0, keepdims=True)
    grad_bias1 = jnp.sum(da1, axis=0, keepdims=True)
    dz_ref[...] = dh1 + norm_back(da1, unit1, inv1, vectors[0:1])
    small = jnp.concatenate(
        [grad_gain1, grad_bias1, grad_gain2, grad_bias2, jnp.zeros((124, features), F32)], axis=0
    )
    gattn_ref[:, 4 * wide:] = (small.T + grad_router).astype(BF)


def forward(section, dims, z, trow, tcol, attn, own, other):
    experts, spread, features, wide, ff = dims
    full, slots = 2 * ROWS, CAP // 2
    heads = wide // HEAD_DIM
    vmem = pl.BlockSpec(memory_space=pltpu.VMEM)
    hbm = pl.BlockSpec(memory_space=pl.ANY)
    kernel = functools.partial(fwd_kernel, (section, experts, spread, wide))
    shape = jax.ShapeDtypeStruct
    return pl.pallas_call(
        kernel,
        out_shape=(
            shape((ROWS, features), BF),
            shape((ROWS, features), F32),
            shape((full, features), BF),
            shape((3, full, wide), BF),
            shape((heads, full, full), F32),
            shape((full, wide), BF),
            shape((full, features), BF),
            shape((full, 128), F32),
            shape((experts * slots, features), BF),
            shape((experts * slots, ff), F32),
            shape((2, ROWS, features), BF),
        ),
        in_specs=[vmem] * 3 + [hbm] * (1 + len(own) + len(other)),
        out_specs=(vmem,) * 11,
        scratch_shapes=[
            pltpu.VMEM((features, 4 * wide + 128), BF),
            pltpu.VMEM((features, ff), BF),
            pltpu.VMEM((features, ff), BF),
            pltpu.VMEM((2, ROWS, features), BF),
            pltpu.VMEM((2, ROWS, features), F32),
            pltpu.VMEM((ROWS, features), F32),
            pltpu.VMEM((2, ROWS, features), BF),
            pltpu.VMEM((experts, slots, features), BF),
            pltpu.VMEM((experts, slots, features), BF),
            pltpu.VMEM((experts * slots, features), F32),
            pltpu.VMEM((experts, slots, features), BF),
            pltpu.VMEM((2, experts, slots, features), BF),
            pltpu.SemaphoreType.DMA((3,)),
            pltpu.SemaphoreType.DMA((2, 2 + 2 * experts)),
        ],
        compiler_params=pltpu.CompilerParams(
            collective_id=section, has_side_effects=True, vmem_limit_bytes=56 * 2**20
        ),
        name=f"section_forward_{section}",
    )(z, trow, tcol, attn, *own, *other)


def backward(section, dims, dy, z, saved, trow, tcol, attn, own, other):
    experts, spread, features, wide, ff = dims
    full, slots = 2 * ROWS, CAP // 2
    vmem = pl.BlockSpec(memory_space=pltpu.VMEM)
    hbm = pl.BlockSpec(memory_space=pl.ANY)
    kernel = functools.partial(bwd_kernel, (section, experts, spread, wide))
    shape = jax.ShapeDtypeStruct
    return pl.pallas_call(
        kernel,
        out_shape=(
            shape((ROWS, features), F32),
            shape((features, ff), BF),
            shape((features, ff), BF),
            shape((features, 4 * wide + 128), BF),
        ),
        in_specs=[vmem] * 14 + [hbm] * (1 + len(own) + len(other)),
        out_specs=(vmem,) * 4,
        scratch_shapes=[
            pltpu.VMEM((features, 4 * wide + 128), BF),
            pltpu.VMEM((features, ff), BF),
            pltpu.VMEM((features, ff), BF),
            pltpu.VMEM((2, ROWS, features), BF),
            pltpu.VMEM((experts, slots, features), BF),
            pltpu.VMEM((experts, slots, features), BF),
            pltpu.VMEM((experts * slots, features), F32),
            pltpu.VMEM((experts, slots, features), BF),
            pltpu.VMEM((2, experts, slots, features), BF),
            pltpu.VMEM((experts * slots, ff), BF),
            pltpu.VMEM((experts * slots, ff), BF),
            pltpu.VMEM((2, features, experts * slots), BF),
            pltpu.VMEM((2, ROWS, features), BF),
            pltpu.VMEM((3, full, wide), BF),
            pltpu.VMEM((2, ROWS, features), F32),
            pltpu.VMEM((ROWS, features), F32),
            pltpu.SemaphoreType.DMA((3,)),
            pltpu.SemaphoreType.DMA((2, 2 + 2 * experts)),
        ],
        compiler_params=pltpu.CompilerParams(
            collective_id=2 + section, has_side_effects=True, vmem_limit_bytes=56 * 2**20
        ),
        name=f"section_backward_{section}",
    )(dy, z, *saved, trow, tcol, attn, *own, *other)


def swap_planes(values):
    return lax.ppermute(values, "pipe", [(0, 1), (1, 0)])


def swap_sides(values):
    return lax.ppermute(values, "tensor", [(0, 1), (1, 0)])


def shift_groups(values, steps, experts, spread):
    pairs = [
        (g * spread + c, (g + steps) % experts * spread + c)
        for g in range(experts) for c in range(spread)
    ]
    return lax.ppermute(values, "dp", pairs)


def shift_columns(values, steps, experts, spread):
    pairs = [
        (g * spread + c, g * spread + (c + steps) % spread)
        for g in range(experts) for c in range(spread)
    ]
    return lax.ppermute(values, "dp", pairs)


def pick(values, index, axis=0):
    return lax.dynamic_index_in_dim(values, index, axis, keepdims=False)


def spread_weights(matrices, mine, dims):
    experts, spread = dims[:2]
    held = []
    for shards in matrices:
        blocks = [pick(shards, mine)]
        for steps in range(1, experts):
            blocks.append(
                shift_groups(pick(shards, (mine + steps) % experts), steps, experts, spread)
            )
        held.append(jnp.stack(blocks))
    own, other = [], []
    for matrix, blocks in enumerate(held):
        columns = [blocks] + [
            shift_columns(blocks, steps, experts, spread) for steps in range(1, spread)
        ]
        if matrix == 0:
            across = [swap_planes(values) for values in columns]
        else:
            first = swap_planes(blocks)
            across = [first] + [
                shift_columns(first, steps, experts, spread) for steps in range(1, spread)
            ]
        for values in columns:
            own += [values, swap_sides(values)]
        for values in across:
            other += [values, swap_sides(values)]
    return own, other


def add(left, right):
    return (left.astype(F32) + right.astype(F32)).astype(BF)


def reduce_grads(per_section, plane, side, mine, column, dims, planes_first):
    experts, spread, features, _, ff = dims
    half = ff // 2
    halved = []
    for full in per_section:
        keep = lax.dynamic_slice_in_dim(full, side * half, half, 1)
        give = lax.dynamic_slice_in_dim(full, (1 - side) * half, half, 1)
        halved.append(add(keep, swap_sides(give)))

    def over_planes(first, second):
        keep = jnp.where(plane == 0, first, second)
        give = jnp.where(plane == 0, second, first)
        return add(keep, swap_planes(give))

    def over_columns(values):
        total = pick(values, column, 1)
        for steps in range(1, spread):
            give = pick(values, (column + steps) % spread, 1)
            total = add(total, shift_columns(give, steps, experts, spread))
        return total

    parts = [values.reshape(experts, spread, features // (experts * spread), half)
             for values in halved]
    if planes_first:
        total = over_columns(over_planes(*parts))
    else:
        total = over_planes(*[over_columns(values) for values in parts])
    blocks = [pick(total, mine)]
    for steps in range(1, experts):
        blocks.append(
            shift_groups(pick(total, (mine + steps) % experts), steps, experts, spread)
        )
    stacked = jnp.stack(blocks)
    return jnp.stack(
        [pick(stacked, (mine - group) % experts) for group in range(experts)]
    ).astype(F32)


def body(
    images_in,
    out_grad,
    attn_gain,
    attn_bias,
    qkv_weight,
    proj_weight,
    moe_gain,
    moe_bias,
    router_weight,
    inner_weight,
    outer_weight,
    expert_ids,
    slot_ids,
):
    plane = lax.axis_index("pipe")
    side = lax.axis_index("tensor")
    micro, local, piece, features = images_in.shape
    shard, wide = qkv_weight.shape[2], qkv_weight.shape[3]
    experts = router_weight.shape[2]
    half = inner_weight.shape[3]
    spread = lax.axis_size("dp") // experts
    dims = (experts, spread, features, wide, 2 * half)
    dp = lax.axis_index("dp")
    mine, column = dp // spread, dp % spread
    packed = jnp.concatenate(
        [qkv_weight[0, 0], qkv_weight[0, 1], qkv_weight[0, 2], proj_weight[0].T,
         jnp.stack([attn_gain[0], attn_bias[0], moe_gain[0], moe_bias[0]], axis=1),
         router_weight[0], jnp.zeros((shard, 128 - 4 - experts), BF)],
        axis=1,
    )
    attn = lax.all_gather(packed, ("pipe", "dp"), axis=0, tiled=True)
    own, other = spread_weights(
        (inner_weight[0], outer_weight[0].transpose(0, 2, 1)), mine, dims
    )

    def my_image(values):
        return jnp.pad(pick(values, plane)[0], ((0, ROWS - piece), (0, 0)))

    routes = expert_ids[0, :, 0]
    slots = slot_ids[0, :, 0]
    kept = slots < CAP
    codes = jnp.where(
        kept, slots // (CAP // 2) * (experts * CAP // 2) + routes * (CAP // 2) + slots % (CAP // 2),
        -1,
    )
    table = jnp.concatenate([codes, routes], axis=-1)
    table_own = pick(table, plane)
    table_other = swap_planes(pick(table, 1 - plane))
    tables = []
    for section in range(2):
        values = jnp.where(plane == section, table_own, table_other).reshape(2, piece, 4)
        values = jnp.pad(values, ((0, 0), (0, ROWS - piece), (0, 0)), constant_values=-1)
        values = values.reshape(2 * ROWS, 4)
        tables.append((
            jnp.pad(values.T, ((0, 4), (0, 0)), constant_values=-1),
            jnp.pad(values, ((0, 0), (0, 124)), constant_values=-1),
        ))

    weights = (attn, own, other)
    z0 = my_image(images_in)
    y0, *saved0 = forward(0, dims, z0, *tables[0], *weights)
    y1, *saved1 = forward(1, dims, y0, *tables[1], *weights)
    dz1, *grads1 = backward(1, dims, my_image(out_grad), y0, saved1, *tables[1], *weights)
    dz0, *grads0 = backward(0, dims, dz1.astype(BF), z0, saved0, *tables[0], *weights)

    inner_out = reduce_grads(
        (grads0[0], grads1[0]), plane, side, mine, column, dims, False
    )
    outer_out = reduce_grads(
        (grads0[1], grads1[1]), plane, side, mine, column, dims, True
    )
    packed_grads = jnp.concatenate([grads0[2], grads1[2]], axis=0)
    packed_out = lax.psum_scatter(
        packed_grads, ("pipe", "dp"), scatter_dimension=0, tiled=True
    ).astype(F32)
    own_small = packed_out[:, 4 * wide:4 * wide + 4 + experts]
    own_small = own_small + swap_sides(own_small)

    def shape_out(first, second):
        first, second = first[:piece], second[:piece]
        keep = jnp.where(plane == 0, first, second)
        came = swap_planes(jnp.where(plane == 0, second, first))
        both = jnp.stack([jnp.where(plane == 0, keep, came), jnp.where(plane == 0, came, keep)])
        return both.reshape(1, micro, local, piece, features)

    return (
        shape_out(y0, y1),
        shape_out(dz0, dz1),
        own_small[:, 0][None],
        own_small[:, 1][None],
        jnp.stack([packed_out[:, j * wide:(j + 1) * wide] for j in range(3)])[None],
        packed_out[:, 3 * wide:4 * wide].T[None],
        own_small[:, 2][None],
        own_small[:, 3][None],
        own_small[:, 4:][None],
        inner_out[None],
        outer_out.transpose(0, 2, 1)[None],
    )


def solution(mesh):
    in_specs = (
        P(None, "dp", "tensor", None),
        P(None, "dp", "tensor", None),
        P("pipe", "dp"),
        P("pipe", "dp"),
        P("pipe", None, "dp", "tensor"),
        P("pipe", "tensor", "dp"),
        P("pipe", "dp"),
        P("pipe", "dp"),
        P("pipe", "dp", None),
        P("pipe", None, "dp", "tensor"),
        P("pipe", None, "tensor", "dp"),
        P("pipe", None, "dp", None, None),
        P("pipe", None, "dp", None, None),
    )
    out_specs = (
        P("pipe", None, "dp", "tensor", None),
        P("pipe", None, "dp", "tensor", None),
        P("pipe", "dp"),
        P("pipe", "dp"),
        P("pipe", None, "dp", "tensor"),
        P("pipe", "tensor", "dp"),
        P("pipe", "dp"),
        P("pipe", "dp"),
        P("pipe", "dp", None),
        P("pipe", None, "dp", "tensor"),
        P("pipe", None, "tensor", "dp"),
    )
    return jax.shard_map(body, mesh=mesh, in_specs=in_specs, out_specs=out_specs, check_vma=False)
```

```python
import functools
import math

import jax
import jax.numpy as jnp
from jax import lax
from jax.experimental import pallas as pl
from jax.experimental.pallas import tpu as pltpu
from jax.sharding import PartitionSpec as P

HEAD_DIM = 64
LIVE = 197
CAP = 128
ROWS = 128
EPS = 1e-06
TILE = 512
BF = jnp.bfloat16
F32 = jnp.float32
MESH = pl.DeviceIdType.MESH


def nn(left, right):
    return lax.dot_general(left, right, (((1,), (0,)), ((), ())), preferred_element_type=F32)


def nt(left, right):
    return lax.dot_general(left, right, (((1,), (1,)), ((), ())), preferred_element_type=F32)


def tn(left, right):
    return lax.dot_general(left, right, (((0,), (0,)), ((), ())), preferred_element_type=F32)


def norm_stats(values):
    centre = values - jnp.mean(values, axis=-1, keepdims=True)
    inv = lax.rsqrt(jnp.mean(centre * centre, axis=-1, keepdims=True) + EPS)
    return centre * inv, inv


def norm_back(grad, unit, inv, gain):
    scaled = grad * gain
    return (
        scaled
        - jnp.mean(scaled, axis=-1, keepdims=True)
        - unit * jnp.mean(scaled * unit, axis=-1, keepdims=True)
    ) * inv


def iota(shape, dim):
    return lax.broadcasted_iota(jnp.int32, shape, dim)


class Place:
    def __init__(self, experts, spread):
        self.experts, self.spread = experts, spread
        self.plane = lax.axis_index("pipe")
        self.side = lax.axis_index("tensor")
        dp = lax.axis_index("dp")
        self.mine = dp // spread
        self.column = lax.rem(dp, spread)
        self.twin = {"tensor": 1 - self.side}
        self.across = {"pipe": 1 - self.plane}

    def ahead(self, steps):
        return lax.rem(self.mine + steps, self.experts)

    def behind(self, steps):
        return lax.rem(self.mine + self.experts - steps, self.experts)

    def peer(self, group):
        return {"dp": group * self.spread + self.column}

    def beside(self, shift):
        return {"dp": self.mine * self.spread + lax.rem(self.column + shift, self.spread)}

    def greet(self, everyone=False):
        barrier = pltpu.get_barrier_semaphore()
        devices = [self.twin]
        devices += [self.peer(self.ahead(steps)) for steps in range(1, self.experts)]
        if everyone:
            devices += [self.across]
            devices += [self.beside(shift) for shift in range(1, self.spread)]
        for device in devices:
            pl.semaphore_signal(barrier, inc=1, device_id=device, device_id_type=MESH)
        pl.semaphore_wait(barrier, len(devices))


def send(source, target, sems, slot, device):
    copy = pltpu.make_async_remote_copy(
        src_ref=source,
        dst_ref=target,
        send_sem=sems.at[0, slot],
        recv_sem=sems.at[1, slot],
        device_id=device,
        device_id_type=MESH,
    )
    copy.start()
    return copy


def spread_kernel(cfg, attn_own, inner_own, outer_own, attn_all, inner_all, outer_all, lsem, sems):
    experts, spread = cfg
    place = Place(experts, spread)
    plane, side, column = place.plane, place.side, place.column
    shard, half = inner_own.shape[1:]
    slot = iter(range(sems.shape[1]))
    place.greet(everyone=True)
    kinds = range(3)
    order = [0] + list(range(1, experts, 2)) + list(range(2, experts, 2))
    sends = []

    def where(kind, section, group, col):
        rows = pl.ds(pl.multiple_of((group * spread + col) * shard, math.gcd(shard, 16)), shard)
        if kind == 0:
            return attn_all.at[section, rows]
        cols = pl.ds(pl.multiple_of(side * half, 128), half)
        return (inner_all if kind == 1 else outer_all).at[section, rows, cols]

    def raw(kind, group):
        return attn_own if kind == 0 else (inner_own if kind == 1 else outer_own).at[group]

    def planes_late(kind, steps):
        return kind == 1 or (kind == 0 and steps < experts // 2)

    def pass_on(source, target, device):
        copy = send(source, target, sems, next(slot), device)
        sends.append(copy)
        return copy

    def to_twin(kind, section, group, col, source=None):
        if kind:
            target = where(kind, section, group, col)
            return [pass_on(target if source is None else source, target, place.twin)]
        return []

    over_groups, over_columns, over_planes, late, twins, local = {}, {}, {}, {}, [], []
    for steps in order[1:]:
        for kind in kinds:
            group = place.ahead(steps)
            over_groups[kind, steps] = pass_on(
                raw(kind, group), where(kind, plane, place.mine, column), place.peer(group)
            )
    for kind in kinds:
        copy = pltpu.make_async_copy(
            raw(kind, place.mine), where(kind, plane, place.mine, column), lsem.at[kind]
        )
        copy.start()
        local.append(copy)

    def first_hop(kind, steps):
        target = where(kind, plane, place.behind(steps), column)
        source = target
        if steps:
            over_groups[kind, steps].wait_recv()
        else:
            source = raw(kind, place.mine)
        for shift in range(1, spread):
            over_columns[kind, steps, shift] = pass_on(source, target, place.beside(shift))
        over_planes[kind, steps] = pass_on(source, target, place.across)
        twins.extend(to_twin(kind, plane, place.behind(steps), column, source))

    def second_hop(kind, steps):
        group = place.behind(steps)
        if planes_late(kind, steps):
            for shift in range(1, spread):
                over_columns[kind, steps, shift].wait_recv()
                col = lax.rem(column + spread - shift, spread)
                target = where(kind, plane, group, col)
                late[kind, steps, shift] = pass_on(target, target, place.across)
                twins.extend(to_twin(kind, plane, group, col))
        else:
            over_planes[kind, steps].wait_recv()
            target = where(kind, 1 - plane, group, column)
            for shift in range(1, spread):
                late[kind, steps, shift] = pass_on(target, target, place.beside(shift))
            twins.extend(to_twin(kind, 1 - plane, group, column))

    def last_hop(kind, steps):
        group = place.behind(steps)
        if planes_late(kind, steps):
            over_planes[kind, steps].wait_recv()
            twins.extend(to_twin(kind, 1 - plane, group, column))
        else:
            for shift in range(1, spread):
                over_columns[kind, steps, shift].wait_recv()
                col = lax.rem(column + spread - shift, spread)
                twins.extend(to_twin(kind, plane, group, col))
        for shift in range(1, spread):
            late[kind, steps, shift].wait_recv()
            col = lax.rem(column + spread - shift, spread)
            twins.extend(to_twin(kind, 1 - plane, group, col))

    for at in range(experts + 2):
        for kind in kinds:
            if at < experts:
                first_hop(kind, order[at])
            if 1 <= at < experts + 1:
                second_hop(kind, order[at - 1])
            if at >= 2:
                last_hop(kind, order[at - 2])
    for copy in twins:
        copy.wait_recv()
    for copy in sends:
        copy.wait_send()
    for copy in local:
        copy.wait()


def add_into(target, came):
    target[...] = (target[...].astype(F32) + came[...].astype(F32)).astype(BF)


def reduce_kernel(cfg, *refs):
    experts, spread = cfg
    gin, gout, gattn = refs[0:2], refs[2:4], refs[4:6]
    (inner_out, outer_out, attn_out,
     acc, twin_in, attn_acc, in_cols, in_planes, out_planes, out_cols, at_cols, at_planes,
     at_cols_late, at_planes_late, z_in, z_out, z_attn, lsem, sems) = refs[6:]
    place = Place(experts, spread)
    plane, side, column = place.plane, place.side, place.column
    shard, half = acc.shape[4:]
    slot = iter(range(sems.shape[1]))
    local_slot = iter(range(lsem.shape[0]))
    place.greet(everyone=True)
    order = list(range(2, experts, 2)) + list(range(1, experts, 2)) + [0]
    sends = []

    def pass_on(source, target, device):
        copy = send(source, target, sems, next(slot), device)
        sends.append(copy)
        return copy

    def left_of(shift):
        return lax.rem(column + spread - shift, spread)

    halves = {}
    for steps in order:
        group = place.ahead(steps)
        for section in range(2):
            for matrix, grads in enumerate((gin, gout)):
                for col in range(spread):
                    rows = pl.ds(
                        pl.multiple_of((group * spread + col) * shard, math.gcd(shard, 16)), shard
                    )
                    give = pl.ds(pl.multiple_of((1 - side) * half, 128), half)
                    keep = pl.ds(pl.multiple_of(side * half, 128), half)
                    away = pass_on(
                        grads[section].at[rows, give],
                        twin_in.at[section, matrix, steps, col], place.twin,
                    )
                    own = pltpu.make_async_copy(
                        grads[section].at[rows, keep],
                        acc.at[section, matrix, steps, col], lsem.at[next(local_slot)],
                    )
                    own.start()
                    halves[steps, section, matrix, col] = (away, own)
    attn_local = {}
    for steps in order:
        group = place.ahead(steps)
        for section in range(2):
            copy = pltpu.make_async_copy(
                gattn[section].at[pl.ds(
                    pl.multiple_of(group * spread * shard, math.gcd(shard, 16)), spread * shard
                )],
                attn_acc.at[section, steps], lsem.at[next(local_slot)],
            )
            copy.start()
            attn_local[steps, section] = copy

    hops = {}
    in_a = lambda section, steps, col: acc.at[section, 0, steps, col]
    out_a = lambda section, steps, col: acc.at[section, 1, steps, col]

    def attn_a(section, steps, col):
        return attn_acc.at[section, steps, pl.ds(
            pl.multiple_of(col * shard, math.gcd(shard, 16)), shard
        )]

    def columns_first(kind, section, steps, block, came):
        for shift in range(1, spread):
            hops[kind, "x", steps, section, shift] = pass_on(
                block(section, steps, lax.rem(column + shift, spread)),
                came.at[section, steps, shift - 1], place.beside(shift),
            )

    def planes_first(kind, steps, block, came):
        for col in range(spread):
            hops[kind, "y", steps, col] = pass_on(
                block(1 - plane, steps, col), came.at[steps, col], place.across
            )

    def planes_second(kind, steps, block, came_columns, came):
        for section in range(2):
            for shift in range(1, spread):
                hops[kind, "x", steps, section, shift].wait_recv()
                add_into(block(section, steps, column),
                         came_columns.at[section, steps, shift - 1])
        hops[kind, "y", steps] = pass_on(
            block(1 - plane, steps, column), came.at[steps], place.across
        )

    def columns_second(kind, steps, block, came_planes, came):
        for col in range(spread):
            hops[kind, "y", steps, col].wait_recv()
            add_into(block(plane, steps, col), came_planes.at[steps, col])
        for shift in range(1, spread):
            hops[kind, "x", steps, shift] = pass_on(
                block(plane, steps, lax.rem(column + shift, spread)),
                came.at[steps, shift - 1], place.beside(shift),
            )

    def first(steps):
        for section in range(2):
            attn_local[steps, section].wait()
        for matrix in range(2):
            for section in range(2):
                for col in range(spread):
                    away, own = halves[steps, section, matrix, col]
                    own.wait()
                    away.wait_recv()
                    add_into(acc.at[section, matrix, steps, col],
                             twin_in.at[section, matrix, steps, col])
            if matrix == 0:
                for section in range(2):
                    columns_first("i", section, steps, in_a, in_cols)
            else:
                planes_first("o", steps, out_a, out_planes)
        if steps % 2:
            planes_first("a", steps, attn_a, at_planes)
        else:
            for section in range(2):
                columns_first("a", section, steps, attn_a, at_cols)

    def second(steps):
        planes_second("i", steps, in_a, in_cols, in_planes)
        columns_second("o", steps, out_a, out_planes, out_cols)
        if steps % 2:
            columns_second("a", steps, attn_a, at_planes, at_cols_late)
        else:
            planes_second("a", steps, attn_a, at_cols, at_planes_late)

    def third(steps):
        hops["i", "y", steps].wait_recv()
        add_into(in_a(plane, steps, column), in_planes.at[steps])
        for shift in range(1, spread):
            hops["o", "x", steps, shift].wait_recv()
            add_into(out_a(plane, steps, column), out_cols.at[steps, shift - 1])
        if steps % 2:
            for shift in range(1, spread):
                hops["a", "x", steps, shift].wait_recv()
                add_into(attn_a(plane, steps, column), at_cols_late.at[steps, shift - 1])
        else:
            hops["a", "y", steps].wait_recv()
            add_into(attn_a(plane, steps, column), at_planes_late.at[steps])
        if steps:
            device = place.peer(place.ahead(steps))
            for name, source, target in (
                ("iz", in_a(plane, steps, column), z_in.at[steps]),
                ("oz", out_a(plane, steps, column), z_out.at[steps]),
                ("az", attn_a(plane, steps, column), z_attn.at[steps]),
            ):
                hops[name, steps] = pass_on(source, target, device)

    for at in range(experts + 2):
        if at < experts:
            first(order[at])
        if 1 <= at < experts + 1:
            second(order[at - 1])
        if at >= 2:
            third(order[at - 2])
    inner_out[place.mine] = acc[plane, 0, 0, column]
    outer_out[place.mine] = acc[plane, 1, 0, column]
    total = attn_a(plane, 0, column)[...].astype(F32)
    for steps in order[:-1]:
        source = place.behind(steps)
        hops["iz", steps].wait_recv()
        inner_out[source] = z_in[steps]
        hops["oz", steps].wait_recv()
        outer_out[source] = z_out[steps]
        hops["az", steps].wait_recv()
        total = total + z_attn[steps].astype(F32)
    attn_out[...] = total
    for copy in sends:
        copy.wait_send()


def exchange_rows(place, out, into, sems, first, own_slot):
    copies = []
    for steps in range(1, place.experts):
        group = place.ahead(steps)
        copies.append(
            send(out.at[group], own_slot(into, place.mine), sems, first + steps - 1,
                 place.peer(group))
        )
    target = own_slot(into, place.mine)
    target[...] = out[place.mine]
    return copies


def gelu_tanh(pre):
    return jnp.tanh(0.7978845608028654 * (pre + 0.044715 * pre * pre * pre))


def fwd_kernel(cfg, *refs):
    section, experts, spread, wide = cfg
    z_ref, trow_ref, tcol_ref, attn_hbm, inner_hbm, outer_hbm = refs[:6]
    (y_ref, h1_ref, a1_ref, qkv_ref, probs_ref, att_ref, a2_ref, rp_ref, rows_ref, pre_ref,
     chosen_ref,
     attn, inner, outer, a1_full, part, came, a2_full, disp, rows, acc, outb, ret,
     wsem, sems) = refs[6:]
    place = Place(experts, spread)
    side = place.side
    features = z_ref.shape[1]
    ff = inner.shape[1]
    slots = CAP // 2
    full = 2 * ROWS
    fetch = pltpu.make_async_copy(attn_hbm.at[section], attn, wsem.at[2])
    fetch.start()
    fetch_inner = pltpu.make_async_copy(inner_hbm.at[section], inner, wsem.at[0])
    fetch_inner.start()
    fetch_outer = pltpu.make_async_copy(outer_hbm.at[section], outer, wsem.at[1])
    fetch_outer.start()
    place.greet()

    z = z_ref[...].astype(F32)
    unit1, _ = norm_stats(z)
    fetch.wait()
    block = attn[:, 4 * wide:]
    vectors = block.astype(F32).T
    a1_full[side] = (unit1 * vectors[0:1] + vectors[1:2]).astype(BF)
    copy_a1 = send(a1_full.at[side], a1_full.at[side], sems, 0, place.twin)
    copy_a1.wait()
    a1 = a1_full[...].reshape(full, features)
    a1_ref[...] = a1
    for j in range(3):
        qkv_ref[j] = nn(a1, attn[:, j * wide:(j + 1) * wide]).astype(BF)
    key = iota((1, full), 1)
    key_row = lax.rem(key, ROWS)
    piece = (LIVE + 3) // 2
    key_live = (key_row < piece) & ((key // ROWS) * piece + key_row < LIVE)
    low_lane = iota((1, 128), 1) < HEAD_DIM
    for pair in range(wide // 128):
        lanes = slice(pair * 128, (pair + 1) * 128)
        q, k, v = qkv_ref[0, :, lanes], qkv_ref[1, :, lanes], qkv_ref[2, :, lanes]
        results = []
        for which in range(2):
            mask = low_lane if which == 0 else ~low_lane
            scores = nt(jnp.where(mask, q, jnp.zeros_like(q)), k) * HEAD_DIM**-0.5
            scores = jnp.where(key_live, scores, -1e30)
            weights = jnp.exp(scores - jnp.max(scores, axis=-1, keepdims=True))
            probs = weights / jnp.sum(weights, axis=-1, keepdims=True)
            probs_ref[2 * pair + which] = probs
            results.append(nn(probs.astype(BF), v))
        att_ref[:, lanes] = jnp.where(low_lane, results[0], results[1]).astype(BF)
    part[...] = nt(att_ref[...], attn[:, 3 * wide:4 * wide]).reshape(2, ROWS, features)
    copy_part = send(part.at[1 - side], came, sems, 1, place.twin)
    copy_part.wait()
    h1 = z + part[side] + came[...]
    h1_ref[...] = h1
    unit2, _ = norm_stats(h1)
    a2_full[side] = (unit2 * vectors[2:3] + vectors[3:4]).astype(BF)
    copy_a2 = send(a2_full.at[side], a2_full.at[side], sems, 2, place.twin)
    copy_a2.wait()
    a2 = a2_full[...].reshape(full, features)
    a2_ref[...] = a2

    slot = iota((experts * slots, full), 0) + side * (experts * slots)
    hit = (trow_ref[0:1, :] == slot) | (trow_ref[1:2, :] == slot)
    disp[...] = nn(hit.astype(F32).astype(BF), a2).astype(BF).reshape(experts, slots, features)
    sent = exchange_rows(place, disp, rows, sems, 3, lambda ref, group: ref.at[group])

    lane = iota((1, 128), 1)
    valid = (lane >= 4) & (lane < 4 + experts)
    logits = jnp.where(valid, nn(a2, block), -1e30)
    odds = jnp.where(valid, jnp.exp(logits - jnp.max(logits, axis=-1, keepdims=True)), 0.0)
    rp_ref[...] = odds / jnp.sum(odds, axis=-1, keepdims=True)

    fetch_inner.wait()
    fetch_outer.wait()
    for copy in sent:
        copy.wait()
    mine = rows[...].reshape(experts * slots, features)
    rows_ref[...] = mine
    acc[...] = jnp.zeros_like(acc)

    def tile_step(step, carry):
        cols = pl.ds(pl.multiple_of(step * TILE, TILE), TILE)
        pre = nn(rows_ref[...], inner[:, cols])
        pre_ref[:, cols] = pre
        act = (0.5 * pre * (1.0 + gelu_tanh(pre))).astype(BF)
        acc[...] += nt(act, outer[:, cols])
        return carry

    lax.fori_loop(0, ff // TILE, tile_step, 0)
    outb[...] = acc[...].astype(BF).reshape(experts, slots, features)
    sent = exchange_rows(
        place, outb, ret, sems, 2 + experts, lambda ref, group: ref.at[side, group]
    )
    for copy in sent:
        copy.wait()
    copy_ret = send(ret.at[side], ret.at[side], sems, 1 + 2 * experts, place.twin)
    copy_ret.wait()
    home = ret[...].reshape(2 * experts * slots, features)
    own_rows = pl.ds(pl.multiple_of(side * ROWS, ROWS), ROWS)
    table = tcol_ref[own_rows, :]
    odds = rp_ref[own_rows, :]
    column = iota((ROWS, 2 * experts * slots), 1)
    y = h1
    for choice in range(2):
        pick = (table[:, choice:choice + 1] == column).astype(F32).astype(BF)
        chosen = nn(pick, home)
        chosen_ref[choice] = chosen.astype(BF)
        hot = table[:, 2 + choice:3 + choice] + 4 == lane
        y = y + chosen * jnp.sum(jnp.where(hot, odds, 0.0), axis=-1, keepdims=True)
    y_ref[...] = y.astype(BF)


def bwd_kernel(cfg, *refs):
    section, experts, spread, wide = cfg
    (dy_ref, z_ref, h1_ref, a1_ref, qkv_ref, probs_ref, att_ref, a2_ref, rp_ref, rows_ref,
     pre_ref, chosen_ref, trow_ref, tcol_ref, attn_hbm, inner_hbm, outer_hbm) = refs[:17]
    (dz_ref, gin_ref, gout_ref, gattn_ref,
     attn, inner, outer, dy_full, disp, dexp, acc, outb, ret, act_all, dpre_all, lhs_t,
     dbr_full, dqkv, part, came, wsem, sems) = refs[17:]
    place = Place(experts, spread)
    side = place.side
    features = z_ref.shape[1]
    ff = inner.shape[1]
    slots = CAP // 2
    full = 2 * ROWS
    fetch = pltpu.make_async_copy(attn_hbm.at[section], attn, wsem.at[2])
    fetch.start()
    fetch_inner = pltpu.make_async_copy(inner_hbm.at[section], inner, wsem.at[0])
    fetch_inner.start()
    fetch_outer = pltpu.make_async_copy(outer_hbm.at[section], outer, wsem.at[1])
    fetch_outer.start()
    place.greet()

    dy_full[side] = dy_ref[...]
    copy_dy = send(dy_full.at[side], dy_full.at[side], sems, 0, place.twin)
    copy_dy.wait()
    lane = iota((1, 128), 1)
    grad = dy_full[...].reshape(full, features).astype(F32)
    slot = iota((experts * slots, full), 0) + side * (experts * slots)
    total = jnp.zeros((experts * slots, features), F32)
    for choice in range(2):
        hot = tcol_ref[:, 2 + choice:3 + choice] + 4 == lane
        gate = jnp.sum(jnp.where(hot, rp_ref[...], 0.0), axis=-1, keepdims=True)
        hit = (trow_ref[choice:choice + 1, :] == slot).astype(F32).astype(BF)
        total = total + nn(hit, (gate * grad).astype(BF))
    disp[...] = total.astype(BF).reshape(experts, slots, features)
    sent = exchange_rows(place, disp, dexp, sems, 1, lambda ref, group: ref.at[group])

    fetch.wait()
    block = attn[:, 4 * wide:]
    vectors = block.astype(F32).T
    own_rows = pl.ds(pl.multiple_of(side * ROWS, ROWS), ROWS)
    table = tcol_ref[own_rows, :]
    odds = rp_ref[own_rows, :]
    dy = dy_ref[...].astype(F32)
    drouter = jnp.zeros((ROWS, 128), F32)
    for choice in range(2):
        dgate = jnp.sum(dy * chosen_ref[choice].astype(F32), axis=-1, keepdims=True)
        dgate = jnp.where(table[:, choice:choice + 1] >= 0, dgate, 0.0)
        hot = table[:, 2 + choice:3 + choice] + 4 == lane
        drouter = drouter + jnp.where(hot, dgate, 0.0)
    dlogit = odds * (drouter - jnp.sum(odds * drouter, axis=-1, keepdims=True))
    high = dlogit.astype(BF)
    rest = (dlogit - high.astype(F32)).astype(BF)
    da2 = nt(high, block) + nt(rest, block)
    a2 = a2_ref[own_rows, :]
    grad_router = tn(a2, high) + tn(a2, rest)

    fetch_inner.wait()
    fetch_outer.wait()
    for copy in sent:
        copy.wait()
    acc[...] = jnp.zeros_like(acc)

    def tile_step(step, carry):
        cols = pl.ds(pl.multiple_of(step * TILE, TILE), TILE)
        grad_act = nn(dexp[...].reshape(experts * slots, features), outer[:, cols])
        pre = pre_ref[:, cols]
        tanh = gelu_tanh(pre)
        act_all[:, cols] = (0.5 * pre * (1.0 + tanh)).astype(BF)
        slope = 0.5 * (1.0 + tanh) + 0.5 * pre * (1.0 - tanh * tanh) * (
            0.7978845608028654 * (1.0 + 3 * 0.044715 * pre * pre)
        )
        dpre = (grad_act * slope).astype(BF)
        dpre_all[:, cols] = dpre
        acc[...] += nt(dpre, inner[:, cols])
        return carry

    lax.fori_loop(0, ff // TILE, tile_step, 0)
    outb[...] = acc[...].astype(BF).reshape(experts, slots, features)
    sent = exchange_rows(
        place, outb, ret, sems, experts, lambda ref, group: ref.at[side, group]
    )
    lhs_t[0] = dexp[...].reshape(experts * slots, features).T
    lhs_t[1] = rows_ref[...].T

    def grad_step(step, carry):
        cols = pl.ds(pl.multiple_of(step * TILE, TILE), TILE)
        gout_ref[:, cols] = nn(lhs_t[0], act_all[:, cols]).astype(BF)
        gin_ref[:, cols] = nn(lhs_t[1], dpre_all[:, cols]).astype(BF)
        return carry

    lax.fori_loop(0, ff // TILE, grad_step, 0)
    for copy in sent:
        copy.wait()
    copy_ret = send(ret.at[side], ret.at[side], sems, 2 * experts - 1, place.twin)
    copy_ret.wait()
    home = ret[...].reshape(2 * experts * slots, features)
    column = iota((ROWS, 2 * experts * slots), 1)
    pick = (table[:, 0:1] == column) | (table[:, 1:2] == column)
    da2 = da2 + nn(pick.astype(F32).astype(BF), home)
    unit2, inv2 = norm_stats(h1_ref[...])
    grad_gain2 = jnp.sum(da2 * unit2, axis=0, keepdims=True)
    grad_bias2 = jnp.sum(da2, axis=0, keepdims=True)
    dh1 = dy + norm_back(da2, unit2, inv2, vectors[2:3])
    dbr_full[side] = dh1.astype(BF)
    copy_dbr = send(dbr_full.at[side], dbr_full.at[side], sems, 2 * experts, place.twin)
    copy_dbr.wait()
    dbr = dbr_full[...].reshape(full, features)
    gattn_ref[:, 3 * wide:4 * wide] = tn(dbr, att_ref[...]).astype(BF)
    datt = nn(dbr, attn[:, 3 * wide:4 * wide]).astype(BF)
    low_lane = lane < HEAD_DIM
    for pair in range(wide // 128):
        lanes = slice(pair * 128, (pair + 1) * 128)
        q, k, v = qkv_ref[0, :, lanes], qkv_ref[1, :, lanes], qkv_ref[2, :, lanes]
        wide_datt = datt[:, lanes]
        dq = dk = dv = 0.0
        for which in range(2):
            mask = low_lane if which == 0 else ~low_lane
            zero = jnp.zeros_like(q)
            probs = probs_ref[2 * pair + which]
            head = jnp.where(mask, wide_datt, zero)
            dv = dv + tn(probs.astype(BF), head)
            dprobs = nt(head, v)
            dscores = probs * (dprobs - jnp.sum(probs * dprobs, axis=-1, keepdims=True))
            dscores = dscores.astype(BF)
            dq = dq + nn(dscores, jnp.where(mask, k, zero))
            dk = dk + tn(dscores, jnp.where(mask, q, zero))
        dqkv[0, :, lanes] = (dq * HEAD_DIM**-0.5).astype(BF)
        dqkv[1, :, lanes] = (dk * HEAD_DIM**-0.5).astype(BF)
        dqkv[2, :, lanes] = dv.astype(BF)
    da1 = jnp.zeros((full, features), F32)
    for j in range(3):
        da1 = da1 + nt(dqkv[j], attn[:, j * wide:(j + 1) * wide])
    part[...] = da1.reshape(2, ROWS, features)
    copy_part = send(part.at[1 - side], came, sems, 2 * experts + 1, place.twin)
    for j in range(3):
        gattn_ref[:, j * wide:(j + 1) * wide] = tn(a1_ref[...], dqkv[j]).astype(BF)
    unit1, inv1 = norm_stats(z_ref[...].astype(F32))
    copy_part.wait()
    da1 = part[side] + came[...]
    grad_gain1 = jnp.sum(da1 * unit1, axis=0, keepdims=True)
    grad_bias1 = jnp.sum(da1, axis=0, keepdims=True)
    dz_ref[...] = dh1 + norm_back(da1, unit1, inv1, vectors[0:1])
    small = jnp.concatenate(
        [grad_gain1, grad_bias1, grad_gain2, grad_bias2, jnp.zeros((124, features), F32)], axis=0
    )
    gattn_ref[:, 4 * wide:] = (small.T + grad_router).astype(BF)


def forward(section, dims, z, trow, tcol, weights):
    experts, spread, features, wide, ff = dims
    full, slots = 2 * ROWS, CAP // 2
    heads = wide // HEAD_DIM
    vmem = pl.BlockSpec(memory_space=pltpu.VMEM)
    hbm = pl.BlockSpec(memory_space=pltpu.HBM)
    kernel = functools.partial(fwd_kernel, (section, experts, spread, wide))
    shape = jax.ShapeDtypeStruct
    return pl.pallas_call(
        kernel,
        out_shape=(
            shape((ROWS, features), BF),
            shape((ROWS, features), F32),
            shape((full, features), BF),
            shape((3, full, wide), BF),
            shape((heads, full, full), F32),
            shape((full, wide), BF),
            shape((full, features), BF),
            shape((full, 128), F32),
            shape((experts * slots, features), BF),
            shape((experts * slots, ff), F32),
            shape((2, ROWS, features), BF),
        ),
        in_specs=[vmem] * 3 + [hbm] * 3,
        out_specs=(vmem,) * 11,
        scratch_shapes=[
            pltpu.VMEM((features, 4 * wide + 128), BF),
            pltpu.VMEM((features, ff), BF),
            pltpu.VMEM((features, ff), BF),
            pltpu.VMEM((2, ROWS, features), BF),
            pltpu.VMEM((2, ROWS, features), F32),
            pltpu.VMEM((ROWS, features), F32),
            pltpu.VMEM((2, ROWS, features), BF),
            pltpu.VMEM((experts, slots, features), BF),
            pltpu.VMEM((experts, slots, features), BF),
            pltpu.VMEM((experts * slots, features), F32),
            pltpu.VMEM((experts, slots, features), BF),
            pltpu.VMEM((2, experts, slots, features), BF),
            pltpu.SemaphoreType.DMA((3,)),
            pltpu.SemaphoreType.DMA((2, 2 + 2 * experts)),
        ],
        compiler_params=pltpu.CompilerParams(
            collective_id=section, has_side_effects=True, vmem_limit_bytes=56 * 2**20
        ),
        name=f"section_forward_{section}",
    )(z, trow, tcol, *weights)


def backward(section, dims, dy, z, saved, trow, tcol, weights):
    experts, spread, features, wide, ff = dims
    full, slots = 2 * ROWS, CAP // 2
    vmem = pl.BlockSpec(memory_space=pltpu.VMEM)
    hbm = pl.BlockSpec(memory_space=pltpu.HBM)
    kernel = functools.partial(bwd_kernel, (section, experts, spread, wide))
    shape = jax.ShapeDtypeStruct
    return pl.pallas_call(
        kernel,
        out_shape=(
            shape((ROWS, features), F32),
            shape((features, ff), BF),
            shape((features, ff), BF),
            shape((features, 4 * wide + 128), BF),
        ),
        in_specs=[vmem] * 14 + [hbm] * 3,
        out_specs=(vmem,) * 4,
        scratch_shapes=[
            pltpu.VMEM((features, 4 * wide + 128), BF),
            pltpu.VMEM((features, ff), BF),
            pltpu.VMEM((features, ff), BF),
            pltpu.VMEM((2, ROWS, features), BF),
            pltpu.VMEM((experts, slots, features), BF),
            pltpu.VMEM((experts, slots, features), BF),
            pltpu.VMEM((experts * slots, features), F32),
            pltpu.VMEM((experts, slots, features), BF),
            pltpu.VMEM((2, experts, slots, features), BF),
            pltpu.VMEM((experts * slots, ff), BF),
            pltpu.VMEM((experts * slots, ff), BF),
            pltpu.VMEM((2, features, experts * slots), BF),
            pltpu.VMEM((2, ROWS, features), BF),
            pltpu.VMEM((3, full, wide), BF),
            pltpu.VMEM((2, ROWS, features), F32),
            pltpu.VMEM((ROWS, features), F32),
            pltpu.SemaphoreType.DMA((3,)),
            pltpu.SemaphoreType.DMA((2, 2 + 2 * experts)),
        ],
        compiler_params=pltpu.CompilerParams(
            collective_id=2 + section, has_side_effects=True, vmem_limit_bytes=56 * 2**20
        ),
        name=f"section_backward_{section}",
    )(dy, z, *saved, trow, tcol, *weights)


def swap_planes(values):
    return lax.ppermute(values, "pipe", [(0, 1), (1, 0)])


def swap_sides(values):
    return lax.ppermute(values, "tensor", [(0, 1), (1, 0)])


def pick(values, index, axis=0):
    return lax.dynamic_index_in_dim(values, index, axis, keepdims=False)


def spread_weights(dims, attn, inner, outer):
    experts, spread, features, _, ff = dims
    shape = jax.ShapeDtypeStruct
    hbm = pl.BlockSpec(memory_space=pltpu.HBM)
    count = 3 * (experts - 1) + 3 * experts * (2 * spread - 1) + 2 * 2 * experts * spread
    return pl.pallas_call(
        functools.partial(spread_kernel, (experts, spread)),
        out_shape=(
            shape((2, features, attn.shape[1]), BF),
            shape((2, features, ff), BF),
            shape((2, features, ff), BF),
        ),
        in_specs=[hbm] * 3,
        out_specs=(hbm,) * 3,
        scratch_shapes=[
            pltpu.SemaphoreType.DMA((3,)),
            pltpu.SemaphoreType.DMA((2, count)),
        ],
        compiler_params=pltpu.CompilerParams(
            collective_id=4, has_side_effects=True, vmem_limit_bytes=56 * 2**20
        ),
        name="spread_weights",
    )(attn, inner, outer)


def reduce_grads(dims, inner, outer, attn):
    experts, spread, features, _, ff = dims
    half = ff // 2
    shard = features // (experts * spread)
    broad = attn[0].shape[1]
    shape = jax.ShapeDtypeStruct
    hbm = pl.BlockSpec(memory_space=pltpu.HBM)
    vmem = pl.BlockSpec(memory_space=pltpu.VMEM)
    blocks = 4 * experts * spread
    count = blocks + experts * (5 * (spread - 1) + 2 * spread + 2) + 3 * (experts - 1)
    return pl.pallas_call(
        functools.partial(reduce_kernel, (experts, spread)),
        out_shape=(
            shape((experts, shard, half), BF),
            shape((experts, shard, half), BF),
            shape((shard, broad), F32),
        ),
        in_specs=[hbm] * 6,
        out_specs=(vmem,) * 3,
        scratch_shapes=[
            pltpu.VMEM((2, 2, experts, spread, shard, half), BF),
            pltpu.VMEM((2, 2, experts, spread, shard, half), BF),
            pltpu.VMEM((2, experts, spread * shard, broad), BF),
            pltpu.VMEM((2, experts, spread - 1, shard, half), BF),
            pltpu.VMEM((experts, shard, half), BF),
            pltpu.VMEM((experts, spread, shard, half), BF),
            pltpu.VMEM((experts, spread - 1, shard, half), BF),
            pltpu.VMEM((2, experts, spread - 1, shard, broad), BF),
            pltpu.VMEM((experts, spread, shard, broad), BF),
            pltpu.VMEM((experts, spread - 1, shard, broad), BF),
            pltpu.VMEM((experts, shard, broad), BF),
            pltpu.VMEM((experts, shard, half), BF),
            pltpu.VMEM((experts, shard, half), BF),
            pltpu.VMEM((experts, shard, broad), BF),
            pltpu.SemaphoreType.DMA((blocks + 2 * experts,)),
            pltpu.SemaphoreType.DMA((2, count)),
        ],
        compiler_params=pltpu.CompilerParams(
            collective_id=5, has_side_effects=True, vmem_limit_bytes=56 * 2**20
        ),
        name="reduce_grads",
    )(*inner, *outer, *attn)


def body(
    images_in,
    out_grad,
    attn_gain,
    attn_bias,
    qkv_weight,
    proj_weight,
    moe_gain,
    moe_bias,
    router_weight,
    inner_weight,
    outer_weight,
    expert_ids,
    slot_ids,
):
    plane = lax.axis_index("pipe")
    micro, local, piece, features = images_in.shape
    shard, wide = qkv_weight.shape[2], qkv_weight.shape[3]
    experts = router_weight.shape[2]
    half = inner_weight.shape[3]
    spread = lax.axis_size("dp") // experts
    dims = (experts, spread, features, wide, 2 * half)
    packed = jnp.concatenate(
        [qkv_weight[0, 0], qkv_weight[0, 1], qkv_weight[0, 2], proj_weight[0].T,
         jnp.stack([attn_gain[0], attn_bias[0], moe_gain[0], moe_bias[0]], axis=1),
         router_weight[0], jnp.zeros((shard, 128 - 4 - experts), BF)],
        axis=1,
    )
    weights = spread_weights(
        dims, packed, inner_weight[0], outer_weight[0].transpose(0, 2, 1)
    )

    def my_image(values):
        return jnp.pad(pick(values, plane)[0], ((0, ROWS - piece), (0, 0)))

    routes = expert_ids[0, :, 0]
    slots = slot_ids[0, :, 0]
    kept = slots < CAP
    codes = jnp.where(
        kept, slots // (CAP // 2) * (experts * CAP // 2) + routes * (CAP // 2) + slots % (CAP // 2),
        -1,
    )
    table = jnp.concatenate([codes, routes], axis=-1)
    table_own = pick(table, plane)
    table_other = swap_planes(pick(table, 1 - plane))
    tables = []
    for section in range(2):
        values = jnp.where(plane == section, table_own, table_other).reshape(2, piece, 4)
        values = jnp.pad(values, ((0, 0), (0, ROWS - piece), (0, 0)), constant_values=-1)
        values = values.reshape(2 * ROWS, 4)
        tables.append((
            jnp.pad(values.T, ((0, 4), (0, 0)), constant_values=-1),
            jnp.pad(values, ((0, 0), (0, 124)), constant_values=-1),
        ))

    z0 = my_image(images_in)
    y0, *saved0 = forward(0, dims, z0, *tables[0], weights)
    y1, *saved1 = forward(1, dims, y0, *tables[1], weights)
    dz1, *grads1 = backward(1, dims, my_image(out_grad), y0, saved1, *tables[1], weights)
    dz0, *grads0 = backward(0, dims, dz1.astype(BF), z0, saved0, *tables[0], weights)

    inner_out, outer_out, packed_out = reduce_grads(
        dims, (grads0[0], grads1[0]), (grads0[1], grads1[1]), (grads0[2], grads1[2])
    )
    inner_out, outer_out = inner_out.astype(F32), outer_out.astype(F32)
    own_small = packed_out[:, 4 * wide:4 * wide + 4 + experts]
    own_small = own_small + swap_sides(own_small)

    def shape_out(first, second):
        first, second = first[:piece], second[:piece]
        keep = jnp.where(plane == 0, first, second)
        came = swap_planes(jnp.where(plane == 0, second, first))
        both = jnp.stack([jnp.where(plane == 0, keep, came), jnp.where(plane == 0, came, keep)])
        return both.reshape(1, micro, local, piece, features)

    return (
        shape_out(y0, y1),
        shape_out(dz0, dz1),
        own_small[:, 0][None],
        own_small[:, 1][None],
        jnp.stack([packed_out[:, j * wide:(j + 1) * wide] for j in range(3)])[None],
        packed_out[:, 3 * wide:4 * wide].T[None],
        own_small[:, 2][None],
        own_small[:, 3][None],
        own_small[:, 4:][None],
        inner_out[None],
        outer_out.transpose(0, 2, 1)[None],
    )


def solution(mesh):
    in_specs = (
        P(None, "dp", "tensor", None),
        P(None, "dp", "tensor", None),
        P("pipe", "dp"),
        P("pipe", "dp"),
        P("pipe", None, "dp", "tensor"),
        P("pipe", "tensor", "dp"),
        P("pipe", "dp"),
        P("pipe", "dp"),
        P("pipe", "dp", None),
        P("pipe", None, "dp", "tensor"),
        P("pipe", None, "tensor", "dp"),
        P("pipe", None, "dp", None, None),
        P("pipe", None, "dp", None, None),
    )
    out_specs = (
        P("pipe", None, "dp", "tensor", None),
        P("pipe", None, "dp", "tensor", None),
        P("pipe", "dp"),
        P("pipe", "dp"),
        P("pipe", None, "dp", "tensor"),
        P("pipe", "tensor", "dp"),
        P("pipe", "dp"),
        P("pipe", "dp"),
        P("pipe", "dp", None),
        P("pipe", None, "dp", "tensor"),
        P("pipe", None, "tensor", "dp"),
    )
    return jax.shard_map(body, mesh=mesh, in_specs=in_specs, out_specs=out_specs, check_vma=False)
```

```python
import functools
import math

import jax
import jax.numpy as jnp
from jax import lax
from jax.experimental import pallas as pl
from jax.experimental.pallas import tpu as pltpu
from jax.sharding import PartitionSpec as P

HEAD_DIM = 64
LIVE = 197
CAP = 128
ROWS = 128
EPS = 1e-06
TILE = 384
LAG = 2
BF = jnp.bfloat16
F32 = jnp.float32
MESH = pl.DeviceIdType.MESH


def nn(left, right):
    return lax.dot_general(left, right, (((1,), (0,)), ((), ())), preferred_element_type=F32)


def nt(left, right):
    return lax.dot_general(left, right, (((1,), (1,)), ((), ())), preferred_element_type=F32)


def tn(left, right):
    return lax.dot_general(left, right, (((0,), (0,)), ((), ())), preferred_element_type=F32)


def norm_stats(values):
    centre = values - jnp.mean(values, axis=-1, keepdims=True)
    inv = lax.rsqrt(jnp.mean(centre * centre, axis=-1, keepdims=True) + EPS)
    return centre * inv, inv


def norm_back(grad, unit, inv, gain):
    scaled = grad * gain
    return (
        scaled
        - jnp.mean(scaled, axis=-1, keepdims=True)
        - unit * jnp.mean(scaled * unit, axis=-1, keepdims=True)
    ) * inv


def iota(shape, dim):
    return lax.broadcasted_iota(jnp.int32, shape, dim)


class Place:
    def __init__(self, experts, spread):
        self.experts, self.spread = experts, spread
        self.plane = lax.axis_index("pipe")
        self.side = lax.axis_index("tensor")
        dp = lax.axis_index("dp")
        self.mine = dp // spread
        self.column = lax.rem(dp, spread)
        self.twin = {"tensor": 1 - self.side}
        self.across = {"pipe": 1 - self.plane}

    def ahead(self, steps):
        return lax.rem(self.mine + steps, self.experts)

    def behind(self, steps):
        return lax.rem(self.mine + self.experts - steps, self.experts)

    def peer(self, group):
        return {"dp": group * self.spread + self.column}

    def beside(self, shift):
        return {"dp": self.mine * self.spread + lax.rem(self.column + shift, self.spread)}

    def left(self, shift):
        return lax.rem(self.column + self.spread - shift, self.spread)

    def greet(self, everyone=False):
        barrier = pltpu.get_barrier_semaphore()
        devices = [self.twin]
        devices += [self.peer(self.ahead(steps)) for steps in range(1, self.experts)]
        devices += [self.beside(shift) for shift in range(1, self.spread)]
        if everyone:
            devices += [self.across]
        for device in devices:
            pl.semaphore_signal(barrier, inc=1, device_id=device, device_id_type=MESH)
        pl.semaphore_wait(barrier, len(devices))


def send(source, target, sems, slot, device):
    copy = pltpu.make_async_remote_copy(
        src_ref=source,
        dst_ref=target,
        send_sem=sems.at[0, slot],
        recv_sem=sems.at[1, slot],
        device_id=device,
        device_id_type=MESH,
    )
    copy.start()
    return copy


class Slots:
    def __init__(self, sems):
        self.sems, self.next, self.sends = sems, 0, []

    def send(self, source, target, device):
        copy = send(source, target, self.sems, self.next, device)
        self.next += 1
        self.sends.append(copy)
        return copy

    def drain(self):
        for copy in self.sends:
            copy.wait_send()


class Spread:
    def __init__(self, place, slots, local, shards, stage, whole):
        self.place, self.slots, self.local = place, slots, local
        self.shards, self.stage, self.whole = shards, stage, whole
        experts = place.experts
        far = list(range(2, experts, 2)) + list(range(1, experts, 2))
        self.away = [(0, steps) for steps in far]
        self.away += [(kind, steps) for steps in far for kind in (1, 2)]
        self.pieces = [(kind, 0) for kind in range(3)] + self.away
        self.over_groups, self.over_columns, self.over_planes, self.late = {}, {}, {}, {}
        self.twins, self.kept = [], []

    def where(self, kind, section, group, col):
        place = self.place
        shard = self.shards[0].shape[0]
        row = (group * place.spread + col) * shard
        rows = pl.ds(pl.multiple_of(row, math.gcd(shard, 16)), shard)
        if kind == 0:
            return self.whole[0].at[section, rows]
        return self.whole[kind].at[section, place.side, rows]

    def held(self, kind, steps):
        place = self.place
        if kind == 0:
            if steps == 0:
                return self.shards[0]
            return self.where(0, place.plane, place.behind(steps), place.column)
        if steps == 0:
            return self.shards[kind].at[place.mine]
        return self.stage.at[kind - 1, steps]

    def start_groups(self, count):
        place = self.place
        for kind, steps in self.away[len(self.over_groups):len(self.over_groups) + count]:
            group = place.ahead(steps)
            if kind == 0:
                source = self.shards[0]
                target = self.where(0, place.plane, place.mine, place.column)
            else:
                source, target = self.shards[kind].at[group], self.stage.at[kind - 1, steps]
            self.over_groups[kind, steps] = self.slots.send(source, target, place.peer(group))

    def to_twin(self, kind, source, target):
        if kind:
            self.twins.append(self.slots.send(source, target, self.place.twin))

    def first_hop(self, kind, steps):
        place, slots = self.place, self.slots
        if steps:
            self.over_groups[kind, steps].wait_recv()
            self.start_groups(1)
        held = self.held(kind, steps)
        target = self.where(kind, place.plane, place.behind(steps), place.column)
        own = held if kind == 0 else held.at[place.column]
        for shift in range(1, place.spread):
            col = lax.rem(place.column + shift, place.spread)
            part = held if kind == 0 else held.at[col]
            self.over_columns[kind, steps, shift] = slots.send(part, target, place.beside(shift))
        self.over_planes[kind, steps] = slots.send(own, target, place.across)
        self.to_twin(kind, own, target)
        if kind or steps == 0:
            copy = pltpu.make_async_copy(own, target, self.local.at[len(self.kept)])
            copy.start()
            self.kept.append(copy)

    def second_hop(self, kind, steps):
        place, slots = self.place, self.slots
        group = place.behind(steps)
        if kind == 0:
            self.over_planes[kind, steps].wait_recv()
            target = self.where(kind, 1 - place.plane, group, place.column)
            for shift in range(1, place.spread):
                self.late[kind, steps, shift] = slots.send(target, target, place.beside(shift))
            return
        for shift in range(1, place.spread):
            self.over_columns[kind, steps, shift].wait_recv()
            target = self.where(kind, place.plane, group, place.left(shift))
            self.late[kind, steps, shift] = slots.send(target, target, place.across)
            self.to_twin(kind, target, target)

    def last_hop(self, kind, steps):
        place = self.place
        group = place.behind(steps)
        if kind:
            self.over_planes[kind, steps].wait_recv()
            target = self.where(kind, 1 - place.plane, group, place.column)
            self.to_twin(kind, target, target)
        for shift in range(1, place.spread):
            if kind == 0:
                self.over_columns[kind, steps, shift].wait_recv()
            self.late[kind, steps, shift].wait_recv()
            target = self.where(kind, 1 - place.plane, group, place.left(shift))
            self.to_twin(kind, target, target)

    def hops(self, begin, end):
        pieces = self.pieces
        for at in range(begin, end):
            if at < len(pieces):
                self.first_hop(*pieces[at])
            if LAG <= at < len(pieces) + LAG:
                self.second_hop(*pieces[at - LAG])
            if at >= 2 * LAG:
                self.last_hop(*pieces[at - 2 * LAG])

    def finish(self):
        for copy in self.twins:
            copy.wait_recv()
        for copy in self.kept:
            copy.wait()


def spread_kernel(cfg, attn_own, inner_own, outer_own, attn_all, inner_all, outer_all, stage,
                  lsem, sems):
    place = Place(*cfg)
    slots = Slots(sems)
    place.greet(everyone=True)
    spread = Spread(place, slots, lsem, (attn_own, inner_own, outer_own), stage,
                    (attn_all, inner_all, outer_all))
    spread.start_groups(3)
    spread.hops(0, len(spread.pieces) + 2 * LAG)
    spread.finish()
    slots.drain()


def add_into(target, came):
    target[...] = (target[...].astype(F32) + came[...].astype(F32)).astype(BF)


def reduce_kernel(cfg, *refs):
    experts, spread = cfg
    grads, gattn = (refs[0:2], refs[2:4]), refs[4:6]
    (inner_out, outer_out, attn_out,
     acc, twin_in, planes_in, blocks, z_in, attn_acc, at_cols, at_planes, z_attn,
     lsem, sems) = refs[6:]
    place = Place(experts, spread)
    slots = Slots(sems)
    plane, side, column = place.plane, place.side, place.column
    shard = acc.shape[4]
    local_slot = iter(range(lsem.shape[0]))
    place.greet(everyone=True)
    order = list(range(2, experts, 2)) + list(range(1, experts, 2)) + [0]
    whole = range(2)
    aligned = math.gcd(shard, 16)

    halves, attn_local, hops = {}, {}, {}
    for steps in order:
        group = place.ahead(steps)
        for section in whole:
            copy = pltpu.make_async_copy(
                gattn[section].at[
                    pl.ds(pl.multiple_of(group * spread * shard, aligned), spread * shard)
                ],
                attn_acc.at[section, steps], lsem.at[next(local_slot)],
            )
            copy.start()
            attn_local[steps, section] = copy
            for matrix in whole:
                for col in range(spread):
                    rows = pl.ds(
                        pl.multiple_of((group * spread + col) * shard, aligned), shard
                    )
                    source = grads[matrix][section]
                    away = slots.send(
                        source.at[1 - side, rows], twin_in.at[section, matrix, steps, col],
                        place.twin,
                    )
                    own = pltpu.make_async_copy(
                        source.at[side, rows], acc.at[section, matrix, steps, col],
                        lsem.at[next(local_slot)],
                    )
                    own.start()
                    halves[steps, section, matrix, col] = (away, own)

    def attn_block(section, steps, col):
        return attn_acc.at[section, steps, pl.ds(pl.multiple_of(col * shard, aligned), shard)]

    def first(kind, steps):
        if kind == 2:
            for section in whole:
                attn_local[steps, section].wait()
                for shift in range(1, spread):
                    hops["ax", steps, section, shift] = slots.send(
                        attn_block(section, steps, lax.rem(column + shift, spread)),
                        at_cols.at[section, steps, shift - 1], place.beside(shift),
                    )
            return
        for col in range(spread):
            for section in whole:
                away, own = halves[steps, section, kind, col]
                own.wait()
                away.wait_recv()
                add_into(acc.at[section, kind, steps, col], twin_in.at[section, kind, steps, col])
            hops["y", kind, steps, col] = slots.send(
                acc.at[1 - plane, kind, steps, col], planes_in.at[kind, steps, col], place.across
            )

    def second(kind, steps):
        if kind == 2:
            for section in whole:
                for shift in range(1, spread):
                    hops["ax", steps, section, shift].wait_recv()
                    add_into(attn_block(section, steps, column),
                             at_cols.at[section, steps, shift - 1])
            hops["ay", steps] = slots.send(
                attn_block(1 - plane, steps, column), at_planes.at[steps], place.across
            )
            return
        for col in range(spread):
            hops["y", kind, steps, col].wait_recv()
            add_into(acc.at[plane, kind, steps, col], planes_in.at[kind, steps, col])
        for shift in range(1, spread):
            hops["x", kind, steps, shift] = slots.send(
                acc.at[plane, kind, steps, lax.rem(column + shift, spread)],
                blocks.at[kind, steps, column], place.beside(shift),
            )
        blocks[kind, steps, column] = acc[plane, kind, steps, column]

    def third(kind, steps):
        device = place.peer(place.ahead(steps))
        if kind == 2:
            hops["ay", steps].wait_recv()
            add_into(attn_block(plane, steps, column), at_planes.at[steps])
            if steps:
                hops["az", steps] = slots.send(
                    attn_block(plane, steps, column), z_attn.at[steps], device
                )
            return
        for shift in range(1, spread):
            hops["x", kind, steps, shift].wait_recv()
        if steps:
            hops["z", kind, steps] = slots.send(
                blocks.at[kind, steps], z_in.at[kind, steps], device
            )

    pieces = [(kind, steps) for steps in order for kind in (2, 1, 0)]
    for at in range(len(pieces) + 2 * LAG):
        if at < len(pieces):
            first(*pieces[at])
        if LAG <= at < len(pieces) + LAG:
            second(*pieces[at - LAG])
        if at >= 2 * LAG:
            third(*pieces[at - 2 * LAG])
    outs = (inner_out, outer_out)
    narrow = acc.shape[5]

    def put(kind, group, source):
        for col in range(spread):
            outs[kind][group, :, col * narrow:(col + 1) * narrow] = source[col]

    for kind in whole:
        put(kind, place.mine, blocks.at[kind, 0])
    total = attn_block(plane, 0, column)[...].astype(F32)
    for steps in order[:-1]:
        hops["az", steps].wait_recv()
        total = total + z_attn[steps].astype(F32)
        for kind in whole:
            hops["z", kind, steps].wait_recv()
            put(kind, place.behind(steps), z_in.at[kind, steps])
    attn_out[...] = total
    slots.drain()


def gather_rows(place, out, rows, slots):
    here = place.mine
    column = place.column
    over_groups, over_columns = {}, []
    for steps in range(1, place.experts):
        group = place.ahead(steps)
        over_groups[steps] = slots.send(out.at[group], rows.at[column, here], place.peer(group))
    for shift in range(1, place.spread):
        over_columns.append(slots.send(out.at[here], rows.at[column, here], place.beside(shift)))
    rows[column, here] = out[here]

    def finish():
        for steps in range(1, place.experts):
            over_groups[steps].wait_recv()
            part = rows.at[column, place.behind(steps)]
            for shift in range(1, place.spread):
                over_columns.append(slots.send(part, part, place.beside(shift)))
        for copy in over_columns:
            copy.wait_recv()

    return finish


def return_rows(place, acc, outb, parts, ret, slots):
    column, slots_in = place.column, outb.shape[2]
    width = place.experts * slots_in

    def block(col, group):
        return pl.ds(pl.multiple_of(col * width + group * slots_in, slots_in), slots_in)

    order = list(range(2, place.experts, 2)) + list(range(1, place.experts, 2)) + [0]
    over_columns, home = {}, []
    for steps in order:
        group = place.ahead(steps)
        for shift in range(1, place.spread):
            col = lax.rem(column + shift, place.spread)
            outb[col, group] = acc[block(col, group), :].astype(BF)
            over_columns[steps, shift] = slots.send(
                outb.at[col, group], parts.at[shift - 1, steps], place.beside(shift)
            )
    for steps in order:
        group = place.ahead(steps)
        total = acc[block(column, group), :]
        for shift in range(1, place.spread):
            over_columns[steps, shift].wait_recv()
            total = total + parts[shift - 1, steps].astype(F32)
        if steps:
            outb[column, group] = total.astype(BF)
            home.append(slots.send(
                outb.at[column, group], ret.at[place.side, place.mine], place.peer(group)
            ))
        else:
            ret[place.side, place.mine] = total.astype(BF)
    return home


def gelu_tanh(pre):
    return jnp.tanh(0.7978845608028654 * (pre + 0.044715 * pre * pre * pre))


def fwd_kernel(cfg, *refs):
    section, experts, spread, wide = cfg
    z_ref, trow_ref, tcol_ref, attn_hbm, inner_hbm, outer_hbm = refs[:6]
    (y_ref, h1_ref, a1_ref, qkv_ref, probs_ref, att_ref, a2_ref, rp_ref, rows_ref, pre_ref,
     chosen_ref,
     attn, inner, outer, a1_full, part, came, a2_full, disp, rows, acc, outb, parts, ret,
     wsem, sems) = refs[6:]
    place = Place(experts, spread)
    side = place.side
    features = z_ref.shape[1]
    narrow = inner.shape[2]
    tile = TILE if narrow % TILE == 0 else narrow
    tiles = narrow // tile
    count = spread * experts * CAP // 2
    lots = CAP // 2
    full = 2 * ROWS
    slots = Slots(sems)
    fetch = pltpu.make_async_copy(attn_hbm.at[section], attn, wsem.at[2])
    fetch.start()
    fetch_inner = pltpu.make_async_copy(inner_hbm.at[section], inner, wsem.at[0])
    fetch_inner.start()
    fetch_outer = pltpu.make_async_copy(outer_hbm.at[section], outer, wsem.at[1])
    fetch_outer.start()
    place.greet()

    z = z_ref[...].astype(F32)
    unit1, _ = norm_stats(z)
    fetch.wait()
    block = attn[:, 4 * wide:]
    vectors = block.astype(F32).T
    a1_full[side] = (unit1 * vectors[0:1] + vectors[1:2]).astype(BF)
    copy_a1 = slots.send(a1_full.at[side], a1_full.at[side], place.twin)
    copy_a1.wait_recv()
    a1 = a1_full[...].reshape(full, features)
    a1_ref[...] = a1
    for j in range(3):
        qkv_ref[j] = nn(a1, attn[:, j * wide:(j + 1) * wide]).astype(BF)
    key = iota((1, full), 1)
    key_row = lax.rem(key, ROWS)
    piece = (LIVE + 3) // 2
    key_live = (key_row < piece) & ((key // ROWS) * piece + key_row < LIVE)
    low_lane = iota((1, 128), 1) < HEAD_DIM
    for pair in range(wide // 128):
        lanes = slice(pair * 128, (pair + 1) * 128)
        q, k, v = qkv_ref[0, :, lanes], qkv_ref[1, :, lanes], qkv_ref[2, :, lanes]
        results = []
        for which in range(2):
            mask = low_lane if which == 0 else ~low_lane
            scores = nt(jnp.where(mask, q, jnp.zeros_like(q)), k) * HEAD_DIM**-0.5
            scores = jnp.where(key_live, scores, -1e30)
            weights = jnp.exp(scores - jnp.max(scores, axis=-1, keepdims=True))
            probs = weights / jnp.sum(weights, axis=-1, keepdims=True)
            probs_ref[2 * pair + which] = probs
            results.append(nn(probs.astype(BF), v))
        att_ref[:, lanes] = jnp.where(low_lane, results[0], results[1]).astype(BF)
    part[...] = nt(att_ref[...], attn[:, 3 * wide:4 * wide]).reshape(2, ROWS, features)
    copy_part = slots.send(part.at[1 - side], came, place.twin)
    copy_part.wait_recv()
    h1 = z + part[side] + came[...]
    h1_ref[...] = h1
    unit2, _ = norm_stats(h1)
    a2_full[side] = (unit2 * vectors[2:3] + vectors[3:4]).astype(BF)
    copy_a2 = slots.send(a2_full.at[side], a2_full.at[side], place.twin)
    copy_a2.wait_recv()
    a2 = a2_full[...].reshape(full, features)
    a2_ref[...] = a2

    slot = iota((experts * lots, full), 0) + side * (experts * lots)
    hit = (trow_ref[0:1, :] == slot) | (trow_ref[1:2, :] == slot)
    disp[...] = nn(hit.astype(F32).astype(BF), a2).astype(BF).reshape(experts, lots, features)
    finish = gather_rows(place, disp, rows, slots)

    lane = iota((1, 128), 1)
    valid = (lane >= 4) & (lane < 4 + experts)
    logits = jnp.where(valid, nn(a2, block), -1e30)
    odds = jnp.where(valid, jnp.exp(logits - jnp.max(logits, axis=-1, keepdims=True)), 0.0)
    rp_ref[...] = odds / jnp.sum(odds, axis=-1, keepdims=True)

    finish()
    rows_ref[...] = rows[...].reshape(count, features)
    acc[...] = jnp.zeros_like(acc)
    fetch_inner.wait()
    fetch_outer.wait()

    def tile_step(step, carry):
        half = step // tiles
        cols = pl.ds(pl.multiple_of(lax.rem(step, tiles) * tile, math.gcd(tile, 128)), tile)
        pre = nn(rows_ref[...], inner[half, :, cols])
        pre_ref[half, :, cols] = pre
        act = (0.5 * pre * (1.0 + gelu_tanh(pre))).astype(BF)
        acc[...] += nt(act, outer[half, :, cols])
        return carry

    lax.fori_loop(0, 2 * tiles, tile_step, 0)
    for copy in return_rows(place, acc, outb, parts, ret, slots):
        copy.wait_recv()
    copy_ret = slots.send(ret.at[side], ret.at[side], place.twin)
    copy_ret.wait_recv()
    home = ret[...].reshape(2 * experts * lots, features)
    own_rows = pl.ds(pl.multiple_of(side * ROWS, ROWS), ROWS)
    table = tcol_ref[own_rows, :]
    odds = rp_ref[own_rows, :]
    column = iota((ROWS, 2 * experts * lots), 1)
    y = h1
    for choice in range(2):
        pick = (table[:, choice:choice + 1] == column).astype(F32).astype(BF)
        chosen = nn(pick, home)
        chosen_ref[choice] = chosen.astype(BF)
        hot = table[:, 2 + choice:3 + choice] + 4 == lane
        y = y + chosen * jnp.sum(jnp.where(hot, odds, 0.0), axis=-1, keepdims=True)
    y_ref[...] = y.astype(BF)
    slots.drain()


def bwd_kernel(cfg, *refs):
    section, experts, spread, wide = cfg
    (dy_ref, z_ref, h1_ref, a1_ref, qkv_ref, probs_ref, att_ref, a2_ref, rp_ref, rows_ref,
     pre_ref, chosen_ref, trow_ref, tcol_ref, attn_hbm, inner_hbm, outer_hbm) = refs[:17]
    (dz_ref, gin_ref, gout_ref, gattn_ref,
     attn, inner, outer, dy_full, disp, dexp, acc, outb, parts, ret, act_all, dpre_all, lhs_t,
     dbr_full, dqkv, part, came, wsem, sems) = refs[17:]
    place = Place(experts, spread)
    side = place.side
    features = z_ref.shape[1]
    narrow = inner.shape[2]
    tile = TILE if narrow % TILE == 0 else narrow
    tiles = narrow // tile
    count = spread * experts * CAP // 2
    lots = CAP // 2
    full = 2 * ROWS
    slots = Slots(sems)
    fetch = pltpu.make_async_copy(attn_hbm.at[section], attn, wsem.at[2])
    fetch.start()
    fetch_inner = pltpu.make_async_copy(inner_hbm.at[section], inner, wsem.at[0])
    fetch_inner.start()
    fetch_outer = pltpu.make_async_copy(outer_hbm.at[section], outer, wsem.at[1])
    fetch_outer.start()
    place.greet()

    dy_full[side] = dy_ref[...]
    copy_dy = slots.send(dy_full.at[side], dy_full.at[side], place.twin)
    copy_dy.wait_recv()
    lane = iota((1, 128), 1)
    grad = dy_full[...].reshape(full, features).astype(F32)
    slot = iota((experts * lots, full), 0) + side * (experts * lots)
    total = jnp.zeros((experts * lots, features), F32)
    for choice in range(2):
        hot = tcol_ref[:, 2 + choice:3 + choice] + 4 == lane
        gate = jnp.sum(jnp.where(hot, rp_ref[...], 0.0), axis=-1, keepdims=True)
        hit = (trow_ref[choice:choice + 1, :] == slot).astype(F32).astype(BF)
        total = total + nn(hit, (gate * grad).astype(BF))
    disp[...] = total.astype(BF).reshape(experts, lots, features)
    finish = gather_rows(place, disp, dexp, slots)

    fetch.wait()
    block = attn[:, 4 * wide:]
    vectors = block.astype(F32).T
    own_rows = pl.ds(pl.multiple_of(side * ROWS, ROWS), ROWS)
    table = tcol_ref[own_rows, :]
    odds = rp_ref[own_rows, :]
    dy = dy_ref[...].astype(F32)
    drouter = jnp.zeros((ROWS, 128), F32)
    for choice in range(2):
        dgate = jnp.sum(dy * chosen_ref[choice].astype(F32), axis=-1, keepdims=True)
        dgate = jnp.where(table[:, choice:choice + 1] >= 0, dgate, 0.0)
        hot = table[:, 2 + choice:3 + choice] + 4 == lane
        drouter = drouter + jnp.where(hot, dgate, 0.0)
    dlogit = odds * (drouter - jnp.sum(odds * drouter, axis=-1, keepdims=True))
    high = dlogit.astype(BF)
    rest = (dlogit - high.astype(F32)).astype(BF)
    da2 = nt(high, block) + nt(rest, block)
    a2 = a2_ref[own_rows, :]
    grad_router = tn(a2, high) + tn(a2, rest)

    finish()
    acc[...] = jnp.zeros_like(acc)
    fetch_inner.wait()
    fetch_outer.wait()

    def tile_at(step):
        return step // tiles, pl.ds(
            pl.multiple_of(lax.rem(step, tiles) * tile, math.gcd(tile, 128)), tile
        )

    def tile_step(step, carry):
        half, cols = tile_at(step)
        grad_act = nn(dexp[...].reshape(count, features), outer[half, :, cols])
        pre = pre_ref[half, :, cols]
        tanh = gelu_tanh(pre)
        act_all[half, :, cols] = (0.5 * pre * (1.0 + tanh)).astype(BF)
        slope = 0.5 * (1.0 + tanh) + 0.5 * pre * (1.0 - tanh * tanh) * (
            0.7978845608028654 * (1.0 + 3 * 0.044715 * pre * pre)
        )
        dpre = (grad_act * slope).astype(BF)
        dpre_all[half, :, cols] = dpre
        acc[...] += nt(dpre, inner[half, :, cols])
        return carry

    lax.fori_loop(0, 2 * tiles, tile_step, 0)
    sent = return_rows(place, acc, outb, parts, ret, slots)
    lhs_t[0] = dexp[...].reshape(count, features).T
    lhs_t[1] = rows_ref[...].T

    def grad_step(step, carry):
        half, cols = tile_at(step)
        gout_ref[half, :, cols] = nn(lhs_t[0], act_all[half, :, cols]).astype(BF)
        gin_ref[half, :, cols] = nn(lhs_t[1], dpre_all[half, :, cols]).astype(BF)
        return carry

    lax.fori_loop(0, 2 * tiles, grad_step, 0)
    for copy in sent:
        copy.wait_recv()
    copy_ret = slots.send(ret.at[side], ret.at[side], place.twin)
    copy_ret.wait_recv()
    home = ret[...].reshape(2 * experts * lots, features)
    column = iota((ROWS, 2 * experts * lots), 1)
    pick = (table[:, 0:1] == column) | (table[:, 1:2] == column)
    da2 = da2 + nn(pick.astype(F32).astype(BF), home)
    unit2, inv2 = norm_stats(h1_ref[...])
    grad_gain2 = jnp.sum(da2 * unit2, axis=0, keepdims=True)
    grad_bias2 = jnp.sum(da2, axis=0, keepdims=True)
    dh1 = dy + norm_back(da2, unit2, inv2, vectors[2:3])
    dbr_full[side] = dh1.astype(BF)
    copy_dbr = slots.send(dbr_full.at[side], dbr_full.at[side], place.twin)
    copy_dbr.wait_recv()
    dbr = dbr_full[...].reshape(full, features)
    gattn_ref[:, 3 * wide:4 * wide] = tn(dbr, att_ref[...]).astype(BF)
    datt = nn(dbr, attn[:, 3 * wide:4 * wide]).astype(BF)
    low_lane = lane < HEAD_DIM
    for pair in range(wide // 128):
        lanes = slice(pair * 128, (pair + 1) * 128)
        q, k, v = qkv_ref[0, :, lanes], qkv_ref[1, :, lanes], qkv_ref[2, :, lanes]
        wide_datt = datt[:, lanes]
        dq = dk = dv = 0.0
        for which in range(2):
            mask = low_lane if which == 0 else ~low_lane
            zero = jnp.zeros_like(q)
            probs = probs_ref[2 * pair + which]
            head = jnp.where(mask, wide_datt, zero)
            dv = dv + tn(probs.astype(BF), head)
            dprobs = nt(head, v)
            dscores = probs * (dprobs - jnp.sum(probs * dprobs, axis=-1, keepdims=True))
            dscores = dscores.astype(BF)
            dq = dq + nn(dscores, jnp.where(mask, k, zero))
            dk = dk + tn(dscores, jnp.where(mask, q, zero))
        dqkv[0, :, lanes] = (dq * HEAD_DIM**-0.5).astype(BF)
        dqkv[1, :, lanes] = (dk * HEAD_DIM**-0.5).astype(BF)
        dqkv[2, :, lanes] = dv.astype(BF)
    da1 = jnp.zeros((full, features), F32)
    for j in range(3):
        da1 = da1 + nt(dqkv[j], attn[:, j * wide:(j + 1) * wide])
    part[...] = da1.reshape(2, ROWS, features)
    copy_part = slots.send(part.at[1 - side], came, place.twin)
    for j in range(3):
        gattn_ref[:, j * wide:(j + 1) * wide] = tn(a1_ref[...], dqkv[j]).astype(BF)
    unit1, inv1 = norm_stats(z_ref[...].astype(F32))
    copy_part.wait_recv()
    da1 = part[side] + came[...]
    grad_gain1 = jnp.sum(da1 * unit1, axis=0, keepdims=True)
    grad_bias1 = jnp.sum(da1, axis=0, keepdims=True)
    dz_ref[...] = dh1 + norm_back(da1, unit1, inv1, vectors[0:1])
    small = jnp.concatenate(
        [grad_gain1, grad_bias1, grad_gain2, grad_bias2, jnp.zeros((124, features), F32)], axis=0
    )
    gattn_ref[:, 4 * wide:] = (small.T + grad_router).astype(BF)
    slots.drain()


def forward(section, dims, z, trow, tcol, weights):
    experts, spread, features, wide, ff = dims
    full, slots = 2 * ROWS, CAP // 2
    narrow = ff // 2 // spread
    count = spread * experts * slots
    sends = 4 + 2 * (experts - 1) + 2 * experts * (spread - 1)
    heads = wide // HEAD_DIM
    vmem = pl.BlockSpec(memory_space=pltpu.VMEM)
    hbm = pl.BlockSpec(memory_space=pltpu.HBM)
    kernel = functools.partial(fwd_kernel, (section, experts, spread, wide))
    shape = jax.ShapeDtypeStruct
    return pl.pallas_call(
        kernel,
        out_shape=(
            shape((ROWS, features), BF),
            shape((ROWS, features), F32),
            shape((full, features), BF),
            shape((3, full, wide), BF),
            shape((heads, full, full), F32),
            shape((full, wide), BF),
            shape((full, features), BF),
            shape((full, 128), F32),
            shape((count, features), BF),
            shape((2, count, narrow), F32),
            shape((2, ROWS, features), BF),
        ),
        in_specs=[vmem] * 3 + [hbm] * 3,
        out_specs=(vmem,) * 11,
        scratch_shapes=[
            pltpu.VMEM((features, 4 * wide + 128), BF),
            pltpu.VMEM((2, features, narrow), BF),
            pltpu.VMEM((2, features, narrow), BF),
            pltpu.VMEM((2, ROWS, features), BF),
            pltpu.VMEM((2, ROWS, features), F32),
            pltpu.VMEM((ROWS, features), F32),
            pltpu.VMEM((2, ROWS, features), BF),
            pltpu.VMEM((experts, slots, features), BF),
            pltpu.VMEM((spread, experts, slots, features), BF),
            pltpu.VMEM((count, features), F32),
            pltpu.VMEM((spread, experts, slots, features), BF),
            pltpu.VMEM((max(1, spread - 1), experts, slots, features), BF),
            pltpu.VMEM((2, experts, slots, features), BF),
            pltpu.SemaphoreType.DMA((3,)),
            pltpu.SemaphoreType.DMA((2, sends)),
        ],
        compiler_params=pltpu.CompilerParams(
            collective_id=section, has_side_effects=True, vmem_limit_bytes=56 * 2**20
        ),
        name=f"section_forward_{section}",
    )(z, trow, tcol, *weights)


def backward(section, dims, dy, z, saved, trow, tcol, weights):
    experts, spread, features, wide, ff = dims
    full, slots = 2 * ROWS, CAP // 2
    narrow = ff // 2 // spread
    count = spread * experts * slots
    sends = 4 + 2 * (experts - 1) + 2 * experts * (spread - 1)
    vmem = pl.BlockSpec(memory_space=pltpu.VMEM)
    hbm = pl.BlockSpec(memory_space=pltpu.HBM)
    kernel = functools.partial(bwd_kernel, (section, experts, spread, wide))
    shape = jax.ShapeDtypeStruct
    return pl.pallas_call(
        kernel,
        out_shape=(
            shape((ROWS, features), F32),
            shape((2, features, narrow), BF),
            shape((2, features, narrow), BF),
            shape((features, 4 * wide + 128), BF),
        ),
        in_specs=[vmem] * 14 + [hbm] * 3,
        out_specs=(vmem,) * 4,
        scratch_shapes=[
            pltpu.VMEM((features, 4 * wide + 128), BF),
            pltpu.VMEM((2, features, narrow), BF),
            pltpu.VMEM((2, features, narrow), BF),
            pltpu.VMEM((2, ROWS, features), BF),
            pltpu.VMEM((experts, slots, features), BF),
            pltpu.VMEM((spread, experts, slots, features), BF),
            pltpu.VMEM((count, features), F32),
            pltpu.VMEM((spread, experts, slots, features), BF),
            pltpu.VMEM((max(1, spread - 1), experts, slots, features), BF),
            pltpu.VMEM((2, experts, slots, features), BF),
            pltpu.VMEM((2, count, narrow), BF),
            pltpu.VMEM((2, count, narrow), BF),
            pltpu.VMEM((2, features, count), BF),
            pltpu.VMEM((2, ROWS, features), BF),
            pltpu.VMEM((3, full, wide), BF),
            pltpu.VMEM((2, ROWS, features), F32),
            pltpu.VMEM((ROWS, features), F32),
            pltpu.SemaphoreType.DMA((3,)),
            pltpu.SemaphoreType.DMA((2, sends)),
        ],
        compiler_params=pltpu.CompilerParams(
            collective_id=2 + section, has_side_effects=True, vmem_limit_bytes=56 * 2**20
        ),
        name=f"section_backward_{section}",
    )(dy, z, *saved, trow, tcol, *weights)


def swap_planes(values):
    return lax.ppermute(values, "pipe", [(0, 1), (1, 0)])


def swap_sides(values):
    return lax.ppermute(values, "tensor", [(0, 1), (1, 0)])


def pick(values, index, axis=0):
    return lax.dynamic_index_in_dim(values, index, axis, keepdims=False)


def spread_weights(dims, attn, inner, outer):
    experts, spread, features, _, ff = dims
    narrow = ff // 2 // spread
    shape = jax.ShapeDtypeStruct
    hbm = pl.BlockSpec(memory_space=pltpu.HBM)
    sends = 3 * (experts - 1) + 3 * experts * (2 * spread - 1) + 2 * 2 * experts * spread
    return pl.pallas_call(
        functools.partial(spread_kernel, (experts, spread)),
        out_shape=(
            shape((2, features, attn.shape[1]), BF),
            shape((2, 2, features, narrow), BF),
            shape((2, 2, features, narrow), BF),
            shape((2, experts, spread, features // (experts * spread), narrow), BF),
        ),
        in_specs=[hbm] * 3,
        out_specs=(hbm,) * 4,
        scratch_shapes=[
            pltpu.SemaphoreType.DMA((1 + 2 * experts,)),
            pltpu.SemaphoreType.DMA((2, sends)),
        ],
        compiler_params=pltpu.CompilerParams(
            collective_id=4, has_side_effects=True, vmem_limit_bytes=56 * 2**20
        ),
        name="spread_weights",
    )(attn, inner, outer)[:3]


def reduce_grads(dims, inner, outer, attn):
    experts, spread, features, _, ff = dims
    narrow = ff // 2 // spread
    shard = features // (experts * spread)
    broad = attn[0].shape[1]
    shape = jax.ShapeDtypeStruct
    hbm = pl.BlockSpec(memory_space=pltpu.HBM)
    vmem = pl.BlockSpec(memory_space=pltpu.VMEM)
    blocks = 4 * experts * spread
    sends = blocks + experts * (2 * (spread - 1) + 1 + 2 * spread + 2 * (spread - 1))
    sends += 3 * (experts - 1)
    return pl.pallas_call(
        functools.partial(reduce_kernel, (experts, spread)),
        out_shape=(
            shape((experts, shard, ff // 2), BF),
            shape((experts, shard, ff // 2), BF),
            shape((shard, broad), F32),
        ),
        in_specs=[hbm] * 6,
        out_specs=(vmem,) * 3,
        scratch_shapes=[
            pltpu.VMEM((2, 2, experts, spread, shard, narrow), BF),
            pltpu.VMEM((2, 2, experts, spread, shard, narrow), BF),
            pltpu.VMEM((2, experts, spread, shard, narrow), BF),
            pltpu.VMEM((2, experts, spread, shard, narrow), BF),
            pltpu.VMEM((2, experts, spread, shard, narrow), BF),
            pltpu.VMEM((2, experts, spread * shard, broad), BF),
            pltpu.VMEM((2, experts, max(1, spread - 1), shard, broad), BF),
            pltpu.VMEM((experts, shard, broad), BF),
            pltpu.VMEM((experts, shard, broad), BF),
            pltpu.SemaphoreType.DMA((blocks + 2 * experts,)),
            pltpu.SemaphoreType.DMA((2, sends)),
        ],
        compiler_params=pltpu.CompilerParams(
            collective_id=5, has_side_effects=True, vmem_limit_bytes=56 * 2**20
        ),
        name="reduce_grads",
    )(*inner, *outer, *attn)


def body(
    images_in,
    out_grad,
    attn_gain,
    attn_bias,
    qkv_weight,
    proj_weight,
    moe_gain,
    moe_bias,
    router_weight,
    inner_weight,
    outer_weight,
    expert_ids,
    slot_ids,
):
    plane = lax.axis_index("pipe")
    micro, local, piece, features = images_in.shape
    shard, wide = qkv_weight.shape[2], qkv_weight.shape[3]
    experts = router_weight.shape[2]
    half = inner_weight.shape[3]
    spread = lax.axis_size("dp") // experts
    dims = (experts, spread, features, wide, 2 * half)
    packed = jnp.concatenate(
        [qkv_weight[0, 0], qkv_weight[0, 1], qkv_weight[0, 2], proj_weight[0].T,
         jnp.concatenate(
             [attn_gain, attn_bias, moe_gain, moe_bias, router_weight[0].T,
              jnp.zeros((128 - 4 - experts, shard), BF)], axis=0,
         ).T],
        axis=1,
    )

    def columns(values):
        return values.reshape(experts, shard, spread, half // spread).transpose(0, 2, 1, 3)

    weights = spread_weights(
        dims, packed, columns(inner_weight[0]), columns(outer_weight[0].transpose(0, 2, 1))
    )

    def my_image(values):
        return jnp.pad(pick(values, plane)[0], ((0, ROWS - piece), (0, 0)))

    routes = expert_ids[0, :, 0]
    slots = slot_ids[0, :, 0]
    kept = slots < CAP
    codes = jnp.where(
        kept, slots // (CAP // 2) * (experts * CAP // 2) + routes * (CAP // 2) + slots % (CAP // 2),
        -1,
    )
    table = jnp.concatenate([codes, routes], axis=-1)
    table_own = pick(table, plane)
    table_other = swap_planes(pick(table, 1 - plane))
    tables = []
    for section in range(2):
        values = jnp.where(plane == section, table_own, table_other).reshape(2, piece, 4)
        values = jnp.pad(values, ((0, 0), (0, ROWS - piece), (0, 0)), constant_values=-1)
        values = values.reshape(2 * ROWS, 4)
        tables.append((
            jnp.pad(values.T, ((0, 4), (0, 0)), constant_values=-1),
            jnp.pad(values, ((0, 0), (0, 124)), constant_values=-1),
        ))

    z0 = my_image(images_in)
    y0, *saved0 = forward(0, dims, z0, *tables[0], weights)
    y1, *saved1 = forward(1, dims, y0, *tables[1], weights)
    dz1, *grads1 = backward(1, dims, my_image(out_grad), y0, saved1, *tables[1], weights)
    dz0, *grads0 = backward(0, dims, dz1.astype(BF), z0, saved0, *tables[0], weights)

    inner_out, outer_out, packed_out = reduce_grads(
        dims, (grads0[0], grads1[0]), (grads0[1], grads1[1]), (grads0[2], grads1[2])
    )
    inner_out, outer_out = inner_out.astype(F32), outer_out.astype(F32)
    own_small = packed_out[:, 4 * wide:4 * wide + 4 + experts]
    own_small = own_small + swap_sides(own_small)

    def shape_out(first, second):
        first, second = first[:piece], second[:piece]
        keep = jnp.where(plane == 0, first, second)
        came = swap_planes(jnp.where(plane == 0, second, first))
        both = jnp.stack([jnp.where(plane == 0, keep, came), jnp.where(plane == 0, came, keep)])
        return both.reshape(1, micro, local, piece, features)

    return (
        shape_out(y0, y1),
        shape_out(dz0, dz1),
        own_small[:, 0][None],
        own_small[:, 1][None],
        jnp.stack([packed_out[:, j * wide:(j + 1) * wide] for j in range(3)])[None],
        packed_out[:, 3 * wide:4 * wide].T[None],
        own_small[:, 2][None],
        own_small[:, 3][None],
        own_small[:, 4:][None],
        inner_out[None],
        outer_out.transpose(0, 2, 1)[None],
    )


def solution(mesh):
    in_specs = (
        P(None, "dp", "tensor", None),
        P(None, "dp", "tensor", None),
        P("pipe", "dp"),
        P("pipe", "dp"),
        P("pipe", None, "dp", "tensor"),
        P("pipe", "tensor", "dp"),
        P("pipe", "dp"),
        P("pipe", "dp"),
        P("pipe", "dp", None),
        P("pipe", None, "dp", "tensor"),
        P("pipe", None, "tensor", "dp"),
        P("pipe", None, "dp", None, None),
        P("pipe", None, "dp", None, None),
    )
    out_specs = (
        P("pipe", None, "dp", "tensor", None),
        P("pipe", None, "dp", "tensor", None),
        P("pipe", "dp"),
        P("pipe", "dp"),
        P("pipe", None, "dp", "tensor"),
        P("pipe", "tensor", "dp"),
        P("pipe", "dp"),
        P("pipe", "dp"),
        P("pipe", "dp", None),
        P("pipe", None, "dp", "tensor"),
        P("pipe", None, "tensor", "dp"),
    )
    return jax.shard_map(body, mesh=mesh, in_specs=in_specs, out_specs=out_specs, check_vma=False)
```

```python
import functools
import math

import jax
import jax.numpy as jnp
from jax import lax
from jax.experimental import pallas as pl
from jax.experimental.pallas import tpu as pltpu
from jax.sharding import PartitionSpec as P

HEAD_DIM = 64
LIVE = 197
CAP = 128
ROWS = 128
EPS = 1e-06
TILE = 384
LAG = 1
BF = jnp.bfloat16
F32 = jnp.float32
MESH = pl.DeviceIdType.MESH


def nn(left, right):
    return lax.dot_general(left, right, (((1,), (0,)), ((), ())), preferred_element_type=F32)


def nt(left, right):
    return lax.dot_general(left, right, (((1,), (1,)), ((), ())), preferred_element_type=F32)


def tn(left, right):
    return lax.dot_general(left, right, (((0,), (0,)), ((), ())), preferred_element_type=F32)


def norm_stats(values):
    centre = values - jnp.mean(values, axis=-1, keepdims=True)
    inv = lax.rsqrt(jnp.mean(centre * centre, axis=-1, keepdims=True) + EPS)
    return centre * inv, inv


def norm_back(grad, unit, inv, gain):
    scaled = grad * gain
    return (
        scaled
        - jnp.mean(scaled, axis=-1, keepdims=True)
        - unit * jnp.mean(scaled * unit, axis=-1, keepdims=True)
    ) * inv


def iota(shape, dim):
    return lax.broadcasted_iota(jnp.int32, shape, dim)


class Place:
    def __init__(self, experts, spread):
        self.experts, self.spread = experts, spread
        self.plane = lax.axis_index("pipe")
        self.side = lax.axis_index("tensor")
        dp = lax.axis_index("dp")
        self.mine = dp // spread
        self.column = lax.rem(dp, spread)
        self.twin = {"tensor": 1 - self.side}
        self.across = {"pipe": 1 - self.plane}

    def ahead(self, steps):
        return lax.rem(self.mine + steps, self.experts)

    def behind(self, steps):
        return lax.rem(self.mine + self.experts - steps, self.experts)

    def peer(self, group):
        return {"dp": group * self.spread + self.column}

    def beside(self, shift):
        return {"dp": self.mine * self.spread + lax.rem(self.column + shift, self.spread)}

    def left(self, shift):
        return lax.rem(self.column + self.spread - shift, self.spread)

    def greet(self, everyone=False):
        barrier = pltpu.get_barrier_semaphore()
        devices = [self.twin]
        devices += [self.peer(self.ahead(steps)) for steps in range(1, self.experts)]
        devices += [self.beside(shift) for shift in range(1, self.spread)]
        if everyone:
            devices += [self.across]
        for device in devices:
            pl.semaphore_signal(barrier, inc=1, device_id=device, device_id_type=MESH)
        pl.semaphore_wait(barrier, len(devices))


def send(source, target, sems, slot, device):
    copy = pltpu.make_async_remote_copy(
        src_ref=source,
        dst_ref=target,
        send_sem=sems.at[0, slot],
        recv_sem=sems.at[1, slot],
        device_id=device,
        device_id_type=MESH,
    )
    copy.start()
    return copy


class Slots:
    def __init__(self, sems):
        self.sems, self.next, self.sends = sems, 0, []

    def send(self, source, target, device):
        copy = send(source, target, self.sems, self.next, device)
        self.next += 1
        self.sends.append(copy)
        return copy

    def drain(self):
        for copy in self.sends:
            copy.wait_send()


class Spread:
    def __init__(self, place, slots, local, shards, stage, whole):
        self.place, self.slots, self.local = place, slots, local
        self.shards, self.stage, self.whole = shards, stage, whole
        experts = place.experts
        far = list(range(1, experts, 2)) + list(range(2, experts, 2))
        self.away = [(kind, steps) for steps in far for kind in (1, 2, 0)]
        self.pieces = [(kind, 0) for kind in range(3)] + self.away
        self.over_groups, self.over_columns, self.over_planes, self.late = {}, {}, {}, {}
        self.twins, self.kept = [], []

    def where(self, kind, section, group, col):
        place = self.place
        shard = self.shards[0].shape[0]
        row = (group * place.spread + col) * shard
        rows = pl.ds(pl.multiple_of(row, math.gcd(shard, 16)), shard)
        if kind == 0:
            return self.whole[0].at[section, rows]
        return self.whole[kind].at[section, place.side, rows]

    def held(self, kind, steps):
        place = self.place
        if kind == 0:
            if steps == 0:
                return self.shards[0]
            return self.where(0, place.plane, place.behind(steps), place.column)
        if steps == 0:
            return self.shards[kind].at[place.mine]
        return self.stage.at[kind - 1, steps]

    def start_groups(self, count):
        place = self.place
        for kind, steps in self.away[len(self.over_groups):len(self.over_groups) + count]:
            group = place.ahead(steps)
            if kind == 0:
                source = self.shards[0]
                target = self.where(0, place.plane, place.mine, place.column)
            else:
                source, target = self.shards[kind].at[group], self.stage.at[kind - 1, steps]
            self.over_groups[kind, steps] = self.slots.send(source, target, place.peer(group))

    def to_twin(self, kind, source, target):
        if kind:
            self.twins.append(self.slots.send(source, target, self.place.twin))

    def first_hop(self, kind, steps):
        place, slots = self.place, self.slots
        if steps:
            self.over_groups[kind, steps].wait_recv()
            self.start_groups(1)
        held = self.held(kind, steps)
        target = self.where(kind, place.plane, place.behind(steps), place.column)
        own = held if kind == 0 else held.at[place.column]
        for shift in range(1, place.spread):
            col = lax.rem(place.column + shift, place.spread)
            part = held if kind == 0 else held.at[col]
            self.over_columns[kind, steps, shift] = slots.send(part, target, place.beside(shift))
        self.over_planes[kind, steps] = slots.send(own, target, place.across)
        self.to_twin(kind, own, target)
        if kind or steps == 0:
            copy = pltpu.make_async_copy(own, target, self.local.at[len(self.kept)])
            copy.start()
            self.kept.append(copy)

    def second_hop(self, kind, steps):
        place, slots = self.place, self.slots
        group = place.behind(steps)
        if kind == 0:
            self.over_planes[kind, steps].wait_recv()
            target = self.where(kind, 1 - place.plane, group, place.column)
            for shift in range(1, place.spread):
                self.late[kind, steps, shift] = slots.send(target, target, place.beside(shift))
            return
        for shift in range(1, place.spread):
            self.over_columns[kind, steps, shift].wait_recv()
            target = self.where(kind, place.plane, group, place.left(shift))
            self.late[kind, steps, shift] = slots.send(target, target, place.across)
            self.to_twin(kind, target, target)

    def last_hop(self, kind, steps):
        place = self.place
        group = place.behind(steps)
        if kind:
            self.over_planes[kind, steps].wait_recv()
            target = self.where(kind, 1 - place.plane, group, place.column)
            self.to_twin(kind, target, target)
        for shift in range(1, place.spread):
            if kind == 0:
                self.over_columns[kind, steps, shift].wait_recv()
            self.late[kind, steps, shift].wait_recv()
            target = self.where(kind, 1 - place.plane, group, place.left(shift))
            self.to_twin(kind, target, target)

    def hops(self, begin, end):
        pieces = self.pieces
        for at in range(begin, end):
            if at < len(pieces):
                self.first_hop(*pieces[at])
            if LAG <= at < len(pieces) + LAG:
                self.second_hop(*pieces[at - LAG])
            if at >= 2 * LAG:
                self.last_hop(*pieces[at - 2 * LAG])

    def finish(self):
        for copy in self.twins:
            copy.wait_recv()
        for copy in self.kept:
            copy.wait()


def spread_kernel(cfg, attn_own, inner_own, outer_own, attn_all, inner_all, outer_all, stage,
                  lsem, sems):
    place = Place(*cfg)
    slots = Slots(sems)
    place.greet(everyone=True)
    spread = Spread(place, slots, lsem, (attn_own, inner_own, outer_own), stage,
                    (attn_all, inner_all, outer_all))
    spread.start_groups(4)
    spread.hops(0, len(spread.pieces) + 2 * LAG)
    spread.finish()
    slots.drain()


def add_into(target, came):
    target[...] = (target[...].astype(F32) + came[...].astype(F32)).astype(BF)


def reduce_kernel(cfg, *refs):
    experts, spread = cfg
    grads, gattn = (refs[0:2], refs[2:4]), refs[4:6]
    (inner_out, outer_out, attn_out,
     acc, twin_in, planes_in, blocks, z_in, attn_acc, at_cols, at_planes, z_attn,
     lsem, sems) = refs[6:]
    place = Place(experts, spread)
    slots = Slots(sems)
    plane, side, column = place.plane, place.side, place.column
    shard = acc.shape[4]
    local_slot = iter(range(lsem.shape[0]))
    place.greet(everyone=True)
    order = list(range(2, experts, 2)) + list(range(1, experts, 2)) + [0]
    whole = range(2)
    aligned = math.gcd(shard, 16)

    halves, attn_local, hops = {}, {}, {}
    for steps in order:
        group = place.ahead(steps)
        for section in whole:
            copy = pltpu.make_async_copy(
                gattn[section].at[
                    pl.ds(pl.multiple_of(group * spread * shard, aligned), spread * shard)
                ],
                attn_acc.at[section, steps], lsem.at[next(local_slot)],
            )
            copy.start()
            attn_local[steps, section] = copy
            for matrix in whole:
                for col in range(spread):
                    rows = pl.ds(
                        pl.multiple_of((group * spread + col) * shard, aligned), shard
                    )
                    source = grads[matrix][section]
                    away = slots.send(
                        source.at[1 - side, rows], twin_in.at[section, matrix, steps, col],
                        place.twin,
                    )
                    own = pltpu.make_async_copy(
                        source.at[side, rows], acc.at[section, matrix, steps, col],
                        lsem.at[next(local_slot)],
                    )
                    own.start()
                    halves[steps, section, matrix, col] = (away, own)

    def attn_block(section, steps, col):
        return attn_acc.at[section, steps, pl.ds(pl.multiple_of(col * shard, aligned), shard)]

    def first(kind, steps):
        if kind == 2:
            for section in whole:
                attn_local[steps, section].wait()
                for shift in range(1, spread):
                    hops["ax", steps, section, shift] = slots.send(
                        attn_block(section, steps, lax.rem(column + shift, spread)),
                        at_cols.at[section, steps, shift - 1], place.beside(shift),
                    )
            return
        for col in range(spread):
            for section in whole:
                away, own = halves[steps, section, kind, col]
                own.wait()
                away.wait_recv()
                add_into(acc.at[section, kind, steps, col], twin_in.at[section, kind, steps, col])
            hops["y", kind, steps, col] = slots.send(
                acc.at[1 - plane, kind, steps, col], planes_in.at[kind, steps, col], place.across
            )

    def second(kind, steps):
        if kind == 2:
            for section in whole:
                for shift in range(1, spread):
                    hops["ax", steps, section, shift].wait_recv()
                    add_into(attn_block(section, steps, column),
                             at_cols.at[section, steps, shift - 1])
            hops["ay", steps] = slots.send(
                attn_block(1 - plane, steps, column), at_planes.at[steps], place.across
            )
            return
        for col in range(spread):
            hops["y", kind, steps, col].wait_recv()
            add_into(acc.at[plane, kind, steps, col], planes_in.at[kind, steps, col])
        for shift in range(1, spread):
            hops["x", kind, steps, shift] = slots.send(
                acc.at[plane, kind, steps, lax.rem(column + shift, spread)],
                blocks.at[kind, steps, column], place.beside(shift),
            )
        blocks[kind, steps, column] = acc[plane, kind, steps, column]

    def third(kind, steps):
        device = place.peer(place.ahead(steps))
        if kind == 2:
            hops["ay", steps].wait_recv()
            add_into(attn_block(plane, steps, column), at_planes.at[steps])
            if steps:
                hops["az", steps] = slots.send(
                    attn_block(plane, steps, column), z_attn.at[steps], device
                )
            return
        for shift in range(1, spread):
            hops["x", kind, steps, shift].wait_recv()
        if steps:
            hops["z", kind, steps] = slots.send(
                blocks.at[kind, steps], z_in.at[kind, steps], device
            )

    pieces = [(kind, steps) for steps in order for kind in (1, 0, 2)]
    for at in range(len(pieces) + 2 * LAG):
        if at < len(pieces):
            first(*pieces[at])
        if LAG <= at < len(pieces) + LAG:
            second(*pieces[at - LAG])
        if at >= 2 * LAG:
            third(*pieces[at - 2 * LAG])
    outs = (inner_out, outer_out)
    narrow = acc.shape[5]

    def put(kind, group, source):
        for col in range(spread):
            outs[kind][group, :, col * narrow:(col + 1) * narrow] = source[col]

    for kind in whole:
        put(kind, place.mine, blocks.at[kind, 0])
    total = attn_block(plane, 0, column)[...].astype(F32)
    for steps in order[:-1]:
        hops["az", steps].wait_recv()
        total = total + z_attn[steps].astype(F32)
        for kind in whole:
            hops["z", kind, steps].wait_recv()
            put(kind, place.behind(steps), z_in.at[kind, steps])
    attn_out[...] = total
    slots.drain()


class Rows:
    def __init__(self, place, slots, out, rows, acc, outb, parts, ret):
        self.place, self.slots, self.rows, self.acc = place, slots, rows, acc
        self.out, self.outb, self.parts, self.ret = out, outb, parts, ret
        self.order = [0] + list(range(2, place.experts, 2)) + list(range(1, place.experts, 2))
        self.over_groups, self.over_columns, self.partial, self.home = {}, {}, {}, []

    def start(self):
        place = self.place
        for steps in self.order[1:]:
            group = place.ahead(steps)
            self.over_groups[steps] = self.slots.send(
                self.out.at[group], self.rows.at[steps, place.column], place.peer(group)
            )
        self.pass_on(0)
        self.rows[0, place.column] = self.out[place.mine]

    def pass_on(self, steps):
        place = self.place
        target = self.rows.at[steps, place.column]
        source = target
        if steps:
            self.over_groups[steps].wait_recv()
        else:
            source = self.out.at[place.mine]
        for shift in range(1, place.spread):
            self.over_columns[steps, shift] = self.slots.send(source, target, place.beside(shift))

    def give_back(self, steps):
        place = self.place
        for shift in range(1, place.spread):
            col = lax.rem(place.column + shift, place.spread)
            self.outb[steps, col] = self.acc[steps, col].astype(BF)
            self.partial[steps, shift] = self.slots.send(
                self.outb.at[steps, col], self.parts.at[steps, shift - 1], place.beside(shift)
            )

    def send_home(self, steps):
        place = self.place
        total = self.acc[steps, place.column]
        for shift in range(1, place.spread):
            self.partial[steps, shift].wait_recv()
            total = total + self.parts[steps, shift - 1].astype(F32)
        if steps == 0:
            self.ret[place.side, place.mine] = total.astype(BF)
            return
        self.outb[steps, place.column] = total.astype(BF)
        self.home.append(self.slots.send(
            self.outb.at[steps, place.column], self.ret.at[place.side, place.mine],
            place.peer(place.behind(steps)),
        ))

    def run(self, compute):
        order = self.order
        for at, steps in enumerate(order):
            if at + 1 < len(order):
                self.pass_on(order[at + 1])
            for shift in range(1, self.place.spread):
                self.over_columns[steps, shift].wait_recv()
            compute(steps)
            self.give_back(steps)
            if at:
                self.send_home(order[at - 1])
        self.send_home(order[-1])

    def finish(self):
        for copy in self.home:
            copy.wait_recv()


def gelu_tanh(pre):
    return jnp.tanh(0.7978845608028654 * (pre + 0.044715 * pre * pre * pre))


def fwd_kernel(cfg, *refs):
    section, experts, spread, wide = cfg
    z_ref, trow_ref, tcol_ref, attn_hbm, inner_hbm, outer_hbm = refs[:6]
    (y_ref, h1_ref, a1_ref, qkv_ref, probs_ref, att_ref, a2_ref, rp_ref, rows_ref, pre_ref,
     chosen_ref,
     attn, inner, outer, a1_full, part, came, a2_full, disp, rows, acc, outb, parts, ret,
     wsem, sems) = refs[6:]
    place = Place(experts, spread)
    side = place.side
    features = z_ref.shape[1]
    narrow = inner.shape[2]
    tile = TILE if narrow % TILE == 0 else narrow
    tiles = narrow // tile
    chunk = spread * CAP // 2
    count = experts * chunk
    lots = CAP // 2
    full = 2 * ROWS
    slots = Slots(sems)
    fetch = pltpu.make_async_copy(attn_hbm.at[section], attn, wsem.at[2])
    fetch.start()
    fetch_inner = pltpu.make_async_copy(inner_hbm.at[section], inner, wsem.at[0])
    fetch_inner.start()
    fetch_outer = pltpu.make_async_copy(outer_hbm.at[section], outer, wsem.at[1])
    fetch_outer.start()
    place.greet()

    z = z_ref[...].astype(F32)
    unit1, _ = norm_stats(z)
    fetch.wait()
    block = attn[:, 4 * wide:]
    vectors = block.astype(F32).T
    a1_full[side] = (unit1 * vectors[0:1] + vectors[1:2]).astype(BF)
    copy_a1 = slots.send(a1_full.at[side], a1_full.at[side], place.twin)
    copy_a1.wait_recv()
    a1 = a1_full[...].reshape(full, features)
    a1_ref[...] = a1
    for j in range(3):
        qkv_ref[j] = nn(a1, attn[:, j * wide:(j + 1) * wide]).astype(BF)
    key = iota((1, full), 1)
    key_row = lax.rem(key, ROWS)
    piece = (LIVE + 3) // 2
    key_live = (key_row < piece) & ((key // ROWS) * piece + key_row < LIVE)
    low_lane = iota((1, 128), 1) < HEAD_DIM
    for pair in range(wide // 128):
        lanes = slice(pair * 128, (pair + 1) * 128)
        q, k, v = qkv_ref[0, :, lanes], qkv_ref[1, :, lanes], qkv_ref[2, :, lanes]
        results = []
        for which in range(2):
            mask = low_lane if which == 0 else ~low_lane
            scores = nt(jnp.where(mask, q, jnp.zeros_like(q)), k) * HEAD_DIM**-0.5
            scores = jnp.where(key_live, scores, -1e30)
            weights = jnp.exp(scores - jnp.max(scores, axis=-1, keepdims=True))
            probs = weights / jnp.sum(weights, axis=-1, keepdims=True)
            probs_ref[2 * pair + which] = probs
            results.append(nn(probs.astype(BF), v))
        att_ref[:, lanes] = jnp.where(low_lane, results[0], results[1]).astype(BF)
    part[...] = nt(att_ref[...], attn[:, 3 * wide:4 * wide]).reshape(2, ROWS, features)
    copy_part = slots.send(part.at[1 - side], came, place.twin)
    copy_part.wait_recv()
    h1 = z + part[side] + came[...]
    h1_ref[...] = h1
    unit2, _ = norm_stats(h1)
    a2_full[side] = (unit2 * vectors[2:3] + vectors[3:4]).astype(BF)
    copy_a2 = slots.send(a2_full.at[side], a2_full.at[side], place.twin)
    copy_a2.wait_recv()
    a2 = a2_full[...].reshape(full, features)
    a2_ref[...] = a2

    slot = iota((experts * lots, full), 0) + side * (experts * lots)
    hit = (trow_ref[0:1, :] == slot) | (trow_ref[1:2, :] == slot)
    disp[...] = nn(hit.astype(F32).astype(BF), a2).astype(BF).reshape(experts, lots, features)
    moves = Rows(place, slots, disp, rows, acc, outb, parts, ret)
    moves.start()

    lane = iota((1, 128), 1)
    valid = (lane >= 4) & (lane < 4 + experts)
    logits = jnp.where(valid, nn(a2, block), -1e30)
    odds = jnp.where(valid, jnp.exp(logits - jnp.max(logits, axis=-1, keepdims=True)), 0.0)
    rp_ref[...] = odds / jnp.sum(odds, axis=-1, keepdims=True)

    fetch_inner.wait()
    fetch_outer.wait()

    def compute(steps):
        span = slice(steps * chunk, (steps + 1) * chunk)
        rows_ref[span, :] = rows[steps].reshape(chunk, features)
        acc[steps] = jnp.zeros_like(acc[steps])

        def tile_step(step, carry):
            half = step // tiles
            cols = pl.ds(pl.multiple_of(lax.rem(step, tiles) * tile, math.gcd(tile, 128)), tile)
            pre = nn(rows_ref[span, :], inner[half, :, cols])
            pre_ref[half, span, cols] = pre
            act = (0.5 * pre * (1.0 + gelu_tanh(pre))).astype(BF)
            acc[steps] += nt(act, outer[half, :, cols]).reshape(spread, lots, features)
            return carry

        lax.fori_loop(0, 2 * tiles, tile_step, 0)

    moves.run(compute)
    moves.finish()
    copy_ret = slots.send(ret.at[side], ret.at[side], place.twin)
    copy_ret.wait_recv()
    home = ret[...].reshape(2 * experts * lots, features)
    own_rows = pl.ds(pl.multiple_of(side * ROWS, ROWS), ROWS)
    table = tcol_ref[own_rows, :]
    odds = rp_ref[own_rows, :]
    column = iota((ROWS, 2 * experts * lots), 1)
    y = h1
    for choice in range(2):
        pick = (table[:, choice:choice + 1] == column).astype(F32).astype(BF)
        chosen = nn(pick, home)
        chosen_ref[choice] = chosen.astype(BF)
        hot = table[:, 2 + choice:3 + choice] + 4 == lane
        y = y + chosen * jnp.sum(jnp.where(hot, odds, 0.0), axis=-1, keepdims=True)
    y_ref[...] = y.astype(BF)
    slots.drain()


def bwd_kernel(cfg, *refs):
    section, experts, spread, wide = cfg
    (dy_ref, z_ref, h1_ref, a1_ref, qkv_ref, probs_ref, att_ref, a2_ref, rp_ref, rows_ref,
     pre_ref, chosen_ref, trow_ref, tcol_ref, attn_hbm, inner_hbm, outer_hbm) = refs[:17]
    (dz_ref, gin_ref, gout_ref, gattn_ref,
     attn, inner, outer, dy_full, disp, dexp, acc, outb, parts, ret, act_all, dpre_all, lhs_t,
     dbr_full, dqkv, part, came, wsem, sems) = refs[17:]
    place = Place(experts, spread)
    side = place.side
    features = z_ref.shape[1]
    narrow = inner.shape[2]
    tile = TILE if narrow % TILE == 0 else narrow
    tiles = narrow // tile
    chunk = spread * CAP // 2
    count = experts * chunk
    lots = CAP // 2
    full = 2 * ROWS
    slots = Slots(sems)
    fetch = pltpu.make_async_copy(attn_hbm.at[section], attn, wsem.at[2])
    fetch.start()
    fetch_inner = pltpu.make_async_copy(inner_hbm.at[section], inner, wsem.at[0])
    fetch_inner.start()
    fetch_outer = pltpu.make_async_copy(outer_hbm.at[section], outer, wsem.at[1])
    fetch_outer.start()
    place.greet()

    dy_full[side] = dy_ref[...]
    copy_dy = slots.send(dy_full.at[side], dy_full.at[side], place.twin)
    copy_dy.wait_recv()
    lane = iota((1, 128), 1)
    grad = dy_full[...].reshape(full, features).astype(F32)
    slot = iota((experts * lots, full), 0) + side * (experts * lots)
    total = jnp.zeros((experts * lots, features), F32)
    for choice in range(2):
        hot = tcol_ref[:, 2 + choice:3 + choice] + 4 == lane
        gate = jnp.sum(jnp.where(hot, rp_ref[...], 0.0), axis=-1, keepdims=True)
        hit = (trow_ref[choice:choice + 1, :] == slot).astype(F32).astype(BF)
        total = total + nn(hit, (gate * grad).astype(BF))
    disp[...] = total.astype(BF).reshape(experts, lots, features)
    moves = Rows(place, slots, disp, dexp, acc, outb, parts, ret)
    moves.start()

    fetch.wait()
    block = attn[:, 4 * wide:]
    vectors = block.astype(F32).T
    own_rows = pl.ds(pl.multiple_of(side * ROWS, ROWS), ROWS)
    table = tcol_ref[own_rows, :]
    odds = rp_ref[own_rows, :]
    dy = dy_ref[...].astype(F32)
    drouter = jnp.zeros((ROWS, 128), F32)
    for choice in range(2):
        dgate = jnp.sum(dy * chosen_ref[choice].astype(F32), axis=-1, keepdims=True)
        dgate = jnp.where(table[:, choice:choice + 1] >= 0, dgate, 0.0)
        hot = table[:, 2 + choice:3 + choice] + 4 == lane
        drouter = drouter + jnp.where(hot, dgate, 0.0)
    dlogit = odds * (drouter - jnp.sum(odds * drouter, axis=-1, keepdims=True))
    high = dlogit.astype(BF)
    rest = (dlogit - high.astype(F32)).astype(BF)
    da2 = nt(high, block) + nt(rest, block)
    a2 = a2_ref[own_rows, :]
    grad_router = tn(a2, high) + tn(a2, rest)

    fetch_inner.wait()
    fetch_outer.wait()

    def tile_at(step):
        return step // tiles, pl.ds(
            pl.multiple_of(lax.rem(step, tiles) * tile, math.gcd(tile, 128)), tile
        )

    def compute(steps):
        span = slice(steps * chunk, (steps + 1) * chunk)
        acc[steps] = jnp.zeros_like(acc[steps])

        def tile_step(step, carry):
            half, cols = tile_at(step)
            grad_act = nn(dexp[steps].reshape(chunk, features), outer[half, :, cols])
            pre = pre_ref[half, span, cols]
            tanh = gelu_tanh(pre)
            act_all[half, span, cols] = (0.5 * pre * (1.0 + tanh)).astype(BF)
            slope = 0.5 * (1.0 + tanh) + 0.5 * pre * (1.0 - tanh * tanh) * (
                0.7978845608028654 * (1.0 + 3 * 0.044715 * pre * pre)
            )
            dpre = (grad_act * slope).astype(BF)
            dpre_all[half, span, cols] = dpre
            acc[steps] += nt(dpre, inner[half, :, cols]).reshape(spread, lots, features)
            return carry

        lax.fori_loop(0, 2 * tiles, tile_step, 0)

    moves.run(compute)
    lhs_t[0] = dexp[...].reshape(count, features).T
    lhs_t[1] = rows_ref[...].T

    def grad_step(step, carry):
        half, cols = tile_at(step)
        gout_ref[half, :, cols] = nn(lhs_t[0], act_all[half, :, cols]).astype(BF)
        gin_ref[half, :, cols] = nn(lhs_t[1], dpre_all[half, :, cols]).astype(BF)
        return carry

    lax.fori_loop(0, 2 * tiles, grad_step, 0)
    moves.finish()
    copy_ret = slots.send(ret.at[side], ret.at[side], place.twin)
    copy_ret.wait_recv()
    home = ret[...].reshape(2 * experts * lots, features)
    column = iota((ROWS, 2 * experts * lots), 1)
    pick = (table[:, 0:1] == column) | (table[:, 1:2] == column)
    da2 = da2 + nn(pick.astype(F32).astype(BF), home)
    unit2, inv2 = norm_stats(h1_ref[...])
    grad_gain2 = jnp.sum(da2 * unit2, axis=0, keepdims=True)
    grad_bias2 = jnp.sum(da2, axis=0, keepdims=True)
    dh1 = dy + norm_back(da2, unit2, inv2, vectors[2:3])
    dbr_full[side] = dh1.astype(BF)
    copy_dbr = slots.send(dbr_full.at[side], dbr_full.at[side], place.twin)
    copy_dbr.wait_recv()
    dbr = dbr_full[...].reshape(full, features)
    gattn_ref[:, 3 * wide:4 * wide] = tn(dbr, att_ref[...]).astype(BF)
    datt = nn(dbr, attn[:, 3 * wide:4 * wide]).astype(BF)
    low_lane = lane < HEAD_DIM
    for pair in range(wide // 128):
        lanes = slice(pair * 128, (pair + 1) * 128)
        q, k, v = qkv_ref[0, :, lanes], qkv_ref[1, :, lanes], qkv_ref[2, :, lanes]
        wide_datt = datt[:, lanes]
        dq = dk = dv = 0.0
        for which in range(2):
            mask = low_lane if which == 0 else ~low_lane
            zero = jnp.zeros_like(q)
            probs = probs_ref[2 * pair + which]
            head = jnp.where(mask, wide_datt, zero)
            dv = dv + tn(probs.astype(BF), head)
            dprobs = nt(head, v)
            dscores = probs * (dprobs - jnp.sum(probs * dprobs, axis=-1, keepdims=True))
            dscores = dscores.astype(BF)
            dq = dq + nn(dscores, jnp.where(mask, k, zero))
            dk = dk + tn(dscores, jnp.where(mask, q, zero))
        dqkv[0, :, lanes] = (dq * HEAD_DIM**-0.5).astype(BF)
        dqkv[1, :, lanes] = (dk * HEAD_DIM**-0.5).astype(BF)
        dqkv[2, :, lanes] = dv.astype(BF)
    da1 = jnp.zeros((full, features), F32)
    for j in range(3):
        da1 = da1 + nt(dqkv[j], attn[:, j * wide:(j + 1) * wide])
    part[...] = da1.reshape(2, ROWS, features)
    copy_part = slots.send(part.at[1 - side], came, place.twin)
    for j in range(3):
        gattn_ref[:, j * wide:(j + 1) * wide] = tn(a1_ref[...], dqkv[j]).astype(BF)
    unit1, inv1 = norm_stats(z_ref[...].astype(F32))
    copy_part.wait_recv()
    da1 = part[side] + came[...]
    grad_gain1 = jnp.sum(da1 * unit1, axis=0, keepdims=True)
    grad_bias1 = jnp.sum(da1, axis=0, keepdims=True)
    dz_ref[...] = dh1 + norm_back(da1, unit1, inv1, vectors[0:1])
    small = jnp.concatenate(
        [grad_gain1, grad_bias1, grad_gain2, grad_bias2, jnp.zeros((124, features), F32)], axis=0
    )
    gattn_ref[:, 4 * wide:] = (small.T + grad_router).astype(BF)
    slots.drain()


def forward(section, dims, z, trow, tcol, weights):
    experts, spread, features, wide, ff = dims
    full, slots = 2 * ROWS, CAP // 2
    narrow = ff // 2 // spread
    count = spread * experts * slots
    sends = 4 + 2 * (experts - 1) + 2 * experts * (spread - 1)
    heads = wide // HEAD_DIM
    vmem = pl.BlockSpec(memory_space=pltpu.VMEM)
    hbm = pl.BlockSpec(memory_space=pltpu.HBM)
    kernel = functools.partial(fwd_kernel, (section, experts, spread, wide))
    shape = jax.ShapeDtypeStruct
    return pl.pallas_call(
        kernel,
        out_shape=(
            shape((ROWS, features), BF),
            shape((ROWS, features), F32),
            shape((full, features), BF),
            shape((3, full, wide), BF),
            shape((heads, full, full), F32),
            shape((full, wide), BF),
            shape((full, features), BF),
            shape((full, 128), F32),
            shape((count, features), BF),
            shape((2, count, narrow), F32),
            shape((2, ROWS, features), BF),
        ),
        in_specs=[vmem] * 3 + [hbm] * 3,
        out_specs=(vmem,) * 11,
        scratch_shapes=[
            pltpu.VMEM((features, 4 * wide + 128), BF),
            pltpu.VMEM((2, features, narrow), BF),
            pltpu.VMEM((2, features, narrow), BF),
            pltpu.VMEM((2, ROWS, features), BF),
            pltpu.VMEM((2, ROWS, features), F32),
            pltpu.VMEM((ROWS, features), F32),
            pltpu.VMEM((2, ROWS, features), BF),
            pltpu.VMEM((experts, slots, features), BF),
            pltpu.VMEM((experts, spread, slots, features), BF),
            pltpu.VMEM((experts, spread, slots, features), F32),
            pltpu.VMEM((experts, spread, slots, features), BF),
            pltpu.VMEM((experts, max(1, spread - 1), slots, features), BF),
            pltpu.VMEM((2, experts, slots, features), BF),
            pltpu.SemaphoreType.DMA((3,)),
            pltpu.SemaphoreType.DMA((2, sends)),
        ],
        compiler_params=pltpu.CompilerParams(
            collective_id=section, has_side_effects=True, vmem_limit_bytes=56 * 2**20
        ),
        name=f"section_forward_{section}",
    )(z, trow, tcol, *weights)


def backward(section, dims, dy, z, saved, trow, tcol, weights):
    experts, spread, features, wide, ff = dims
    full, slots = 2 * ROWS, CAP // 2
    narrow = ff // 2 // spread
    count = spread * experts * slots
    sends = 4 + 2 * (experts - 1) + 2 * experts * (spread - 1)
    vmem = pl.BlockSpec(memory_space=pltpu.VMEM)
    hbm = pl.BlockSpec(memory_space=pltpu.HBM)
    kernel = functools.partial(bwd_kernel, (section, experts, spread, wide))
    shape = jax.ShapeDtypeStruct
    return pl.pallas_call(
        kernel,
        out_shape=(
            shape((ROWS, features), F32),
            shape((2, features, narrow), BF),
            shape((2, features, narrow), BF),
            shape((features, 4 * wide + 128), BF),
        ),
        in_specs=[vmem] * 14 + [hbm] * 3,
        out_specs=(vmem,) * 4,
        scratch_shapes=[
            pltpu.VMEM((features, 4 * wide + 128), BF),
            pltpu.VMEM((2, features, narrow), BF),
            pltpu.VMEM((2, features, narrow), BF),
            pltpu.VMEM((2, ROWS, features), BF),
            pltpu.VMEM((experts, slots, features), BF),
            pltpu.VMEM((experts, spread, slots, features), BF),
            pltpu.VMEM((experts, spread, slots, features), F32),
            pltpu.VMEM((experts, spread, slots, features), BF),
            pltpu.VMEM((experts, max(1, spread - 1), slots, features), BF),
            pltpu.VMEM((2, experts, slots, features), BF),
            pltpu.VMEM((2, count, narrow), BF),
            pltpu.VMEM((2, count, narrow), BF),
            pltpu.VMEM((2, features, count), BF),
            pltpu.VMEM((2, ROWS, features), BF),
            pltpu.VMEM((3, full, wide), BF),
            pltpu.VMEM((2, ROWS, features), F32),
            pltpu.VMEM((ROWS, features), F32),
            pltpu.SemaphoreType.DMA((3,)),
            pltpu.SemaphoreType.DMA((2, sends)),
        ],
        compiler_params=pltpu.CompilerParams(
            collective_id=2 + section, has_side_effects=True, vmem_limit_bytes=56 * 2**20
        ),
        name=f"section_backward_{section}",
    )(dy, z, *saved, trow, tcol, *weights)


def swap_planes(values):
    return lax.ppermute(values, "pipe", [(0, 1), (1, 0)])


def swap_sides(values):
    return lax.ppermute(values, "tensor", [(0, 1), (1, 0)])


def pick(values, index, axis=0):
    return lax.dynamic_index_in_dim(values, index, axis, keepdims=False)


def spread_weights(dims, attn, inner, outer):
    experts, spread, features, _, ff = dims
    narrow = ff // 2 // spread
    shape = jax.ShapeDtypeStruct
    vmem = pl.BlockSpec(memory_space=pltpu.VMEM)
    hbm = pl.BlockSpec(memory_space=pltpu.HBM)
    sends = 3 * (experts - 1) + 3 * experts * (2 * spread - 1) + 2 * 2 * experts * spread
    return pl.pallas_call(
        functools.partial(spread_kernel, (experts, spread)),
        out_shape=(
            shape((2, features, attn.shape[1]), BF),
            shape((2, 2, features, narrow), BF),
            shape((2, 2, features, narrow), BF),
        ),
        in_specs=[vmem] * 3,
        out_specs=(hbm,) * 3,
        scratch_shapes=[
            pltpu.VMEM((2, experts, spread, features // (experts * spread), narrow), BF),
            pltpu.SemaphoreType.DMA((1 + 2 * experts,)),
            pltpu.SemaphoreType.DMA((2, sends)),
        ],
        compiler_params=pltpu.CompilerParams(
            collective_id=4, has_side_effects=True, vmem_limit_bytes=56 * 2**20
        ),
        name="spread_weights",
    )(attn, inner, outer)


def reduce_grads(dims, inner, outer, attn):
    experts, spread, features, _, ff = dims
    narrow = ff // 2 // spread
    shard = features // (experts * spread)
    broad = attn[0].shape[1]
    shape = jax.ShapeDtypeStruct
    hbm = pl.BlockSpec(memory_space=pltpu.HBM)
    vmem = pl.BlockSpec(memory_space=pltpu.VMEM)
    blocks = 4 * experts * spread
    sends = blocks + experts * (2 * (spread - 1) + 1 + 2 * spread + 2 * (spread - 1))
    sends += 3 * (experts - 1)
    return pl.pallas_call(
        functools.partial(reduce_kernel, (experts, spread)),
        out_shape=(
            shape((experts, shard, ff // 2), BF),
            shape((experts, shard, ff // 2), BF),
            shape((shard, broad), F32),
        ),
        in_specs=[hbm] * 6,
        out_specs=(vmem,) * 3,
        scratch_shapes=[
            pltpu.VMEM((2, 2, experts, spread, shard, narrow), BF),
            pltpu.VMEM((2, 2, experts, spread, shard, narrow), BF),
            pltpu.VMEM((2, experts, spread, shard, narrow), BF),
            pltpu.VMEM((2, experts, spread, shard, narrow), BF),
            pltpu.VMEM((2, experts, spread, shard, narrow), BF),
            pltpu.VMEM((2, experts, spread * shard, broad), BF),
            pltpu.VMEM((2, experts, max(1, spread - 1), shard, broad), BF),
            pltpu.VMEM((experts, shard, broad), BF),
            pltpu.VMEM((experts, shard, broad), BF),
            pltpu.SemaphoreType.DMA((blocks + 2 * experts,)),
            pltpu.SemaphoreType.DMA((2, sends)),
        ],
        compiler_params=pltpu.CompilerParams(
            collective_id=5, has_side_effects=True, vmem_limit_bytes=56 * 2**20
        ),
        name="reduce_grads",
    )(*inner, *outer, *attn)


def body(
    images_in,
    out_grad,
    attn_gain,
    attn_bias,
    qkv_weight,
    proj_weight,
    moe_gain,
    moe_bias,
    router_weight,
    inner_weight,
    outer_weight,
    expert_ids,
    slot_ids,
):
    plane = lax.axis_index("pipe")
    micro, local, piece, features = images_in.shape
    shard, wide = qkv_weight.shape[2], qkv_weight.shape[3]
    experts = router_weight.shape[2]
    half = inner_weight.shape[3]
    spread = lax.axis_size("dp") // experts
    dims = (experts, spread, features, wide, 2 * half)
    packed = jnp.concatenate(
        [qkv_weight[0, 0], qkv_weight[0, 1], qkv_weight[0, 2], proj_weight[0].T,
         jnp.concatenate(
             [attn_gain, attn_bias, moe_gain, moe_bias, router_weight[0].T,
              jnp.zeros((128 - 4 - experts, shard), BF)], axis=0,
         ).T],
        axis=1,
    )

    def columns(values):
        return values.reshape(experts, shard, spread, half // spread).transpose(0, 2, 1, 3)

    weights = spread_weights(
        dims, packed, columns(inner_weight[0]), columns(outer_weight[0].transpose(0, 2, 1))
    )

    def my_image(values):
        return jnp.pad(pick(values, plane)[0], ((0, ROWS - piece), (0, 0)))

    routes = expert_ids[0, :, 0]
    slots = slot_ids[0, :, 0]
    kept = slots < CAP
    codes = jnp.where(
        kept, slots // (CAP // 2) * (experts * CAP // 2) + routes * (CAP // 2) + slots % (CAP // 2),
        -1,
    )
    table = jnp.concatenate([codes, routes], axis=-1)
    table_own = pick(table, plane)
    table_other = swap_planes(pick(table, 1 - plane))
    tables = []
    for section in range(2):
        values = jnp.where(plane == section, table_own, table_other).reshape(2, piece, 4)
        values = jnp.pad(values, ((0, 0), (0, ROWS - piece), (0, 0)), constant_values=-1)
        values = values.reshape(2 * ROWS, 4)
        tables.append((
            jnp.pad(values.T, ((0, 4), (0, 0)), constant_values=-1),
            jnp.pad(values, ((0, 0), (0, 124)), constant_values=-1),
        ))

    z0 = my_image(images_in)
    y0, *saved0 = forward(0, dims, z0, *tables[0], weights)
    y1, *saved1 = forward(1, dims, y0, *tables[1], weights)
    dz1, *grads1 = backward(1, dims, my_image(out_grad), y0, saved1, *tables[1], weights)
    dz0, *grads0 = backward(0, dims, dz1.astype(BF), z0, saved0, *tables[0], weights)

    inner_out, outer_out, packed_out = reduce_grads(
        dims, (grads0[0], grads1[0]), (grads0[1], grads1[1]), (grads0[2], grads1[2])
    )
    inner_out, outer_out = inner_out.astype(F32), outer_out.astype(F32)
    own_small = packed_out[:, 4 * wide:4 * wide + 4 + experts]
    own_small = own_small + swap_sides(own_small)

    def shape_out(first, second):
        first, second = first[:piece], second[:piece]
        keep = jnp.where(plane == 0, first, second)
        came = swap_planes(jnp.where(plane == 0, second, first))
        both = jnp.stack([jnp.where(plane == 0, keep, came), jnp.where(plane == 0, came, keep)])
        return both.reshape(1, micro, local, piece, features)

    return (
        shape_out(y0, y1),
        shape_out(dz0, dz1),
        own_small[:, 0][None],
        own_small[:, 1][None],
        jnp.stack([packed_out[:, j * wide:(j + 1) * wide] for j in range(3)])[None],
        packed_out[:, 3 * wide:4 * wide].T[None],
        own_small[:, 2][None],
        own_small[:, 3][None],
        own_small[:, 4:][None],
        inner_out[None],
        outer_out.transpose(0, 2, 1)[None],
    )


def solution(mesh):
    in_specs = (
        P(None, "dp", "tensor", None),
        P(None, "dp", "tensor", None),
        P("pipe", "dp"),
        P("pipe", "dp"),
        P("pipe", None, "dp", "tensor"),
        P("pipe", "tensor", "dp"),
        P("pipe", "dp"),
        P("pipe", "dp"),
        P("pipe", "dp", None),
        P("pipe", None, "dp", "tensor"),
        P("pipe", None, "tensor", "dp"),
        P("pipe", None, "dp", None, None),
        P("pipe", None, "dp", None, None),
    )
    out_specs = (
        P("pipe", None, "dp", "tensor", None),
        P("pipe", None, "dp", "tensor", None),
        P("pipe", "dp"),
        P("pipe", "dp"),
        P("pipe", None, "dp", "tensor"),
        P("pipe", "tensor", "dp"),
        P("pipe", "dp"),
        P("pipe", "dp"),
        P("pipe", "dp", None),
        P("pipe", None, "dp", "tensor"),
        P("pipe", None, "tensor", "dp"),
    )
    return jax.shard_map(body, mesh=mesh, in_specs=in_specs, out_specs=out_specs, check_vma=False)
```

```python
import functools
import math

import jax
import jax.numpy as jnp
from jax import lax
from jax.experimental import pallas as pl
from jax.experimental.pallas import tpu as pltpu
from jax.sharding import PartitionSpec as P

HEAD_DIM = 64
LIVE = 197
CAP = 128
ROWS = 128
EPS = 1e-06
TILE = 384
LAG = 1
BF = jnp.bfloat16
F32 = jnp.float32
MESH = pl.DeviceIdType.MESH


def nn(left, right):
    return lax.dot_general(left, right, (((1,), (0,)), ((), ())), preferred_element_type=F32)


def nt(left, right):
    return lax.dot_general(left, right, (((1,), (1,)), ((), ())), preferred_element_type=F32)


def tn(left, right):
    return lax.dot_general(left, right, (((0,), (0,)), ((), ())), preferred_element_type=F32)


def norm_stats(values):
    centre = values - jnp.mean(values, axis=-1, keepdims=True)
    inv = lax.rsqrt(jnp.mean(centre * centre, axis=-1, keepdims=True) + EPS)
    return centre * inv, inv


def norm_back(grad, unit, inv, gain):
    scaled = grad * gain
    return (
        scaled
        - jnp.mean(scaled, axis=-1, keepdims=True)
        - unit * jnp.mean(scaled * unit, axis=-1, keepdims=True)
    ) * inv


def iota(shape, dim):
    return lax.broadcasted_iota(jnp.int32, shape, dim)


class Place:
    def __init__(self, experts, spread):
        self.experts, self.spread = experts, spread
        self.plane = lax.axis_index("pipe")
        self.side = lax.axis_index("tensor")
        dp = lax.axis_index("dp")
        self.mine = dp // spread
        self.column = lax.rem(dp, spread)
        self.twin = {"tensor": 1 - self.side}
        self.across = {"pipe": 1 - self.plane}

    def ahead(self, steps):
        return lax.rem(self.mine + steps, self.experts)

    def behind(self, steps):
        return lax.rem(self.mine + self.experts - steps, self.experts)

    def peer(self, group):
        return {"dp": group * self.spread + self.column}

    def beside(self, shift):
        return {"dp": self.mine * self.spread + lax.rem(self.column + shift, self.spread)}

    def left(self, shift):
        return lax.rem(self.column + self.spread - shift, self.spread)

    def greet(self, everyone=False):
        barrier = pltpu.get_barrier_semaphore()
        devices = [self.twin]
        devices += [self.peer(self.ahead(steps)) for steps in range(1, self.experts)]
        devices += [self.beside(shift) for shift in range(1, self.spread)]
        if everyone:
            devices += [self.across]
        for device in devices:
            pl.semaphore_signal(barrier, inc=1, device_id=device, device_id_type=MESH)
        pl.semaphore_wait(barrier, len(devices))


def send(source, target, sems, slot, device):
    copy = pltpu.make_async_remote_copy(
        src_ref=source,
        dst_ref=target,
        send_sem=sems.at[0, slot],
        recv_sem=sems.at[1, slot],
        device_id=device,
        device_id_type=MESH,
    )
    copy.start()
    return copy


class Slots:
    def __init__(self, sems):
        self.sems, self.next, self.sends = sems, 0, []

    def send(self, source, target, device):
        copy = send(source, target, self.sems, self.next, device)
        self.next += 1
        self.sends.append(copy)
        return copy

    def drain(self):
        for copy in self.sends:
            copy.wait_send()


class Spread:
    def __init__(self, place, slots, local, shards, stage, whole):
        self.place, self.slots, self.local = place, slots, local
        self.shards, self.stage, self.whole = shards, stage, whole
        experts = place.experts
        far = list(range(1, experts, 2)) + list(range(2, experts, 2))
        self.away = [(kind, steps) for steps in far for kind in (1, 2, 0)]
        self.pieces = [(kind, 0) for kind in range(3)] + self.away
        self.over_groups, self.over_columns, self.over_planes, self.late = {}, {}, {}, {}
        self.twins, self.kept = [], []

    def where(self, kind, section, group, col):
        place = self.place
        shard = self.shards[0].shape[0]
        row = (group * place.spread + col) * shard
        rows = pl.ds(pl.multiple_of(row, math.gcd(shard, 16)), shard)
        if kind == 0:
            return self.whole[0].at[section, rows]
        return self.whole[kind].at[section, place.side, rows]

    def held(self, kind, steps):
        place = self.place
        if kind == 0:
            if steps == 0:
                return self.shards[0]
            return self.where(0, place.plane, place.behind(steps), place.column)
        if steps == 0:
            return self.shards[kind].at[place.mine]
        return self.stage.at[kind - 1, steps]

    def start_groups(self, count):
        place = self.place
        for kind, steps in self.away[len(self.over_groups):len(self.over_groups) + count]:
            group = place.ahead(steps)
            if kind == 0:
                source = self.shards[0]
                target = self.where(0, place.plane, place.mine, place.column)
            else:
                source, target = self.shards[kind].at[group], self.stage.at[kind - 1, steps]
            self.over_groups[kind, steps] = self.slots.send(source, target, place.peer(group))

    def to_twin(self, kind, source, target):
        if kind:
            self.twins.append(self.slots.send(source, target, self.place.twin))

    def first_hop(self, kind, steps):
        place, slots = self.place, self.slots
        if steps:
            self.over_groups[kind, steps].wait_recv()
            self.start_groups(1)
        held = self.held(kind, steps)
        target = self.where(kind, place.plane, place.behind(steps), place.column)
        own = held if kind == 0 else held.at[place.column]
        for shift in range(1, place.spread):
            col = lax.rem(place.column + shift, place.spread)
            part = held if kind == 0 else held.at[col]
            self.over_columns[kind, steps, shift] = slots.send(part, target, place.beside(shift))
        self.over_planes[kind, steps] = slots.send(own, target, place.across)
        self.to_twin(kind, own, target)
        if kind or steps == 0:
            copy = pltpu.make_async_copy(own, target, self.local.at[len(self.kept)])
            copy.start()
            self.kept.append(copy)

    def second_hop(self, kind, steps):
        place, slots = self.place, self.slots
        group = place.behind(steps)
        if kind == 0:
            self.over_planes[kind, steps].wait_recv()
            target = self.where(kind, 1 - place.plane, group, place.column)
            for shift in range(1, place.spread):
                self.late[kind, steps, shift] = slots.send(target, target, place.beside(shift))
            return
        for shift in range(1, place.spread):
            self.over_columns[kind, steps, shift].wait_recv()
            target = self.where(kind, place.plane, group, place.left(shift))
            self.late[kind, steps, shift] = slots.send(target, target, place.across)
            self.to_twin(kind, target, target)

    def last_hop(self, kind, steps):
        place = self.place
        group = place.behind(steps)
        if kind:
            self.over_planes[kind, steps].wait_recv()
            target = self.where(kind, 1 - place.plane, group, place.column)
            self.to_twin(kind, target, target)
        for shift in range(1, place.spread):
            if kind == 0:
                self.over_columns[kind, steps, shift].wait_recv()
            self.late[kind, steps, shift].wait_recv()
            target = self.where(kind, 1 - place.plane, group, place.left(shift))
            self.to_twin(kind, target, target)

    def hops(self, begin, end):
        pieces = self.pieces
        for at in range(begin, end):
            if at < len(pieces):
                self.first_hop(*pieces[at])
            if LAG <= at < len(pieces) + LAG:
                self.second_hop(*pieces[at - LAG])
            if at >= 2 * LAG:
                self.last_hop(*pieces[at - 2 * LAG])

    def finish(self):
        for copy in self.twins:
            copy.wait_recv()
        for copy in self.kept:
            copy.wait()


def spread_kernel(cfg, attn_own, inner_own, outer_own, attn_all, inner_all, outer_all, stage,
                  lsem, sems):
    place = Place(*cfg)
    slots = Slots(sems)
    place.greet(everyone=True)
    spread = Spread(place, slots, lsem, (attn_own, inner_own, outer_own), stage,
                    (attn_all, inner_all, outer_all))
    spread.start_groups(4)
    spread.hops(0, len(spread.pieces) + 2 * LAG)
    spread.finish()
    slots.drain()


def add_into(target, came):
    target[...] = (target[...].astype(F32) + came[...].astype(F32)).astype(BF)


def reduce_kernel(cfg, *refs):
    experts, spread = cfg
    grads, gattn = (refs[0:2], refs[2:4]), refs[4:6]
    (inner_out, outer_out, attn_out,
     acc, twin_in, planes_in, blocks, z_in, attn_acc, at_cols, at_planes, z_attn,
     lsem, sems) = refs[6:]
    place = Place(experts, spread)
    slots = Slots(sems)
    plane, side, column = place.plane, place.side, place.column
    shard = acc.shape[4]
    local_slot = iter(range(lsem.shape[0]))
    place.greet(everyone=True)
    order = list(range(2, experts, 2)) + list(range(1, experts, 2)) + [0]
    whole = range(2)
    aligned = math.gcd(shard, 16)

    halves, attn_local, hops = {}, {}, {}

    def post(steps):
        group = place.ahead(steps)
        for section in whole:
            copy = pltpu.make_async_copy(
                gattn[section].at[
                    pl.ds(pl.multiple_of(group * spread * shard, aligned), spread * shard)
                ],
                attn_acc.at[section, steps], lsem.at[next(local_slot)],
            )
            copy.start()
            attn_local[steps, section] = copy
            for matrix in whole:
                for col in range(spread):
                    rows = pl.ds(
                        pl.multiple_of((group * spread + col) * shard, aligned), shard
                    )
                    source = grads[matrix][section]
                    away = slots.send(
                        source.at[1 - side, rows], twin_in.at[section, matrix, steps, col],
                        place.twin,
                    )
                    own = pltpu.make_async_copy(
                        source.at[side, rows], acc.at[section, matrix, steps, col],
                        lsem.at[next(local_slot)],
                    )
                    own.start()
                    halves[steps, section, matrix, col] = (away, own)

    def attn_block(section, steps, col):
        return attn_acc.at[section, steps, pl.ds(pl.multiple_of(col * shard, aligned), shard)]

    def first(kind, steps):
        if kind == 2:
            for section in whole:
                attn_local[steps, section].wait()
                for shift in range(1, spread):
                    hops["ax", steps, section, shift] = slots.send(
                        attn_block(section, steps, lax.rem(column + shift, spread)),
                        at_cols.at[section, steps, shift - 1], place.beside(shift),
                    )
            return
        for col in range(spread):
            for section in whole:
                away, own = halves[steps, section, kind, col]
                own.wait()
                away.wait_recv()
                add_into(acc.at[section, kind, steps, col], twin_in.at[section, kind, steps, col])
            hops["y", kind, steps, col] = slots.send(
                acc.at[1 - plane, kind, steps, col], planes_in.at[kind, steps, col], place.across
            )

    def second(kind, steps):
        if kind == 2:
            for section in whole:
                for shift in range(1, spread):
                    hops["ax", steps, section, shift].wait_recv()
                    add_into(attn_block(section, steps, column),
                             at_cols.at[section, steps, shift - 1])
            hops["ay", steps] = slots.send(
                attn_block(1 - plane, steps, column), at_planes.at[steps], place.across
            )
            return
        for col in range(spread):
            hops["y", kind, steps, col].wait_recv()
            add_into(acc.at[plane, kind, steps, col], planes_in.at[kind, steps, col])
        for shift in range(1, spread):
            hops["x", kind, steps, shift] = slots.send(
                acc.at[plane, kind, steps, lax.rem(column + shift, spread)],
                blocks.at[kind, steps, column], place.beside(shift),
            )
        blocks[kind, steps, column] = acc[plane, kind, steps, column]

    def third(kind, steps):
        device = place.peer(place.ahead(steps))
        if kind == 2:
            hops["ay", steps].wait_recv()
            add_into(attn_block(plane, steps, column), at_planes.at[steps])
            if steps:
                hops["az", steps] = slots.send(
                    attn_block(plane, steps, column), z_attn.at[steps], device
                )
            return
        for shift in range(1, spread):
            hops["x", kind, steps, shift].wait_recv()
        if steps:
            hops["z", kind, steps] = slots.send(
                blocks.at[kind, steps], z_in.at[kind, steps], device
            )

    post(order[0])
    pieces = [(kind, steps) for steps in order for kind in (1, 0, 2)]
    for at in range(len(pieces) + 2 * LAG):
        if at % 3 == 0 and at // 3 + 1 < experts:
            post(order[at // 3 + 1])
        if at < len(pieces):
            first(*pieces[at])
        if LAG <= at < len(pieces) + LAG:
            second(*pieces[at - LAG])
        if at >= 2 * LAG:
            third(*pieces[at - 2 * LAG])
    outs = (inner_out, outer_out)
    narrow = acc.shape[5]

    def put(kind, group, source):
        for col in range(spread):
            outs[kind][group, :, col * narrow:(col + 1) * narrow] = source[col]

    for kind in whole:
        put(kind, place.mine, blocks.at[kind, 0])
    total = attn_block(plane, 0, column)[...].astype(F32)
    for steps in order[:-1]:
        hops["az", steps].wait_recv()
        total = total + z_attn[steps].astype(F32)
        for kind in whole:
            hops["z", kind, steps].wait_recv()
            put(kind, place.behind(steps), z_in.at[kind, steps])
    attn_out[...] = total
    slots.drain()


class Rows:
    def __init__(self, place, slots, out, rows, acc, outb, parts, ret):
        self.place, self.slots, self.rows, self.acc = place, slots, rows, acc
        self.out, self.outb, self.parts, self.ret = out, outb, parts, ret
        self.order = [0] + list(range(2, place.experts, 2)) + list(range(1, place.experts, 2))
        self.over_groups, self.over_columns, self.partial, self.home = {}, {}, {}, []

    def start(self):
        place = self.place
        for steps in self.order[1:]:
            group = place.ahead(steps)
            self.over_groups[steps] = self.slots.send(
                self.out.at[group], self.rows.at[steps, place.column], place.peer(group)
            )
        self.pass_on(0)
        self.rows[0, place.column] = self.out[place.mine]

    def pass_on(self, steps):
        place = self.place
        target = self.rows.at[steps, place.column]
        source = target
        if steps:
            self.over_groups[steps].wait_recv()
        else:
            source = self.out.at[place.mine]
        for shift in range(1, place.spread):
            self.over_columns[steps, shift] = self.slots.send(source, target, place.beside(shift))

    def give_back(self, steps):
        place = self.place
        for shift in range(1, place.spread):
            col = lax.rem(place.column + shift, place.spread)
            self.outb[steps, col] = self.acc[steps, col].astype(BF)
            self.partial[steps, shift] = self.slots.send(
                self.outb.at[steps, col], self.parts.at[steps, shift - 1], place.beside(shift)
            )

    def send_home(self, steps):
        place = self.place
        total = self.acc[steps, place.column]
        for shift in range(1, place.spread):
            self.partial[steps, shift].wait_recv()
            total = total + self.parts[steps, shift - 1].astype(F32)
        if steps == 0:
            self.ret[place.side, place.mine] = total.astype(BF)
            return
        self.outb[steps, place.column] = total.astype(BF)
        self.home.append(self.slots.send(
            self.outb.at[steps, place.column], self.ret.at[place.side, place.mine],
            place.peer(place.behind(steps)),
        ))

    def run(self, compute):
        order = self.order
        for at, steps in enumerate(order):
            if at + 1 < len(order):
                self.pass_on(order[at + 1])
            for shift in range(1, self.place.spread):
                self.over_columns[steps, shift].wait_recv()
            compute(steps)
            self.give_back(steps)
            if at:
                self.send_home(order[at - 1])
        self.send_home(order[-1])

    def finish(self):
        for copy in self.home:
            copy.wait_recv()


def gelu_tanh(pre):
    return jnp.tanh(0.7978845608028654 * (pre + 0.044715 * pre * pre * pre))


def fwd_kernel(cfg, *refs):
    section, experts, spread, wide = cfg
    z_ref, trow_ref, tcol_ref, attn_hbm, inner_hbm, outer_hbm = refs[:6]
    (y_ref, h1_ref, a1_ref, qkv_ref, probs_ref, att_ref, a2_ref, rp_ref, rows_ref, pre_ref,
     chosen_ref,
     attn, inner, outer, a1_full, part, came, a2_full, disp, rows, acc, outb, parts, ret,
     wsem, sems) = refs[6:]
    place = Place(experts, spread)
    side = place.side
    features = z_ref.shape[1]
    narrow = inner.shape[2]
    tile = TILE if narrow % TILE == 0 else narrow
    tiles = narrow // tile
    chunk = spread * CAP // 2
    count = experts * chunk
    lots = CAP // 2
    full = 2 * ROWS
    slots = Slots(sems)
    fetch = pltpu.make_async_copy(attn_hbm.at[section], attn, wsem.at[2])
    fetch.start()
    fetch_inner = pltpu.make_async_copy(inner_hbm.at[section], inner, wsem.at[0])
    fetch_inner.start()
    fetch_outer = pltpu.make_async_copy(outer_hbm.at[section], outer, wsem.at[1])
    fetch_outer.start()
    place.greet()

    z = z_ref[...].astype(F32)
    unit1, _ = norm_stats(z)
    fetch.wait()
    block = attn[:, 4 * wide:]
    vectors = block.astype(F32).T
    a1_full[side] = (unit1 * vectors[0:1] + vectors[1:2]).astype(BF)
    copy_a1 = slots.send(a1_full.at[side], a1_full.at[side], place.twin)
    copy_a1.wait_recv()
    a1 = a1_full[...].reshape(full, features)
    a1_ref[...] = a1
    for j in range(3):
        qkv_ref[j] = nn(a1, attn[:, j * wide:(j + 1) * wide]).astype(BF)
    key = iota((1, full), 1)
    key_row = lax.rem(key, ROWS)
    piece = (LIVE + 3) // 2
    key_live = (key_row < piece) & ((key // ROWS) * piece + key_row < LIVE)
    low_lane = iota((1, 128), 1) < HEAD_DIM
    for pair in range(wide // 128):
        lanes = slice(pair * 128, (pair + 1) * 128)
        q, k, v = qkv_ref[0, :, lanes], qkv_ref[1, :, lanes], qkv_ref[2, :, lanes]
        results = []
        for which in range(2):
            mask = low_lane if which == 0 else ~low_lane
            scores = nt(jnp.where(mask, q, jnp.zeros_like(q)), k) * HEAD_DIM**-0.5
            scores = jnp.where(key_live, scores, -1e30)
            weights = jnp.exp(scores - jnp.max(scores, axis=-1, keepdims=True))
            probs = weights / jnp.sum(weights, axis=-1, keepdims=True)
            probs_ref[2 * pair + which] = probs
            results.append(nn(probs.astype(BF), v))
        att_ref[:, lanes] = jnp.where(low_lane, results[0], results[1]).astype(BF)
    part[...] = nt(att_ref[...], attn[:, 3 * wide:4 * wide]).reshape(2, ROWS, features)
    copy_part = slots.send(part.at[1 - side], came, place.twin)
    copy_part.wait_recv()
    h1 = z + part[side] + came[...]
    h1_ref[...] = h1
    unit2, _ = norm_stats(h1)
    a2_full[side] = (unit2 * vectors[2:3] + vectors[3:4]).astype(BF)
    copy_a2 = slots.send(a2_full.at[side], a2_full.at[side], place.twin)
    copy_a2.wait_recv()
    a2 = a2_full[...].reshape(full, features)
    a2_ref[...] = a2

    slot = iota((experts * lots, full), 0) + side * (experts * lots)
    hit = (trow_ref[0:1, :] == slot) | (trow_ref[1:2, :] == slot)
    disp[...] = nn(hit.astype(F32).astype(BF), a2).astype(BF).reshape(experts, lots, features)
    moves = Rows(place, slots, disp, rows, acc, outb, parts, ret)
    moves.start()

    lane = iota((1, 128), 1)
    valid = (lane >= 4) & (lane < 4 + experts)
    logits = jnp.where(valid, nn(a2, block), -1e30)
    odds = jnp.where(valid, jnp.exp(logits - jnp.max(logits, axis=-1, keepdims=True)), 0.0)
    rp_ref[...] = odds / jnp.sum(odds, axis=-1, keepdims=True)

    fetch_inner.wait()
    fetch_outer.wait()

    def compute(steps):
        span = slice(steps * chunk, (steps + 1) * chunk)
        rows_ref[span, :] = rows[steps].reshape(chunk, features)
        acc[steps] = jnp.zeros_like(acc[steps])

        def tile_step(step, carry):
            half = step // tiles
            cols = pl.ds(pl.multiple_of(lax.rem(step, tiles) * tile, math.gcd(tile, 128)), tile)
            pre = nn(rows_ref[span, :], inner[half, :, cols])
            pre_ref[half, span, cols] = pre
            act = (0.5 * pre * (1.0 + gelu_tanh(pre))).astype(BF)
            acc[steps] += nt(act, outer[half, :, cols]).reshape(spread, lots, features)
            return carry

        lax.fori_loop(0, 2 * tiles, tile_step, 0)

    moves.run(compute)
    moves.finish()
    copy_ret = slots.send(ret.at[side], ret.at[side], place.twin)
    copy_ret.wait_recv()
    home = ret[...].reshape(2 * experts * lots, features)
    own_rows = pl.ds(pl.multiple_of(side * ROWS, ROWS), ROWS)
    table = tcol_ref[own_rows, :]
    odds = rp_ref[own_rows, :]
    column = iota((ROWS, 2 * experts * lots), 1)
    y = h1
    for choice in range(2):
        pick = (table[:, choice:choice + 1] == column).astype(F32).astype(BF)
        chosen = nn(pick, home)
        chosen_ref[choice] = chosen.astype(BF)
        hot = table[:, 2 + choice:3 + choice] + 4 == lane
        y = y + chosen * jnp.sum(jnp.where(hot, odds, 0.0), axis=-1, keepdims=True)
    y_ref[...] = y.astype(BF)
    slots.drain()


def bwd_kernel(cfg, *refs):
    section, experts, spread, wide = cfg
    (dy_ref, z_ref, h1_ref, a1_ref, qkv_ref, probs_ref, att_ref, a2_ref, rp_ref, rows_ref,
     pre_ref, chosen_ref, trow_ref, tcol_ref, attn_hbm, inner_hbm, outer_hbm) = refs[:17]
    (dz_ref, low_ref, gin_ref, gout_ref, gattn_ref,
     attn, inner, outer, dy_full, disp, dexp, acc, outb, parts, ret, act_all, dpre_all, lhs_t,
     dbr_full, dqkv, part, came, wsem, sems) = refs[17:]
    place = Place(experts, spread)
    side = place.side
    features = z_ref.shape[1]
    narrow = inner.shape[2]
    tile = TILE if narrow % TILE == 0 else narrow
    tiles = narrow // tile
    chunk = spread * CAP // 2
    count = experts * chunk
    lots = CAP // 2
    full = 2 * ROWS
    slots = Slots(sems)
    fetch = pltpu.make_async_copy(attn_hbm.at[section], attn, wsem.at[2])
    fetch.start()
    fetch_inner = pltpu.make_async_copy(inner_hbm.at[section], inner, wsem.at[0])
    fetch_inner.start()
    fetch_outer = pltpu.make_async_copy(outer_hbm.at[section], outer, wsem.at[1])
    fetch_outer.start()
    place.greet()

    dy_full[side] = dy_ref[...]
    copy_dy = slots.send(dy_full.at[side], dy_full.at[side], place.twin)
    copy_dy.wait_recv()
    lane = iota((1, 128), 1)
    grad = dy_full[...].reshape(full, features).astype(F32)
    slot = iota((experts * lots, full), 0) + side * (experts * lots)
    total = jnp.zeros((experts * lots, features), F32)
    for choice in range(2):
        hot = tcol_ref[:, 2 + choice:3 + choice] + 4 == lane
        gate = jnp.sum(jnp.where(hot, rp_ref[...], 0.0), axis=-1, keepdims=True)
        hit = (trow_ref[choice:choice + 1, :] == slot).astype(F32).astype(BF)
        total = total + nn(hit, (gate * grad).astype(BF))
    disp[...] = total.astype(BF).reshape(experts, lots, features)
    moves = Rows(place, slots, disp, dexp, acc, outb, parts, ret)
    moves.start()

    fetch.wait()
    block = attn[:, 4 * wide:]
    vectors = block.astype(F32).T
    own_rows = pl.ds(pl.multiple_of(side * ROWS, ROWS), ROWS)
    table = tcol_ref[own_rows, :]
    odds = rp_ref[own_rows, :]
    dy = dy_ref[...].astype(F32)
    drouter = jnp.zeros((ROWS, 128), F32)
    for choice in range(2):
        dgate = jnp.sum(dy * chosen_ref[choice].astype(F32), axis=-1, keepdims=True)
        dgate = jnp.where(table[:, choice:choice + 1] >= 0, dgate, 0.0)
        hot = table[:, 2 + choice:3 + choice] + 4 == lane
        drouter = drouter + jnp.where(hot, dgate, 0.0)
    dlogit = odds * (drouter - jnp.sum(odds * drouter, axis=-1, keepdims=True))
    high = dlogit.astype(BF)
    rest = (dlogit - high.astype(F32)).astype(BF)
    da2 = nt(high, block) + nt(rest, block)
    a2 = a2_ref[own_rows, :]
    grad_router = tn(a2, high) + tn(a2, rest)

    fetch_inner.wait()
    fetch_outer.wait()

    def tile_at(step):
        return step // tiles, pl.ds(
            pl.multiple_of(lax.rem(step, tiles) * tile, math.gcd(tile, 128)), tile
        )

    def compute(steps):
        span = slice(steps * chunk, (steps + 1) * chunk)
        acc[steps] = jnp.zeros_like(acc[steps])

        def tile_step(step, carry):
            half, cols = tile_at(step)
            grad_act = nn(dexp[steps].reshape(chunk, features), outer[half, :, cols])
            pre = pre_ref[half, span, cols]
            tanh = gelu_tanh(pre)
            act_all[half, span, cols] = (0.5 * pre * (1.0 + tanh)).astype(BF)
            slope = 0.5 * (1.0 + tanh) + 0.5 * pre * (1.0 - tanh * tanh) * (
                0.7978845608028654 * (1.0 + 3 * 0.044715 * pre * pre)
            )
            dpre = (grad_act * slope).astype(BF)
            dpre_all[half, span, cols] = dpre
            acc[steps] += nt(dpre, inner[half, :, cols]).reshape(spread, lots, features)
            return carry

        lax.fori_loop(0, 2 * tiles, tile_step, 0)

    moves.run(compute)
    lhs_t[0] = dexp[...].reshape(count, features).T
    lhs_t[1] = rows_ref[...].T

    def grad_step(step, carry):
        half, cols = tile_at(step)
        gout_ref[half, :, cols] = nn(lhs_t[0], act_all[half, :, cols]).astype(BF)
        gin_ref[half, :, cols] = nn(lhs_t[1], dpre_all[half, :, cols]).astype(BF)
        return carry

    lax.fori_loop(0, 2 * tiles, grad_step, 0)
    moves.finish()
    copy_ret = slots.send(ret.at[side], ret.at[side], place.twin)
    copy_ret.wait_recv()
    home = ret[...].reshape(2 * experts * lots, features)
    column = iota((ROWS, 2 * experts * lots), 1)
    pick = (table[:, 0:1] == column) | (table[:, 1:2] == column)
    da2 = da2 + nn(pick.astype(F32).astype(BF), home)
    unit2, inv2 = norm_stats(h1_ref[...])
    grad_gain2 = jnp.sum(da2 * unit2, axis=0, keepdims=True)
    grad_bias2 = jnp.sum(da2, axis=0, keepdims=True)
    dh1 = dy + norm_back(da2, unit2, inv2, vectors[2:3])
    dbr_full[side] = dh1.astype(BF)
    copy_dbr = slots.send(dbr_full.at[side], dbr_full.at[side], place.twin)
    copy_dbr.wait_recv()
    dbr = dbr_full[...].reshape(full, features)
    gattn_ref[:, 3 * wide:4 * wide] = tn(dbr, att_ref[...]).astype(BF)
    datt = nn(dbr, attn[:, 3 * wide:4 * wide]).astype(BF)
    low_lane = lane < HEAD_DIM
    for pair in range(wide // 128):
        lanes = slice(pair * 128, (pair + 1) * 128)
        q, k, v = qkv_ref[0, :, lanes], qkv_ref[1, :, lanes], qkv_ref[2, :, lanes]
        wide_datt = datt[:, lanes]
        dq = dk = dv = 0.0
        for which in range(2):
            mask = low_lane if which == 0 else ~low_lane
            zero = jnp.zeros_like(q)
            probs = probs_ref[2 * pair + which]
            head = jnp.where(mask, wide_datt, zero)
            dv = dv + tn(probs.astype(BF), head)
            dprobs = nt(head, v)
            dscores = probs * (dprobs - jnp.sum(probs * dprobs, axis=-1, keepdims=True))
            dscores = dscores.astype(BF)
            dq = dq + nn(dscores, jnp.where(mask, k, zero))
            dk = dk + tn(dscores, jnp.where(mask, q, zero))
        dqkv[0, :, lanes] = (dq * HEAD_DIM**-0.5).astype(BF)
        dqkv[1, :, lanes] = (dk * HEAD_DIM**-0.5).astype(BF)
        dqkv[2, :, lanes] = dv.astype(BF)
    da1 = jnp.zeros((full, features), F32)
    for j in range(3):
        da1 = da1 + nt(dqkv[j], attn[:, j * wide:(j + 1) * wide])
    part[...] = da1.reshape(2, ROWS, features)
    copy_part = slots.send(part.at[1 - side], came, place.twin)
    for j in range(3):
        gattn_ref[:, j * wide:(j + 1) * wide] = tn(a1_ref[...], dqkv[j]).astype(BF)
    unit1, inv1 = norm_stats(z_ref[...].astype(F32))
    copy_part.wait_recv()
    da1 = part[side] + came[...]
    grad_gain1 = jnp.sum(da1 * unit1, axis=0, keepdims=True)
    grad_bias1 = jnp.sum(da1, axis=0, keepdims=True)
    dz = dh1 + norm_back(da1, unit1, inv1, vectors[0:1])
    dz_ref[...] = dz
    low_ref[...] = dz.astype(BF)
    small = jnp.concatenate(
        [grad_gain1, grad_bias1, grad_gain2, grad_bias2, jnp.zeros((124, features), F32)], axis=0
    )
    gattn_ref[:, 4 * wide:] = (small.T + grad_router).astype(BF)
    slots.drain()


def forward(section, dims, z, trow, tcol, weights):
    experts, spread, features, wide, ff = dims
    full, slots = 2 * ROWS, CAP // 2
    narrow = ff // 2 // spread
    count = spread * experts * slots
    sends = 4 + 2 * (experts - 1) + 2 * experts * (spread - 1)
    heads = wide // HEAD_DIM
    vmem = pl.BlockSpec(memory_space=pltpu.VMEM)
    hbm = pl.BlockSpec(memory_space=pltpu.HBM)
    kernel = functools.partial(fwd_kernel, (section, experts, spread, wide))
    shape = jax.ShapeDtypeStruct
    return pl.pallas_call(
        kernel,
        out_shape=(
            shape((ROWS, features), BF),
            shape((ROWS, features), F32),
            shape((full, features), BF),
            shape((3, full, wide), BF),
            shape((heads, full, full), F32),
            shape((full, wide), BF),
            shape((full, features), BF),
            shape((full, 128), F32),
            shape((count, features), BF),
            shape((2, count, narrow), F32),
            shape((2, ROWS, features), BF),
        ),
        in_specs=[vmem] * 3 + [hbm] * 3,
        out_specs=(vmem,) * 11,
        scratch_shapes=[
            pltpu.VMEM((features, 4 * wide + 128), BF),
            pltpu.VMEM((2, features, narrow), BF),
            pltpu.VMEM((2, features, narrow), BF),
            pltpu.VMEM((2, ROWS, features), BF),
            pltpu.VMEM((2, ROWS, features), F32),
            pltpu.VMEM((ROWS, features), F32),
            pltpu.VMEM((2, ROWS, features), BF),
            pltpu.VMEM((experts, slots, features), BF),
            pltpu.VMEM((experts, spread, slots, features), BF),
            pltpu.VMEM((experts, spread, slots, features), F32),
            pltpu.VMEM((experts, spread, slots, features), BF),
            pltpu.VMEM((experts, max(1, spread - 1), slots, features), BF),
            pltpu.VMEM((2, experts, slots, features), BF),
            pltpu.SemaphoreType.DMA((3,)),
            pltpu.SemaphoreType.DMA((2, sends)),
        ],
        compiler_params=pltpu.CompilerParams(
            collective_id=section, has_side_effects=True, vmem_limit_bytes=56 * 2**20
        ),
        name=f"section_forward_{section}",
    )(z, trow, tcol, *weights)


def backward(section, dims, dy, z, saved, trow, tcol, weights):
    experts, spread, features, wide, ff = dims
    full, slots = 2 * ROWS, CAP // 2
    narrow = ff // 2 // spread
    count = spread * experts * slots
    sends = 4 + 2 * (experts - 1) + 2 * experts * (spread - 1)
    vmem = pl.BlockSpec(memory_space=pltpu.VMEM)
    hbm = pl.BlockSpec(memory_space=pltpu.HBM)
    kernel = functools.partial(bwd_kernel, (section, experts, spread, wide))
    shape = jax.ShapeDtypeStruct
    return pl.pallas_call(
        kernel,
        out_shape=(
            shape((ROWS, features), F32),
            shape((ROWS, features), BF),
            shape((2, features, narrow), BF),
            shape((2, features, narrow), BF),
            shape((features, 4 * wide + 128), BF),
        ),
        in_specs=[vmem] * 14 + [hbm] * 3,
        out_specs=(vmem,) * 5,
        scratch_shapes=[
            pltpu.VMEM((features, 4 * wide + 128), BF),
            pltpu.VMEM((2, features, narrow), BF),
            pltpu.VMEM((2, features, narrow), BF),
            pltpu.VMEM((2, ROWS, features), BF),
            pltpu.VMEM((experts, slots, features), BF),
            pltpu.VMEM((experts, spread, slots, features), BF),
            pltpu.VMEM((experts, spread, slots, features), F32),
            pltpu.VMEM((experts, spread, slots, features), BF),
            pltpu.VMEM((experts, max(1, spread - 1), slots, features), BF),
            pltpu.VMEM((2, experts, slots, features), BF),
            pltpu.VMEM((2, count, narrow), BF),
            pltpu.VMEM((2, count, narrow), BF),
            pltpu.VMEM((2, features, count), BF),
            pltpu.VMEM((2, ROWS, features), BF),
            pltpu.VMEM((3, full, wide), BF),
            pltpu.VMEM((2, ROWS, features), F32),
            pltpu.VMEM((ROWS, features), F32),
            pltpu.SemaphoreType.DMA((3,)),
            pltpu.SemaphoreType.DMA((2, sends)),
        ],
        compiler_params=pltpu.CompilerParams(
            collective_id=2 + section, has_side_effects=True, vmem_limit_bytes=56 * 2**20
        ),
        name=f"section_backward_{section}",
    )(dy, z, *saved, trow, tcol, *weights)


def swap_planes(values):
    return lax.ppermute(values, "pipe", [(0, 1), (1, 0)])


def swap_sides(values):
    return lax.ppermute(values, "tensor", [(0, 1), (1, 0)])


def pick(values, index, axis=0):
    return lax.dynamic_index_in_dim(values, index, axis, keepdims=False)


def spread_weights(dims, attn, inner, outer):
    experts, spread, features, _, ff = dims
    narrow = ff // 2 // spread
    shape = jax.ShapeDtypeStruct
    vmem = pl.BlockSpec(memory_space=pltpu.VMEM)
    hbm = pl.BlockSpec(memory_space=pltpu.HBM)
    sends = 3 * (experts - 1) + 3 * experts * (2 * spread - 1) + 2 * 2 * experts * spread
    return pl.pallas_call(
        functools.partial(spread_kernel, (experts, spread)),
        out_shape=(
            shape((2, features, attn.shape[1]), BF),
            shape((2, 2, features, narrow), BF),
            shape((2, 2, features, narrow), BF),
        ),
        in_specs=[vmem] * 3,
        out_specs=(hbm,) * 3,
        scratch_shapes=[
            pltpu.VMEM((2, experts, spread, features // (experts * spread), narrow), BF),
            pltpu.SemaphoreType.DMA((1 + 2 * experts,)),
            pltpu.SemaphoreType.DMA((2, sends)),
        ],
        compiler_params=pltpu.CompilerParams(
            collective_id=4, has_side_effects=True, vmem_limit_bytes=56 * 2**20
        ),
        name="spread_weights",
    )(attn, inner, outer)


def reduce_grads(dims, inner, outer, attn):
    experts, spread, features, _, ff = dims
    narrow = ff // 2 // spread
    shard = features // (experts * spread)
    broad = attn[0].shape[1]
    shape = jax.ShapeDtypeStruct
    hbm = pl.BlockSpec(memory_space=pltpu.HBM)
    vmem = pl.BlockSpec(memory_space=pltpu.VMEM)
    blocks = 4 * experts * spread
    sends = blocks + experts * (2 * (spread - 1) + 1 + 2 * spread + 2 * (spread - 1))
    sends += 3 * (experts - 1)
    return pl.pallas_call(
        functools.partial(reduce_kernel, (experts, spread)),
        out_shape=(
            shape((experts, shard, ff // 2), BF),
            shape((experts, shard, ff // 2), BF),
            shape((shard, broad), F32),
        ),
        in_specs=[hbm] * 6,
        out_specs=(vmem,) * 3,
        scratch_shapes=[
            pltpu.VMEM((2, 2, experts, spread, shard, narrow), BF),
            pltpu.VMEM((2, 2, experts, spread, shard, narrow), BF),
            pltpu.VMEM((2, experts, spread, shard, narrow), BF),
            pltpu.VMEM((2, experts, spread, shard, narrow), BF),
            pltpu.VMEM((2, experts, spread, shard, narrow), BF),
            pltpu.VMEM((2, experts, spread * shard, broad), BF),
            pltpu.VMEM((2, experts, max(1, spread - 1), shard, broad), BF),
            pltpu.VMEM((experts, shard, broad), BF),
            pltpu.VMEM((experts, shard, broad), BF),
            pltpu.SemaphoreType.DMA((blocks + 2 * experts,)),
            pltpu.SemaphoreType.DMA((2, sends)),
        ],
        compiler_params=pltpu.CompilerParams(
            collective_id=5, has_side_effects=True, vmem_limit_bytes=56 * 2**20
        ),
        name="reduce_grads",
    )(*inner, *outer, *attn)


def body(
    images_in,
    out_grad,
    attn_gain,
    attn_bias,
    qkv_weight,
    proj_weight,
    moe_gain,
    moe_bias,
    router_weight,
    inner_weight,
    outer_weight,
    expert_ids,
    slot_ids,
):
    plane = lax.axis_index("pipe")
    micro, local, piece, features = images_in.shape
    shard, wide = qkv_weight.shape[2], qkv_weight.shape[3]
    experts = router_weight.shape[2]
    half = inner_weight.shape[3]
    spread = lax.axis_size("dp") // experts
    dims = (experts, spread, features, wide, 2 * half)
    packed = jnp.concatenate(
        [qkv_weight[0, 0], qkv_weight[0, 1], qkv_weight[0, 2], proj_weight[0].T,
         jnp.stack([attn_gain[0], attn_bias[0], moe_gain[0], moe_bias[0]], axis=1),
         router_weight[0], jnp.zeros((shard, 128 - 4 - experts), BF)],
        axis=1,
    )

    def columns(values):
        return values.reshape(experts, shard, spread, half // spread).transpose(0, 2, 1, 3)

    weights = spread_weights(
        dims, packed, columns(inner_weight[0]), columns(outer_weight[0].transpose(0, 2, 1))
    )

    def my_image(values):
        return jnp.pad(pick(values, plane)[0], ((0, ROWS - piece), (0, 0)))

    routes = expert_ids[0, :, 0]
    slots = slot_ids[0, :, 0]
    kept = slots < CAP
    codes = jnp.where(
        kept, slots // (CAP // 2) * (experts * CAP // 2) + routes * (CAP // 2) + slots % (CAP // 2),
        -1,
    )
    table = jnp.concatenate([codes, routes], axis=-1)
    table_own = pick(table, plane)
    table_other = swap_planes(pick(table, 1 - plane))
    tables = []
    for section in range(2):
        values = jnp.where(plane == section, table_own, table_other).reshape(2, piece, 4)
        values = jnp.pad(values, ((0, 0), (0, ROWS - piece), (0, 0)), constant_values=-1)
        values = values.reshape(2 * ROWS, 4)
        tables.append((
            jnp.pad(values.T, ((0, 4), (0, 0)), constant_values=-1),
            jnp.pad(values, ((0, 0), (0, 124)), constant_values=-1),
        ))

    z0 = my_image(images_in)
    y0, *saved0 = forward(0, dims, z0, *tables[0], weights)
    y1, *saved1 = forward(1, dims, y0, *tables[1], weights)
    dz1, low1, *grads1 = backward(1, dims, my_image(out_grad), y0, saved1, *tables[1], weights)
    dz0, _, *grads0 = backward(0, dims, low1, z0, saved0, *tables[0], weights)

    inner_out, outer_out, packed_out = reduce_grads(
        dims, (grads0[0], grads1[0]), (grads0[1], grads1[1]), (grads0[2], grads1[2])
    )
    inner_out, outer_out = inner_out.astype(F32), outer_out.astype(F32)
    own_small = packed_out[:, 4 * wide:4 * wide + 4 + experts]
    own_small = own_small + swap_sides(own_small)

    def shape_out(first, second):
        first, second = first[:piece], second[:piece]
        keep = jnp.where(plane == 0, first, second)
        came = swap_planes(jnp.where(plane == 0, second, first))
        both = jnp.stack([jnp.where(plane == 0, keep, came), jnp.where(plane == 0, came, keep)])
        return both.reshape(1, micro, local, piece, features)

    return (
        shape_out(y0, y1),
        shape_out(dz0, dz1),
        own_small[:, 0][None],
        own_small[:, 1][None],
        jnp.stack([packed_out[:, j * wide:(j + 1) * wide] for j in range(3)])[None],
        packed_out[:, 3 * wide:4 * wide].T[None],
        own_small[:, 2][None],
        own_small[:, 3][None],
        own_small[:, 4:][None],
        inner_out[None],
        outer_out.transpose(0, 2, 1)[None],
    )


def solution(mesh):
    in_specs = (
        P(None, "dp", "tensor", None),
        P(None, "dp", "tensor", None),
        P("pipe", "dp"),
        P("pipe", "dp"),
        P("pipe", None, "dp", "tensor"),
        P("pipe", "tensor", "dp"),
        P("pipe", "dp"),
        P("pipe", "dp"),
        P("pipe", "dp", None),
        P("pipe", None, "dp", "tensor"),
        P("pipe", None, "tensor", "dp"),
        P("pipe", None, "dp", None, None),
        P("pipe", None, "dp", None, None),
    )
    out_specs = (
        P("pipe", None, "dp", "tensor", None),
        P("pipe", None, "dp", "tensor", None),
        P("pipe", "dp"),
        P("pipe", "dp"),
        P("pipe", None, "dp", "tensor"),
        P("pipe", "tensor", "dp"),
        P("pipe", "dp"),
        P("pipe", "dp"),
        P("pipe", "dp", None),
        P("pipe", None, "dp", "tensor"),
        P("pipe", None, "tensor", "dp"),
    )
    return jax.shard_map(body, mesh=mesh, in_specs=in_specs, out_specs=out_specs, check_vma=False)
```
